32 devices in a mesh: shard: 16 (over z, x, core), rep: 2 (over y).
Axes of the slice: x: 2, y: 2, z: 4, core: 2. Of those that a mesh axis runs over, the one named last changes fastest.
Arguments:
- hidden_in: bfloat16 [2, 32, 128, 1024], P(None, ('shard', 'rep')), may hold values from -6 to 6
- encoded: bfloat16 [2, 32, 256, 1024], P(None, ('shard', 'rep')), may hold values from -6 to 6
- dec_segments: int32 [2, 32, 128], P(None, ('shard', 'rep')), may hold values from 0 to 2, never falling along the last dimension, each value on 1 to 64 neighbouring positions
- enc_segments: int32 [2, 32, 256], P(None, ('shard', 'rep')), may hold values from 0 to 2, never falling along the last dimension, each value on 1 to 128 neighbouring positions
- buckets: int32 [128], replicated, may hold values from 0 to 31
- out_cot: bfloat16 [2, 32, 128, 1024], P(None, ('shard', 'rep')), may hold values from -6 to 6
- norm_self: bfloat16 [1024], P('shard'), may hold values from 0.5 to 1.5
- self_query: bfloat16 [1024, 1024], P('shard'), may hold values from -0.0234375 to 0.0234375
- self_key: bfloat16 [1024, 1024], P('shard'), may hold values from -0.1875 to 0.1875
- self_value: bfloat16 [1024, 1024], P('shard'), may hold values from -0.1875 to 0.1875
- self_out: bfloat16 [1024, 1024], P('shard'), may hold values from -1.5 to 1.5
- relative_bias_table: bfloat16 [32, 16], replicated, may hold values from -4 to 4
- norm_cross: bfloat16 [1024], P('shard'), may hold values from 0.5 to 1.5
- cross_query: bfloat16 [1024, 1024], P('shard'), may hold values from -0.0234375 to 0.0234375
- cross_key: bfloat16 [1024, 1024], P('shard'), may hold values from -0.1875 to 0.1875
- cross_value: bfloat16 [1024, 1024], P('shard'), may hold values from -0.1875 to 0.1875
- cross_out: bfloat16 [1024, 1024], P('shard'), may hold values from -1.5 to 1.5
- norm_ff: bfloat16 [1024], P('shard'), may hold values from 0.5 to 1.5
- ff_gate: bfloat16 [1024, 2816], P('shard'), may hold values from -0.1875 to 0.1875
- ff_up: bfloat16 [1024, 2816], P('shard'), may hold values from -0.1875 to 0.1875
- ff_down: bfloat16 [2816, 1024], P('shard'), may hold values from -0.21875 to 0.21875
Outputs:
- out_hidden: bfloat16 [2, 32, 128, 1024], P(None, ('shard', 'rep'))
- grad_hidden: float32 [2, 32, 128, 1024], P(None, ('shard', 'rep'))
- grad_encoded: float32 [2, 32, 256, 1024], P(None, ('shard', 'rep'))
- grad_norm_self: float32 [1024], P('shard')
- grad_self_query: float32 [1024, 1024], P('shard')
- grad_self_key: float32 [1024, 1024], P('shard')
- grad_self_value: float32 [1024, 1024], P('shard')
- grad_self_out: float32 [1024, 1024], P('shard')
- grad_rel_table: float32 [32, 16], replicated
- grad_norm_cross: float32 [1024], P('shard')
- grad_cross_query: float32 [1024, 1024], P('shard')
- grad_cross_key: float32 [1024, 1024], P('shard')
- grad_cross_value: float32 [1024, 1024], P('shard')
- grad_cross_out: float32 [1024, 1024], P('shard')
- grad_norm_ff: float32 [1024], P('shard')
- grad_ff_gate: float32 [1024, 2816], P('shard')
- grad_ff_up: float32 [1024, 2816], P('shard')
- grad_ff_down: float32 [2816, 1024], P('shard')
The draws below stay inside these ranges and needn't reach their ends.
Inputs may be any that keep to these rules, and one draw needn't show every extreme that they name: `dec_segments`: within a sequence the decoder document numbers never fall; each of the 3 documents holds one or more positions, the longest exactly half of 128. `enc_segments`: within a sequence the encoder document numbers never fall; each of the 3 documents holds one or more positions, the longest exactly half of 256.
All inputs are finite; a program needn't handle non-finite values.
Results may differ from the reference program's by a relative error of at most 0.019.
Values may be sent and summed in bfloat16 or wider, within the bound.
A program may use at most 192 MiB of HBM per device.

```python
import math
import jax
import jax.numpy as jnp
import numpy as np
from jax import lax

D = 1024
HEADS = 16
HEAD = 64
FF = 2816
NB = 32
SEQ = 128
ENC = 256
MB = 2
DOCS = 3
SEQS = 32


def touch_ends(drawn, key, smallest, top_value):
    index_at = [jax.random.randint(jax.random.fold_in(key, axis), (), 0, length) for axis, length in enumerate(drawn.shape)]
    longest = drawn.shape.index(max(drawn.shape))
    next_to = index_at[:longest] + [(index_at[longest] + 1) % drawn.shape[longest]] + index_at[longest + 1:]
    return drawn.at[tuple(index_at)].set(smallest).at[tuple(next_to)].set(top_value)


def levels(key, extent, split, smallest, largest):
    level, own = 1.0, jax.random.fold_in(key, 6)
    for axis_at, shards_of in split:
        steps = jnp.exp(jax.random.uniform(jax.random.fold_in(own, axis_at), (shards_of,), jnp.float32, smallest / len(split), largest / len(split)))
        level = level * jnp.repeat(steps, extent[axis_at] // shards_of).reshape([-1 if axis == axis_at else 1 for axis in range(len(extent))])
    return level


def split_up(amount, total, most, skew):
    portions = [(1 << 20) // math.isqrt(rank ** skew) + 1 for rank in range(2, amount + 1)]
    surplus, given = total - most - (amount - 1), [1] * (amount - 1)
    while surplus > 0:
        free = [i for i in range(amount - 1) if given[i] < most]
        mass, remaining = sum([portions[i] for i in free]), surplus
        for i in free:
            more = min(most - given[i], max(1, remaining * portions[i] // mass), surplus)
            given[i] = given[i] + more
            surplus = surplus - more
    return np.array([most] + given)


def ragged_sizes(key, amount, total, most, skew):
    if amount == 2:
        one = jax.random.randint(key, (), max(1, total - most), min(most, total - 1) + 1)
        return jnp.stack([one, total - one])
    lengths = jnp.asarray(split_up(amount, total, most, skew), jnp.int32)
    pairs = (amount - 1) // 2
    giver, receiver = lengths[1:1 + 2 * pairs:2], lengths[2:2 + 2 * pairs:2]
    slack = jnp.minimum(giver - 1, most - receiver)
    shifted = jax.random.randint(jax.random.fold_in(key, 1), (pairs,), 0, 1 << 20) % (slack + 1)
    lengths = lengths.at[1:1 + 2 * pairs:2].set(giver - shifted).at[2:2 + 2 * pairs:2].set(receiver + shifted)
    return lengths[jax.random.permutation(jax.random.fold_in(key, 2), amount)]


def gaussian(rng, shape, spread, limit, split=(), kind=jnp.bfloat16):
    values = jax.random.normal(rng, shape, jnp.float32) * spread
    if len(split) > 0:
        values = levels(rng, shape, split, -0.22, 0.18) * values
    return jnp.clip(values, min=-limit, max=limit).astype(kind)


def setup_inputs(seed: int = 0) -> dict:
    streams_of = jax.random.split(jax.random.key(seed), 22)
    return {
        "hidden_in": gaussian(streams_of[0], (MB, SEQS, SEQ, D), 1.0, 6.0, ((1, 32),)),
        "encoded": gaussian(streams_of[1], (MB, SEQS, ENC, D), 1.0, 6.0, ((1, 32),)),
        "dec_segments": jax.vmap(lambda own: jnp.searchsorted(jnp.cumsum(ragged_sizes(own, DOCS, SEQ, SEQ // 2, 0)), jnp.arange(SEQ), side="right"))(jax.random.split(streams_of[2], MB * SEQS)).reshape((MB, SEQS, SEQ)).astype(jnp.int32),
        "enc_segments": jax.vmap(lambda own: jnp.searchsorted(jnp.cumsum(ragged_sizes(own, DOCS, ENC, ENC // 2, 0)), jnp.arange(ENC), side="right"))(jax.random.split(streams_of[3], MB * SEQS)).reshape((MB, SEQS, ENC)).astype(jnp.int32),
        "buckets": touch_ends(jax.random.randint(streams_of[4], (SEQ,), 0, NB), jax.random.fold_in(streams_of[4], 1), 0, NB - 1).astype(jnp.int32),
        "out_cot": gaussian(streams_of[5], (MB, SEQS, SEQ, D), 1.0, 6.0, ((1, 32),)),
        "norm_self": jnp.clip(1.0 + 0.1 * jax.random.normal(streams_of[6], (D,), jnp.float32), 0.5, 1.5).astype(jnp.bfloat16),
        "self_query": gaussian(streams_of[7], (D, D), (D * HEAD) ** -0.5, 0.0234375, ((0, 16),)),
        "self_key": gaussian(streams_of[8], (D, D), D ** -0.5, 0.1875, ((0, 16),)),
        "self_value": gaussian(streams_of[9], (D, D), D ** -0.5, 0.1875, ((0, 16),)),
        "self_out": gaussian(streams_of[10], (D, D), (D // 64) ** -0.5, 1.5, ((0, 16),)),
        "relative_bias_table": gaussian(streams_of[11], (NB, HEADS), 1.0, 4.0),
        "norm_cross": jnp.clip(1.0 + 0.1 * jax.random.normal(streams_of[12], (D,), jnp.float32), 0.5, 1.5).astype(jnp.bfloat16),
        "cross_query": gaussian(streams_of[13], (D, D), (D * HEAD) ** -0.5, 0.0234375, ((0, 16),)),
        "cross_key": gaussian(streams_of[14], (D, D), D ** -0.5, 0.1875, ((0, 16),)),
        "cross_value": gaussian(streams_of[15], (D, D), D ** -0.5, 0.1875, ((0, 16),)),
        "cross_out": gaussian(streams_of[16], (D, D), (D // 64) ** -0.5, 1.5, ((0, 16),)),
        "norm_ff": jnp.clip(1.0 + 0.1 * jax.random.normal(streams_of[17], (D,), jnp.float32), 0.5, 1.5).astype(jnp.bfloat16),
        "ff_gate": gaussian(streams_of[18], (D, FF), D ** -0.5, 0.1875, ((0, 16),)),
        "ff_up": gaussian(streams_of[19], (D, FF), D ** -0.5, 0.1875, ((0, 16),)),
        "ff_down": gaussian(streams_of[20], (FF, D), (FF // 4) ** -0.5, 0.21875, ((0, 16),)),
    }


@jax.custom_vjp
def low(v):
    return lax.optimization_barrier(v.astype(jnp.bfloat16)).astype(jnp.float32)

@jax.custom_vjp
def low_back(v):
    return v

def low_keep(v):
    return (low(v), None)

def low_pass(kept, grad):
    return (grad,)

def back_keep(v):
    return (v, None)

def back_low(kept, grad):
    return (low(grad),)
low.defvjp(low_keep, low_pass)
low_back.defvjp(back_keep, back_low)
EPS = 1e-06
NEG = -1e+30
HIGH = lax.Precision.HIGHEST

def matmul(left, right):
    return jnp.dot(left, right, precision=HIGH, preferred_element_type=jnp.float32)

def rms_norm(values, gain):
    return values * lax.rsqrt(lax.optimization_barrier(jnp.mean(values * values, axis=-1, keepdims=True)) + EPS) * gain

def split_heads(values):
    return values.reshape(values.shape[0], HEADS, HEAD)

def attend(query, keys, values, position_bias, allowed):
    scores = jnp.einsum('qhd,khd->hqk', split_heads(query), split_heads(keys), precision=HIGH) + position_bias
    scores = low_back(scores)
    scores = jnp.where(allowed[None], scores, NEG)
    top = lax.optimization_barrier(jnp.max(scores, axis=-1, keepdims=True))
    expo = jnp.exp(scores - top)
    probs = low(expo / lax.optimization_barrier(jnp.sum(expo, axis=-1, keepdims=True)))
    mixed = jnp.einsum('hqk,khd->qhd', probs, split_heads(values), precision=HIGH)
    return mixed.reshape(query.shape[0], D)

def layer(tokens, encoded, dec_seg, enc_seg, pair_bucket, params):
    gain_self, w_query, w_key, w_value, w_out, table, gain_cross, c_query, c_key, c_value, c_out, gain_ff, w_gate, w_up, w_down = params
    spots = jnp.arange(tokens.shape[0])
    self_mask = (spots[:, None] >= spots[None, :]) & (dec_seg[:, None] == dec_seg[None, :])
    cross_mask = dec_seg[:, None] == enc_seg[None, :]
    position_bias = jnp.transpose(table[pair_bucket], (2, 0, 1))
    first = low(rms_norm(tokens, gain_self))
    query = low_back(low(matmul(first, w_query)))
    keys = low_back(low(matmul(first, w_key)))
    values = low_back(low(matmul(first, w_value)))
    mixed = low_back(low(attend(query, keys, values, position_bias, self_mask)))
    middle = tokens + low_back(matmul(mixed, w_out))
    second = low(rms_norm(middle, gain_cross))
    cquery = low_back(low(matmul(second, c_query)))
    ckeys = low_back(low(matmul(encoded, c_key)))
    cvalues = low_back(low(matmul(encoded, c_value)))
    cmixed = low_back(low(attend(cquery, ckeys, cvalues, 0.0, cross_mask)))
    late = middle + low_back(matmul(cmixed, c_out))
    third = low(rms_norm(late, gain_ff))
    gate = low_back(matmul(third, w_gate))
    upper = low_back(matmul(third, w_up))
    hidden = low(jax.nn.gelu(gate, approximate=True) * upper)
    return late + low_back(matmul(hidden, w_down))

def reference(hidden_in, encoded, dec_segments, enc_segments, buckets, out_cot, norm_self, self_query, self_key, self_value, self_out, relative_bias_table, norm_cross, cross_query, cross_key, cross_value, cross_out, norm_ff, ff_gate, ff_up, ff_down):
    attention_weights = (norm_self, self_query, self_key, self_value, self_out, relative_bias_table, norm_cross, cross_query, cross_key, cross_value, cross_out, norm_ff, ff_gate, ff_up, ff_down)
    params = tuple((item.astype(jnp.float32) for item in attention_weights))
    count = MB * SEQS
    group = math.gcd(count, max(1, 4096 // SEQ))
    blocks = count // group
    spots = jnp.arange(SEQ)
    pair_bucket = buckets[jnp.maximum(spots[:, None] - spots[None, :], 0)]

    def regroup(array):
        return array.reshape((blocks, group) + array.shape[2:])

    def step(totals, items):
        tokens, enc_rows, dec_seg, enc_seg, cot = items

        def forward(tok_rows, enc_vals, *layer_params):
            return jax.vmap(lambda a, b, c, e: layer(a, b, c, e, pair_bucket, layer_params))(tok_rows, enc_vals, dec_seg, enc_seg)
        result, pull = jax.vjp(forward, tokens.astype(jnp.float32), enc_rows.astype(jnp.float32), *params)
        grads = pull(cot.astype(jnp.float32))
        totals = tuple((acc + grad for acc, grad in zip(totals, grads[2:])))
        return (totals, (result.astype(jnp.bfloat16), grads[0], grads[1]))
    zeros = tuple((jnp.zeros_like(item) for item in params))
    totals, (result, grad_tok, grad_enc) = lax.scan(step, zeros, (regroup(hidden_in), regroup(encoded), regroup(dec_segments), regroup(enc_segments), regroup(out_cot)))
    return (result.reshape(MB, SEQS, SEQ, D), grad_tok.reshape(MB, SEQS, SEQ, D), grad_enc.reshape(MB, SEQS, ENC, D), totals[0], totals[1], totals[2], totals[3], totals[4], totals[5], totals[6], totals[7], totals[8], totals[9], totals[10], totals[11], totals[12], totals[13], totals[14])
```

```python
import functools
import math

import jax
import jax.numpy as jnp
from jax import lax
from jax.experimental import pallas as pl
from jax.experimental.pallas import tpu as pltpu
from jax.sharding import PartitionSpec as P

MESH = pl.DeviceIdType.MESH
BF = jnp.bfloat16
F32 = jnp.float32
EPS = 1e-06
NEG = -1e30
C1 = math.sqrt(2.0 / math.pi)
C2 = 0.044715
TILE = 256


def each(count, f):
    def step(i, carry):
        f(i)
        return carry
    lax.fori_loop(0, count, step, 0)


def tile_at(i, size=TILE):
    return pl.ds(pl.multiple_of(i * size, size), size)


def dot(a, b):
    return jnp.dot(a, b, preferred_element_type=F32)


def dot_t(a, b):
    return lax.dot_general(a, b, (((1,), (1,)), ((), ())), preferred_element_type=F32)


def dot_rows(a, b):
    return lax.dot_general(a, b, (((0,), (0,)), ((), ())), preferred_element_type=F32)


def normed(src, gain, dst):
    def rows(i):
        r = tile_at(i, 32)
        v = src[r, :].astype(F32)
        t = lax.rsqrt(jnp.mean(v * v, axis=-1, keepdims=True) + EPS)
        dst[r, :] = (v * t * gain[...]).astype(BF)
    each(src.shape[0] // 32, rows)


def norm_back(src, gain, grad, base, dst, gain_sum):
    gain_sum[...] = jnp.zeros(gain_sum.shape, F32)

    def rows(i):
        r = tile_at(i, 16)
        v = src[r, :].astype(F32)
        dy = grad[r, :]
        g = gain[...]
        t = lax.rsqrt(jnp.mean(v * v, axis=-1, keepdims=True) + EPS)
        vt = v * t
        gdy = g * dy
        inner = jnp.mean(vt * gdy, axis=-1, keepdims=True)
        dst[r, :] = base[r, :].astype(F32) + t * (gdy - vt * inner)
        gain_sum[...] += jnp.sum(vt * dy, axis=0, keepdims=True)
    each(src.shape[0] // 16, rows)


def turn(src, dst):
    for b in range(src.shape[0] // 128):
        def block(c, b=b):
            dst[tile_at(c), b * 128:(b + 1) * 128] = src[b * 128:(b + 1) * 128, tile_at(c)].T
        each(src.shape[1] // TILE, block)


def head_masks():
    lane = lax.broadcasted_iota(jnp.int32, (1, 128), 1)
    even = (lane < 64).astype(F32).astype(BF)
    return even, (lane >= 64).astype(F32).astype(BF)


def pair_rows(x, masks):
    return jnp.concatenate([x * masks[0], x * masks[1]], axis=0)


def side_by_side(x):
    half = x.shape[0] // 2
    return jnp.concatenate([x[:half], x[half:]], axis=1)


def attend(i, q, k, v, p, o, neg, bias, length, keys):
    masks = head_masks()
    pairs = q.shape[1] // 128
    b, pair = lax.div(i, pairs), lax.rem(i, pairs)
    lanes = tile_at(pair, 128)
    rows, krows = tile_at(b, length), tile_at(b, keys)
    s = dot_t(pair_rows(q[rows, lanes], masks), k[krows, lanes])
    if bias is not None:
        s = s + bias[pair]
    n = neg[b]
    s = s + jnp.concatenate([n, n], axis=0)
    e = jnp.exp(s - jnp.max(s, axis=-1, keepdims=True))
    pb = (e * (1.0 / jnp.sum(e, axis=-1, keepdims=True))).astype(BF)
    p[i] = pb
    o[rows, lanes] = dot(side_by_side(pb), pair_rows(v[krows, lanes], masks)).astype(BF)


def attend_back(i, q, k, v, p, do, dq, dk, dv, diag, length, keys):
    masks = head_masks()
    pairs = q.shape[1] // 128
    b, pair = lax.div(i, pairs), lax.rem(i, pairs)
    lanes = tile_at(pair, 128)
    rows, krows = tile_at(b, length), tile_at(b, keys)
    dos = pair_rows(do[rows, lanes], masks)
    dp = dot_t(dos, v[krows, lanes])
    pb = p[i]
    pf = pb.astype(F32)
    ds = (pf * (dp - jnp.sum(pf * dp, axis=-1, keepdims=True))).astype(BF)
    dq[rows, lanes] = dot(side_by_side(ds), pair_rows(k[krows, lanes], masks)).astype(BF)
    dk[krows, lanes] = dot_rows(ds, pair_rows(q[rows, lanes], masks)).astype(BF)
    dv[krows, lanes] = dot_rows(pb, dos).astype(BF)
    if diag is not None:
        i0 = lax.broadcasted_iota(jnp.int32, (length, length), 0)
        i1 = lax.broadcasted_iota(jnp.int32, (length, length), 1)
        flip = (i0 + i1 == length - 1).astype(F32).astype(BF)
        for h in range(2):
            u = pltpu.roll(dot(flip, ds[h * length:(h + 1) * length]), 1, 1, stride=1, stride_axis=0)
            diag[2 * pair + h] += jnp.sum(u, axis=0, keepdims=True)


def position_bias(taps, bias, length):
    def pair(i):
        for h in range(2):
            w = jnp.broadcast_to(taps[2 * i + h], (length, length))
            bias[i, h * length:(h + 1) * length, :] = pltpu.roll(w, 0, 1, stride=1, stride_axis=0)
    each(bias.shape[0], pair)


def seg_masks(dcol, drow, erow, neg_self, neg_cross, length):
    for b in range(dcol.shape[0]):
        col = dcol[b]
        i = lax.broadcasted_iota(jnp.int32, (length, length), 0)
        j = lax.broadcasted_iota(jnp.int32, (length, length), 1)
        neg_self[b] = jnp.where((j <= i) & (col == drow[b]), 0.0, NEG)
        neg_cross[b] = jnp.where(col == erow[b], 0.0, NEG)


def project(a, w, dst, base=None, kind=BF):
    def tile(c):
        v = dot(a[...], w[:, tile_at(c)])
        if base is not None:
            v = v + base[:, tile_at(c)].astype(F32)
        dst[:, tile_at(c)] = v.astype(kind)
    each(dst.shape[1] // TILE, tile)


def project_t(terms, dst, kind=F32):
    def tile(c):
        v = None
        for a, w in terms:
            u = dot_t(a[...], w[tile_at(c), :])
            v = u if v is None else v + u
        dst[:, tile_at(c)] = v.astype(kind)
    each(dst.shape[1] // TILE, tile)


def feed_tile(c, h, cot, wg, wu, wd, hid, dgate, dup):
    cols = tile_at(c)
    hv = h[...]
    gate = dot(hv, wg[:, cols])
    up = dot(hv, wu[:, cols])
    dhid = dot_t(cot[...], wd[cols, :])
    sq = gate * gate
    th = jnp.tanh(C1 * gate * (1.0 + C2 * sq))
    hp = 0.5 * (1.0 + th)
    act = gate * hp
    hid[:, cols] = (act * up).astype(BF)
    slope = hp + (0.5 * C1) * gate * (1.0 - th * th) * (1.0 + (3.0 * C2) * sq)
    dgate[:, cols] = (dhid * up * slope).astype(BF)
    dup[:, cols] = (dhid * act).astype(BF)


def geometry(n):
    chips = n // 2
    side = chips // 2
    s = lax.axis_index("shard")
    rep = lax.axis_index("rep")
    core = lax.rem(s, 2)
    chip = lax.div(s, 2)
    x = lax.rem(chip, 2)
    z = lax.div(chip, 2)
    ring = z + x * (chips - 1 - 2 * z)

    def device_at(position):
        p = lax.rem(position + 2 * chips, chips)
        px = lax.div(p, side)
        pz = p + px * (chips - 1 - 2 * p)
        return (pz * 2 + px) * 2 + core

    return chips, s, rep, core, ring, device_at


def rdma(src, dst, ss, rs, dev):
    return pltpu.make_async_remote_copy(src_ref=src, dst_ref=dst, send_sem=ss, recv_sem=rs, device_id=dev, device_id_type=MESH)


class Gather:
    def __init__(self, geo, pieces, across, sems):
        self.chips, self.me, self.rep, self.core, self.ring, self.device_at = geo
        self.hops = self.chips - 1
        self.pieces, self.across = pieces, across
        self.ring_s, self.ring_r, self.sib_s, self.sib_r, self.y_s, self.y_r, self.yy_s, self.yy_r, self.own_s, self.own_r = sems
        self.other = 1 - 2 * self.core
        self.sibling = (self.me + self.other, self.rep)
        self.opposite = (self.me, 1 - self.rep)
        self.ahead = ((self.device_at(self.ring + 1), self.rep), (self.device_at(self.ring - 1), self.rep))

    def source(self, way, t):
        return self.device_at(self.ring - 1 - t) if way == 0 else self.device_at(self.ring + 1 + t)

    def each(self, rep, count=None):
        most = max(len(self.pieces(0, rep)), len(self.pieces(1, rep)))
        for p in range(most if count is None else count):
            for way in range(2):
                ps = self.pieces(way, rep)
                if p < len(ps):
                    yield way, p, ps[p]

    def ring_copy(self, way, t, p, ref):
        return rdma(ref, ref, self.ring_s.at[way, t, p], self.ring_r.at[way, t, p], self.ahead[way])

    def sib_copy(self, way, t, p, ref):
        return rdma(ref, ref, self.sib_s.at[way, t, p], self.sib_r.at[way, t, p], self.sibling)

    def y_copy(self, way, t, p, ref):
        return rdma(ref, ref, self.y_s.at[way, t, p], self.y_r.at[way, t, p], self.opposite)

    def yy_copy(self, way, t, p, ref):
        return rdma(ref, ref, self.yy_s.at[way, t, p], self.yy_r.at[way, t, p], self.sibling)

    def own_copies(self, src):
        found = []
        for rep in (self.rep, 1 - self.rep):
            for way, p, ref in self.each(rep, None if rep is self.rep else self.across):
                i = 0 if rep is self.rep else 1
                r = ref(src)
                found.append(rdma(r, r, self.own_s.at[i, way, p], self.own_r.at[i, way, p], self.sibling))
        return found

    def start(self):
        for way, p, ref in self.each(self.rep):
            self.ring_copy(way, 0, p, ref(self.me)).start()
        for c in self.own_copies(self.me):
            c.start()

    def hop(self, t, last=False):
        for way, p, ref in self.each(self.rep):
            r = ref(self.source(way, t))
            self.ring_copy(way, t, p, r).wait_recv()
            if not last:
                self.ring_copy(way, t + 1, p, r).start()
            if p < self.across:
                self.y_copy(way, t, p, r).start()
            self.sib_copy(way, t, p, r).start()

    def relay(self, t):
        for way, p, ref in self.each(1 - self.rep, self.across):
            r = ref(self.source(way, t))
            self.y_copy(way, t, p, r).wait_recv()
            self.yy_copy(way, t, p, r).start()

    def complete(self):
        def step(t):
            for way, p, ref in self.each(self.rep):
                self.sib_copy(way, t, p, ref(self.source(way, t) + self.other)).wait_recv()
            for way, p, ref in self.each(1 - self.rep, self.across):
                self.yy_copy(way, t, p, ref(self.source(way, t) + self.other)).wait_recv()
        each(self.hops, step)
        for c in self.own_copies(self.me + self.other):
            c.wait_recv()

    def drain(self):
        def step(t):
            for way, p, ref in self.each(self.rep):
                r = ref(self.source(way, t))
                self.ring_copy(way, t, p, r).wait_send()
                self.sib_copy(way, t, p, r).wait_send()
                if p < self.across:
                    self.y_copy(way, t, p, r).wait_send()
            for way, p, ref in self.each(1 - self.rep, self.across):
                self.yy_copy(way, t, p, ref(self.source(way, t))).wait_send()
        each(self.hops, step)
        for c in self.own_copies(self.me):
            c.wait_send()


def gather_sems(hops, pieces, across):
    dma = pltpu.SemaphoreType.DMA
    return [dma((2, hops, pieces))] * 4 + [dma((2, hops, across))] * 4 + [dma((2, 2, pieces))] * 2


def forward_kernel(n, dims, *refs):
    length, keys = dims
    ins, refs = refs[:11], refs[11:]
    gn_in, x, enc, cot, dcol, drow, erow, taps = refs[:8]
    w_out, out, xt, enct, hfft, hidt, dgu, r1, x1, qkv, cq, ckv, p1, p2, gain3, gains = refs[8:24]
    w, gu, dn, gn, bias, neg_s, neg_c, h, hid, x2, dh, o = refs[24:36]
    first_sems, second_sems = refs[36:46], refs[46:56]
    load_s, store_s = refs[56:58]
    geo = geometry(n)
    chips, me, rep, core, ring, device_at = geo
    hops = chips - 1
    rows, rows_d = ins[0].shape[0], ins[10].shape[0]
    half, half_g = w.shape[2] // 2, gu.shape[2] // 2
    count = dcol.shape[0]
    pairs = w.shape[2] // 128

    def block(src):
        return pl.ds(pl.multiple_of(src * rows, rows), rows)

    def block_d(src):
        return pl.ds(pl.multiple_of(src * rows_d, rows_d), rows_d)

    def attention_pieces(way, r):
        c = pl.ds(way * half, half)
        found = [lambda s: w.at[r, block(s), c], lambda s: w.at[4 + r, block(s), c],
                 lambda s: w.at[pl.ds(2, 2), block(s), c], lambda s: w.at[pl.ds(6, 2), block(s), c]]
        return found + [lambda s: gn.at[s]] if way == 0 else found

    def feed_pieces(way, r):
        return [lambda s: gu.at[r, block(s), pl.ds(way * half_g, half_g)], lambda s: dn.at[block_d(s), pl.ds(way * half, half)]]

    first = Gather(geo, attention_pieces, 2, first_sems)
    second = Gather(geo, feed_pieces, 1, second_sems)

    places = [w.at[i, block(me), :] for i in range(8)] + [gu.at[i, block(me), :] for i in range(2)] + [dn.at[block_d(me), :]]
    loads = [pltpu.make_async_copy(a, b, load_s.at[i]) for i, (a, b) in enumerate(zip(ins + (gn_in,), places + [gn.at[me]]))]
    for c in loads:
        c.start()
    barrier = pltpu.get_barrier_semaphore()
    for dev in first.ahead + (first.sibling, first.opposite):
        pl.semaphore_signal(barrier, inc=1, device_id=dev, device_id_type=MESH)
    for c in loads:
        c.wait()
    pl.semaphore_wait(barrier, 4)

    first.start()
    turn(enc, enct)
    first.hop(0)
    position_bias(taps, bias, length)
    seg_masks(dcol, drow, erow, neg_s, neg_c, length)

    def middle(t):
        first.hop(t)
        first.relay(t - 1)
    lax.fori_loop(1, hops - 1, lambda t, c: (middle(t), c)[1], 0)
    second.start()
    first.hop(hops - 1, True)
    first.relay(hops - 2)
    first.relay(hops - 1)
    first.complete()
    store = pltpu.make_async_copy(w, w_out, store_s)
    store.start()

    per = 128 // rows
    for j in range(w.shape[2] // 128):
        v = gn[j * per]
        for i in range(1, per):
            v = v + gn[j * per + i]
        for i in range(3):
            gains[i, :, j * 128:(j + 1) * 128] = v[i:i + 1, :]

    def some(begin, end, f):
        lax.fori_loop(begin, end, lambda i, c: (f(i), c)[1], 0)

    def heads():
        normed(x, gains.at[0], h)
        for i in range(3):
            project(h, w.at[i], qkv.at[i])

    def own(i):
        attend(i, qkv.at[0], qkv.at[1], qkv.at[2], p1, o, neg_s, bias, length, length)

    def cross_heads():
        turn(h, xt.at[0])
        turn(o, xt.at[1])
        project(o, w.at[3], x1, base=x, kind=F32)
        normed(x1, gains.at[1], h)
        project(h, w.at[4], cq)

    def cross_keys():
        turn(h, xt.at[2])
        for i in range(2):
            project(enc, w.at[6 + i], ckv.at[i])

    def cross(i):
        attend(i, cq, ckv.at[0], ckv.at[1], p2, o, neg_c, None, length, keys)

    def before_feed():
        turn(o, xt.at[3])
        project(o, w.at[5], x2, base=x1, kind=F32)
        normed(x2, gains.at[2], h)
        turn(h, hfft)

    total = count * pairs
    mid = total // 2
    chunks = [heads, lambda: some(0, mid, own), lambda: some(mid, total, own), cross_heads, cross_keys,
              lambda: some(0, mid, cross), lambda: some(mid, total, cross)]
    for t in range(len(chunks)):
        chunks[t]()
        second.hop(t, t == hops - 1)
        if t > 0:
            second.relay(t - 1)
    if hops > len(chunks):
        def rest(t):
            second.hop(t)
            second.relay(t - 1)
        some(len(chunks), hops - 1, rest)
        second.hop(hops - 1, True)
        second.relay(hops - 2)
    before_feed()
    second.relay(hops - 1)
    second.complete()

    each(hid.shape[1] // TILE, lambda c: feed_tile(c, h, cot, gu.at[0], gu.at[1], dn, hid, dgu.at[0], dgu.at[1]))
    project_t([(dgu.at[0], gu.at[0]), (dgu.at[1], gu.at[1])], dh)
    norm_back(x2, gains.at[2], dh, cot, r1, gain3)
    project(hid, dn, out, base=x2)
    turn(hid, hidt)
    first.drain()
    second.drain()
    store.wait()


def forward(n, weights, gn, x, enc, cot, dcol, drow, erow, taps):
    hops = n // 2 - 1
    rows, width = weights[0].shape
    ff = weights[8].shape[1]
    tokens, etokens = x.shape[0], enc.shape[0]
    count, length, _ = dcol.shape
    keys = etokens // count
    pairs = width // 128
    S = jax.ShapeDtypeStruct

    def v(*shape, t=BF):
        return pltpu.VMEM(shape, t)

    vm, hbm = pl.BlockSpec(memory_space=pltpu.VMEM), pl.BlockSpec(memory_space=pl.ANY)
    return pl.pallas_call(
        functools.partial(forward_kernel, n, (length, keys)),
        name="gather_forward",
        out_shape=(
            S((8, width, width), BF), S((tokens, width), BF), S((4, width, tokens), BF), S((width, etokens), BF),
            S((width, tokens), BF), S((ff, tokens), BF), S((2, tokens, ff), BF), S((tokens, width), F32), S((tokens, width), F32),
            S((3, tokens, width), BF), S((tokens, width), BF), S((2, etokens, width), BF),
            S((count * pairs, 2 * length, length), BF), S((count * pairs, 2 * length, keys), BF),
            S((1, width), F32), S((3, 1, width), F32),
        ),
        in_specs=[hbm] * 12 + [vm] * 7,
        out_specs=[hbm] + [vm] * 15,
        scratch_shapes=[
            v(8, width, width), v(2, width, ff), v(ff, width), v(n, 8, 128, t=F32),
            v(pairs, 2 * length, length, t=F32), v(count, length, length, t=F32), v(count, length, keys, t=F32),
            v(tokens, width), v(tokens, ff), v(tokens, width, t=F32), v(tokens, width, t=F32), v(tokens, width),
        ] + gather_sems(hops, 5, 2) + gather_sems(hops, 2, 1) + [pltpu.SemaphoreType.DMA((12,)), pltpu.SemaphoreType.DMA(())],
        compiler_params=pltpu.CompilerParams(collective_id=0, has_side_effects=True, vmem_limit_bytes=67043328),
    )(*weights, gn, x, enc, cot, dcol, drow, erow, taps)


def backward_kernel(dims, *refs):
    length, keys = dims
    x, w, gains, r1, x1, qkv, cq, ckv, p1, p2, dtok, denc, dy, dye, gain12, diag, dh, r0, do = refs
    diag[...] = jnp.zeros(diag.shape, F32)
    total = p1.shape[0]
    dy[5] = r1[...].astype(BF)
    project_t([(dy.at[5], w.at[5])], do, kind=BF)
    each(total, lambda i: attend_back(i, cq, ckv.at[0], ckv.at[1], p2, do, dy.at[4], dye.at[0], dye.at[1], None, length, keys))
    project_t([(dye.at[0], w.at[6]), (dye.at[1], w.at[7])], denc)
    project_t([(dy.at[4], w.at[4])], dh)
    norm_back(x1, gains.at[1], dh, r1, r0, gain12.at[1])
    dy[3] = r0[...].astype(BF)
    project_t([(dy.at[3], w.at[3])], do, kind=BF)
    each(total, lambda i: attend_back(i, qkv.at[0], qkv.at[1], qkv.at[2], p1, do, dy.at[0], dy.at[1], dy.at[2], diag, length, length))
    project_t([(dy.at[0], w.at[0]), (dy.at[1], w.at[1]), (dy.at[2], w.at[2])], dh)
    norm_back(x, gains.at[0], dh, r0, dtok, gain12.at[0])


def backward(x, w, gains, r1, x1, qkv, cq, ckv, p1, p2):
    tokens, width = x.shape
    etokens = ckv.shape[1]
    length, keys = p1.shape[2], p2.shape[2]
    S = jax.ShapeDtypeStruct
    vm = pl.BlockSpec(memory_space=pltpu.VMEM)
    return pl.pallas_call(
        functools.partial(backward_kernel, (length, keys)),
        name="attention_backward",
        out_shape=(S((tokens, width), F32), S((etokens, width), F32), S((6, tokens, width), BF), S((2, etokens, width), BF),
                   S((2, 1, width), F32), S((width // 64, 1, 128), F32)),
        in_specs=[vm] * 10,
        out_specs=[vm] * 6,
        scratch_shapes=[pltpu.VMEM((tokens, width), F32), pltpu.VMEM((tokens, width), F32), pltpu.VMEM((tokens, width), BF)],
        compiler_params=pltpu.CompilerParams(vmem_limit_bytes=67043328),
    )(x, w, gains, r1, x1, qkv, cq, ckv, p1, p2)


class Group:
    def __init__(self, left, right, size, refs):
        self.left, self.right = left, right
        self.count, self.rows, self.half, self.share = size
        self.ss, self.sr, self.ys, self.yr, self.rs, self.rr, self.own, self.got = refs

    def part(self, i, dev, start, width):
        return dot(self.left(i, dev), self.right(i, pl.ds(pl.multiple_of(start, 128), width)))


def group_shapes(size, slots):
    count, rows, half, share = size
    sib_slots, y_slots, ring_slots = slots

    def v(*shape):
        return pltpu.VMEM(shape, BF)
    return [v(2, 2, count, rows, half), v(sib_slots, 2, count, rows, half), v(2, 2, count, rows, share), v(y_slots, 2, count, rows, share),
            v(2, 2, count, rows, half - share), v(ring_slots, 2, count, rows, half - share)]


def reduce_sems(groups, slots):
    dma = pltpu.SemaphoreType.DMA
    sib_slots, y_slots, ring_slots = slots
    return [dma((2, 2, groups)), dma((sib_slots, 2, groups)), dma((2, 2, groups)), dma((y_slots, 2, groups)),
            dma((2, 2, groups)), dma((ring_slots, 2, groups)), dma((2, 2 * groups)), dma((2, 2 * groups)),
            pltpu.SemaphoreType.REGULAR((3, 2))]


class Reduce:
    def __init__(self, geo, groups, slots, sems):
        self.chips, self.me, self.rep, self.core, self.ring, self.device_at = geo
        self.groups = groups
        self.slots = slots
        self.sib_s, self.sib_r, self.y_s, self.y_r, self.ring_s, self.ring_r, self.fin_s, self.fin_r, self.free = sems
        self.other = 1 - self.rep
        self.sibling = (self.me + 1 - 2 * self.core, self.rep)
        self.opposite = (self.me, self.other)
        self.after = ((self.device_at(self.ring + 1), self.rep), (self.device_at(self.ring - 1), self.rep))

    def block(self, t, way, core):
        return self.device_at(self.ring + (2 * way - 1) * (1 + t)) + core - self.core

    def toward(self, way):
        return (self.after[0][0] + way * (self.after[1][0] - self.after[0][0]), self.rep)

    def behind(self, way):
        return (self.after[1][0] + way * (self.after[0][0] - self.after[1][0]), self.rep)

    def sib_copies(self, t, way):
        s, r = lax.rem(t, 2), lax.rem(t, self.slots[0])
        return [rdma(g.ss.at[s, way], g.sr.at[r, way], self.sib_s.at[s, way, i], self.sib_r.at[r, way, i], self.sibling)
                for i, g in enumerate(self.groups)]

    def y_copies(self, t, way):
        s, r = lax.rem(t, 2), lax.rem(t, self.slots[1])
        return [rdma(g.ys.at[s, way], g.yr.at[r, way], self.y_s.at[s, way, i], self.y_r.at[r, way, i], self.opposite)
                for i, g in enumerate(self.groups)]

    def ring_copies(self, t, way):
        s, r = lax.rem(t, 2), lax.rem(t + 1, self.slots[2])
        return [rdma(g.rs.at[s, way], g.rr.at[r, way], self.ring_s.at[s, way, i], self.ring_r.at[r, way, i], self.toward(way))
                for i, g in enumerate(self.groups)]

    def claim(self, kind, step, way):
        if self.slots[kind] < self.chips:
            @pl.when(step >= self.slots[kind])
            def _():
                pl.semaphore_wait(self.free.at[kind, way], 1)

    def release(self, kind, step, way, dev):
        if self.slots[kind] < self.chips:
            @pl.when(step + self.slots[kind] < self.chips)
            def _():
                pl.semaphore_signal(self.free.at[kind, way], inc=1, device_id=dev, device_id_type=MESH)

    def settle(self, t, copies):
        @pl.when(t >= 2)
        def _():
            for c in copies:
                c.wait_send()

    def to_sibling(self, t):
        s = lax.rem(t, 2)

        def go(way):
            dev = self.block(t, way, 1 - self.core)
            self.settle(t, self.sib_copies(t, way))
            for g in self.groups:
                for i in range(g.count):
                    g.ss[s, way, i] = g.part(i, dev, way * g.half, g.half).astype(BF)
            self.claim(0, t, way)
            for c in self.sib_copies(t, way):
                c.start()
        each(2, go)

    def to_across(self, t):
        s, r = lax.rem(t, 2), lax.rem(t, self.slots[0])

        def go(way):
            dev = self.block(t, way, self.core)
            self.settle(t, self.y_copies(t, way))
            for c in self.sib_copies(t, way):
                c.wait_recv()
            for g in self.groups:
                at = pl.multiple_of(self.other * g.share, 128)
                for i in range(g.count):
                    v = g.part(i, dev, way * g.half + at, g.share)
                    g.ys[s, way, i] = (v + g.sr[r, way, i, :, pl.ds(at, g.share)].astype(F32)).astype(BF)
            self.claim(1, t, way)
            for c in self.y_copies(t, way):
                c.start()
        each(2, go)

    def to_ring(self, t):
        s, b, y, r = lax.rem(t, 2), lax.rem(t, self.slots[0]), lax.rem(t, self.slots[1]), lax.rem(t, self.slots[2])

        for k, g in enumerate(self.groups):
            def go(way, k=k, g=g):
                dev = self.block(t, way, self.core)
                self.settle(t, self.ring_copies(t, way)[k:k + 1])
                self.y_copies(t, way)[k].wait_recv()

                @pl.when(t >= 1)
                def _():
                    self.ring_copies(t - 1, way)[k].wait_recv()
                at = pl.multiple_of(self.rep * g.share, 128)
                for i in range(g.count):
                    v = g.part(i, dev, way * g.half + at, g.share) + g.sr[b, way, i, :, pl.ds(at, g.share)].astype(F32)
                    v = v + g.yr[y, way, i].astype(F32) + g.rr[r, way, i, :, :g.share].astype(F32)
                    g.rs[s, way, i, :, :g.share] = v.astype(BF)
                    v = g.part(i, dev, way * g.half + 2 * g.share, g.half - 2 * g.share)
                    v = v + g.sr[b, way, i, :, 2 * g.share:].astype(F32) + g.rr[r, way, i, :, g.share:].astype(F32)
                    g.rs[s, way, i, :, g.share:] = v.astype(BF)

                @pl.when(t < self.chips - 1)
                def _():
                    if k == 0:
                        self.claim(2, t + 1, way)
                    self.ring_copies(t, way)[k].start()
                if k == len(self.groups) - 1:
                    self.release(0, t, way, self.sibling)
                    self.release(1, t, way, self.opposite)
                    self.release(2, t, way, self.behind(way))
            each(2, go)

    def prepare(self):
        for g in self.groups:
            g.rr[0] = jnp.zeros(g.rr.shape[1:], BF)

    def final_copies(self):
        s = (self.chips - 1) % 2
        found = []
        for way in range(2):
            for i, g in enumerate(self.groups):
                mine = g.rs.at[s, way]
                cols = pl.ds(pl.multiple_of(way * g.half + self.rep * g.share, 128), g.share)
                wide = g.half - 2 * g.share
                found.append(rdma(mine.at[:, :, pl.ds(0, g.share)], g.own.at[:, :, cols],
                                  self.fin_s.at[way, 2 * i], self.fin_r.at[way, 2 * i], self.opposite))
                found.append(rdma(mine.at[:, :, pl.ds(g.share, wide)], g.got.at[:, :, pl.ds(way * wide, wide)],
                                  self.fin_s.at[way, 2 * i + 1], self.fin_r.at[way, 2 * i + 1], self.opposite))
        return found

    def send_finals(self):
        s = (self.chips - 1) % 2
        for c in self.final_copies():
            c.start()
        for way in range(2):
            for g in self.groups:
                cols = pl.ds(pl.multiple_of(way * g.half + self.rep * g.share, 128), g.share)
                g.own[:, :, cols] = g.rs[s, way, :, :, :g.share]
                g.own[:, :, way * g.half + 2 * g.share:(way + 1) * g.half] = g.rs[s, way, :, :, g.share:]

    def finish(self):
        for way in range(2):
            for i, g in enumerate(self.groups):
                wide = g.half - 2 * g.share
                ref = g.own.at[:, :, pl.ds(pl.multiple_of(way * g.half + self.other * g.share, 128), g.share)]
                rdma(ref, ref, self.fin_s.at[way, 2 * i], self.fin_r.at[way, 2 * i], self.opposite).wait_recv()
                ref = g.got.at[:, :, pl.ds(way * wide, wide)]
                rdma(ref, ref, self.fin_s.at[way, 2 * i + 1], self.fin_r.at[way, 2 * i + 1], self.opposite).wait_recv()
        for c in self.final_copies():
            c.wait_send()
        for way in range(2):
            for t in (self.chips - 2, self.chips - 1):
                for c in self.sib_copies(t, way) + self.y_copies(t, way):
                    c.wait_send()
            for c in self.ring_copies(self.chips - 2, way):
                c.wait_send()


class Butterfly:
    def __init__(self, geo, n, buf, got, sems):
        _, self.me, self.rep, _, _, _ = geo
        self.stages = n.bit_length() - 1
        self.buf, self.got = buf, got
        self.send, self.recv = sems

    def partner(self, bit):
        return (self.me + bit - 2 * bit * lax.rem(lax.div(self.me, bit), 2), self.rep)

    def copy(self, j, dev):
        return rdma(self.buf.at[j], self.got.at[j], self.send.at[j], self.recv.at[j], dev)

    def begin(self):
        self.copy(0, (self.me, 1 - self.rep)).start()

    def stage(self, j, bit):
        self.copy(j - 1, self.partner(bit)).wait_recv()
        self.buf[j] = self.buf[j - 1] + self.got[j - 1]
        self.copy(j, self.partner(bit)).start()

    def end(self, dst):
        self.copy(self.stages, self.partner(1)).wait_recv()
        dst[...] = self.buf[self.stages] + self.got[self.stages]
        for j in range(self.stages + 1):
            self.copy(j, self.partner(1)).wait_send()


def reduce_kernel(n, sizes, slots, *refs):
    xt, enct, hfft, hidt, dy, dye, dgu, cot, small = refs[:9]
    outs, small_o = refs[9:17], refs[17]
    bufs, sems = refs[18:42], refs[42:51]
    sm, sm_got, sm_s, sm_r = refs[51:]
    geo = geometry(n)
    chips, me, rep, core, ring, device_at = geo
    rows, rows_d = sizes[0][1], sizes[3][1]
    which = (0, 0, 0, 1, 2, 3)

    def block(dev, size):
        return pl.ds(pl.multiple_of(dev * size, size), size)
    lefts = [lambda i, dev: xt[which[i], block(dev, rows), :], lambda i, dev: enct[block(dev, rows), :],
             lambda i, dev: hfft[block(dev, rows), :], lambda i, dev: hidt[block(dev, rows_d), :]]
    rights = [lambda i, c: dy[i, :, c], lambda i, c: dye[i, :, c], lambda i, c: dgu[i, :, c], lambda i, c: cot[:, c]]
    groups = [Group(lefts[k], rights[k], sizes[k], bufs[6 * k:6 * k + 6] + outs[2 * k:2 * k + 2]) for k in range(4)]
    red = Reduce(geo, groups, slots, sems)
    tree = Butterfly(geo, n, sm, sm_got, (sm_s, sm_r))

    barrier = pltpu.get_barrier_semaphore()
    greet = [red.after[0], red.after[1], red.sibling, red.opposite] + [tree.partner(1 << j) for j in range(tree.stages)]
    for dev in greet:
        pl.semaphore_signal(barrier, inc=1, device_id=dev, device_id_type=MESH)
    pl.semaphore_wait(barrier, len(greet))

    red.prepare()
    sm[0] = small[...]
    tree.begin()
    red.to_sibling(0)
    red.to_sibling(1)
    red.to_across(0)
    red.to_sibling(2)
    red.to_across(1)

    def step(t, bit):
        red.to_ring(t)

        @pl.when(t + 2 < chips)
        def _():
            red.to_across(t + 2)

        @pl.when(t + 3 < chips)
        def _():
            red.to_sibling(t + 3)

        @pl.when(t < tree.stages)
        def _():
            tree.stage(t + 1, bit)
        return bit * 2

    lax.fori_loop(0, chips, step, 1)
    red.send_finals()
    tree.end(small_o)
    red.finish()


def shares(half):
    return max(1, half // 512) * 128


def reduce_grads(n, xt, enct, hfft, hidt, dy, dye, dgu, cot, small):
    chips = n // 2
    width, ff = dy.shape[2], dgu.shape[2]
    rows, rows_d = width // n, hidt.shape[0] // n
    sizes = [(6, rows, width // 2, shares(width // 2)), (2, rows, width // 2, shares(width // 2)),
             (2, rows, ff // 2, shares(ff // 2)), (1, rows_d, width // 2, shares(width // 2))]
    slots = (chips, chips, chips)
    stages = n.bit_length() - 1
    dma = pltpu.SemaphoreType.DMA
    S = jax.ShapeDtypeStruct
    vm = pl.BlockSpec(memory_space=pltpu.VMEM)
    outs = []
    for count, r, half, share in sizes:
        outs += [S((count, r, 2 * half), BF), S((count, r, 2 * (half - 2 * share)), BF)]
    return pl.pallas_call(
        functools.partial(reduce_kernel, n, sizes, slots),
        name="reduce_grads",
        out_shape=tuple(outs) + (S(small.shape, F32),),
        in_specs=[vm] * 9,
        out_specs=[vm] * 9,
        scratch_shapes=[b for size in sizes for b in group_shapes(size, slots)] + reduce_sems(4, slots)
        + [pltpu.VMEM((stages + 1,) + small.shape, F32)] * 2 + [dma((stages + 1,))] * 2,
        compiler_params=pltpu.CompilerParams(collective_id=1, has_side_effects=True, vmem_limit_bytes=67043328),
    )(xt, enct, hfft, hidt, dy, dye, dgu, cot, small)


def finish_kernel(sizes, *refs):
    at = 8
    for k, (count, rows, half, share) in enumerate(sizes):
        own, got = refs[2 * k], refs[2 * k + 1]
        wide = half - 2 * share
        for i in range(count):
            dst = refs[at]
            at += 1
            for way in range(2):
                lo = way * half
                dst[:, lo:lo + 2 * share] = own[i, :, lo:lo + 2 * share].astype(F32)
                v = own[i, :, lo + 2 * share:lo + half].astype(F32) + got[i, :, way * wide:(way + 1) * wide].astype(F32)
                dst[:, lo + 2 * share:lo + half] = v


def finish_grads(parts):
    sizes, outs = [], []
    for own, got in zip(parts[0::2], parts[1::2]):
        count, rows, width = own.shape
        half = width // 2
        sizes.append((count, rows, half, (half - got.shape[2] // 2) // 2))
        outs += [jax.ShapeDtypeStruct((rows, width), F32)] * count
    vm = pl.BlockSpec(memory_space=pltpu.VMEM)
    return pl.pallas_call(
        functools.partial(finish_kernel, sizes),
        name="finish_grads",
        out_shape=tuple(outs),
        in_specs=[vm] * len(parts),
        out_specs=[vm] * len(outs),
        compiler_params=pltpu.CompilerParams(vmem_limit_bytes=40 << 20),
    )(*parts)


def body(hidden_in, encoded, dec_segments, enc_segments, buckets, out_cot, norm_self, self_query, self_key, self_value,
         self_out, table, norm_cross, cross_query, cross_key, cross_value, cross_out, norm_ff, ff_gate, ff_up, ff_down, *, n):
    micro, per, length, width = hidden_in.shape
    keys = encoded.shape[2]
    count = micro * per
    rows, rows_d, ff = self_query.shape[0], ff_down.shape[0], ff_gate.shape[1]
    me = lax.axis_index("shard")
    spare = -rows_d % 16
    if spare:
        ff_down = jnp.pad(ff_down, ((0, spare), (0, 0)))
        ff_gate, ff_up = [jnp.pad(w.reshape(rows, n, rows_d), ((0, 0), (0, 0), (0, spare))).reshape(rows, -1) for w in (ff_gate, ff_up)]
    fit = 128 // rows
    lane = lax.rem(me, fit) * rows
    gn = jnp.pad(jnp.stack([norm_self, norm_cross, norm_ff]).astype(F32), ((0, 5), (0, 128 - rows)))
    gn = jnp.roll(gn, lane, axis=1) if fit > 1 else gn

    back = jnp.concatenate([buckets[:1], buckets[:0:-1]])
    hot = (back[None] == jnp.arange(table.shape[0])[:, None]).astype(BF)
    taps = jnp.einsum("mh,ml->hl", table, hot, preferred_element_type=F32)[:, None]

    x = hidden_in.reshape(count * length, width)
    enc = encoded.reshape(count * keys, width)
    cot = out_cot.reshape(count * length, width)
    dseg = dec_segments.reshape(count, length)
    eseg = enc_segments.reshape(count, keys)
    weights = (self_query, self_key, self_value, self_out, cross_query, cross_out, cross_key, cross_value, ff_gate, ff_up, ff_down)
    w, out, xt, enct, hfft, hidt, dgu, r1, x1, qkv, cq, ckv, p1, p2, gain3, gains = forward(
        n, weights, gn, x, enc, cot, dseg[:, :, None], dseg[:, None, :], eseg[:, None, :], taps)
    dtok, denc, dy, dye, gain12, diag = backward(x, w, gains, r1, x1, qkv, cq, ckv, p1, p2)
    small = jnp.concatenate([gain12.reshape(-1, 128), gain3.reshape(-1, 128), diag[:, 0]])
    *parts, small = reduce_grads(n, xt, enct, hfft, hidt, dy, dye, dgu, cot, small)
    gq, gk, gv, gso, gcq, gco, gck, gcv, gg, gup, gd = finish_grads(parts)
    if spare:
        gd = gd[:rows_d]
        gg, gup = [g.reshape(rows, n, -1)[:, :, :rows_d].reshape(rows, ff) for g in (gg, gup)]
    tiles = width // 128
    flat = small[:3 * tiles].reshape(3, width)
    own = lax.dynamic_slice(flat, (0, me * rows), (3, rows))
    dtable = jnp.einsum("hl,ml->mh", small[3 * tiles:], hot.astype(F32), precision=lax.Precision.HIGHEST)
    return (
        out.reshape(hidden_in.shape), dtok.reshape(hidden_in.shape), denc.reshape(encoded.shape),
        own[0], gq, gk, gv, gso, dtable, own[1], gcq, gck, gcv, gco, own[2], gg, gup, gd,
    )


def solution(mesh):
    tok = P(None, ("shard", "rep"), None, None)
    seg = P(None, ("shard", "rep"), None)
    vec, mat, rep = P("shard"), P("shard", None), P()
    return jax.shard_map(
        functools.partial(body, n=mesh.shape["shard"]),
        mesh=mesh,
        in_specs=(tok, tok, seg, seg, rep, tok, vec, mat, mat, mat, mat, rep, vec, mat, mat, mat, mat, vec, mat, mat, mat),
        out_specs=(tok, tok, tok, vec, mat, mat, mat, mat, rep, vec, mat, mat, mat, mat, vec, mat, mat, mat),
        check_vma=False,
    )
```

```python
import functools
import math

import jax
import jax.numpy as jnp
from jax import lax
from jax.experimental import pallas as pl
from jax.experimental.pallas import tpu as pltpu
from jax.sharding import PartitionSpec as P

MESH = pl.DeviceIdType.MESH
BF = jnp.bfloat16
F32 = jnp.float32
EPS = 1e-06
NEG = -1e30
C1 = math.sqrt(2.0 / math.pi)
C2 = 0.044715
TILE = 256


def each(count, f):
    def step(i, carry):
        f(i)
        return carry
    lax.fori_loop(0, count, step, 0)


def tile_at(i, size=TILE):
    return pl.ds(pl.multiple_of(i * size, size), size)


def dot(a, b):
    return jnp.dot(a, b, preferred_element_type=F32)


def dot_t(a, b):
    return lax.dot_general(a, b, (((1,), (1,)), ((), ())), preferred_element_type=F32)


def dot_rows(a, b):
    return lax.dot_general(a, b, (((0,), (0,)), ((), ())), preferred_element_type=F32)


def normed(src, gain, dst):
    def rows(i):
        r = tile_at(i, 32)
        v = src[r, :].astype(F32)
        t = lax.rsqrt(jnp.mean(v * v, axis=-1, keepdims=True) + EPS)
        dst[r, :] = (v * t * gain[...]).astype(BF)
    each(src.shape[0] // 32, rows)


def norm_back(src, gain, grad, base, dst, gain_sum):
    gain_sum[...] = jnp.zeros(gain_sum.shape, F32)

    def rows(i):
        r = tile_at(i, 16)
        v = src[r, :].astype(F32)
        dy = grad[r, :]
        g = gain[...]
        t = lax.rsqrt(jnp.mean(v * v, axis=-1, keepdims=True) + EPS)
        vt = v * t
        gdy = g * dy
        inner = jnp.mean(vt * gdy, axis=-1, keepdims=True)
        dst[r, :] = base[r, :].astype(F32) + t * (gdy - vt * inner)
        gain_sum[...] += jnp.sum(vt * dy, axis=0, keepdims=True)
    each(src.shape[0] // 16, rows)


def turn(src, dst):
    for b in range(src.shape[0] // 128):
        def block(c, b=b):
            dst[tile_at(c), b * 128:(b + 1) * 128] = src[b * 128:(b + 1) * 128, tile_at(c)].T
        each(src.shape[1] // TILE, block)


def head_masks():
    lane = lax.broadcasted_iota(jnp.int32, (1, 128), 1)
    even = (lane < 64).astype(F32).astype(BF)
    return even, (lane >= 64).astype(F32).astype(BF)


def pair_rows(x, masks):
    return jnp.concatenate([x * masks[0], x * masks[1]], axis=0)


def side_by_side(x):
    half = x.shape[0] // 2
    return jnp.concatenate([x[:half], x[half:]], axis=1)


def attend(i, q, k, v, p, o, neg, bias, length, keys):
    masks = head_masks()
    pairs = q.shape[1] // 128
    b, pair = lax.div(i, pairs), lax.rem(i, pairs)
    lanes = tile_at(pair, 128)
    rows, krows = tile_at(b, length), tile_at(b, keys)
    s = dot_t(pair_rows(q[rows, lanes], masks), k[krows, lanes])
    if bias is not None:
        s = s + bias[pair]
    n = neg[b]
    s = s + jnp.concatenate([n, n], axis=0)
    e = jnp.exp(s - jnp.max(s, axis=-1, keepdims=True))
    pb = (e * (1.0 / jnp.sum(e, axis=-1, keepdims=True))).astype(BF)
    p[i] = pb
    o[rows, lanes] = dot(side_by_side(pb), pair_rows(v[krows, lanes], masks)).astype(BF)


def attend_back(i, q, k, v, p, do, dq, dk, dv, diag, length, keys):
    masks = head_masks()
    pairs = q.shape[1] // 128
    b, pair = lax.div(i, pairs), lax.rem(i, pairs)
    lanes = tile_at(pair, 128)
    rows, krows = tile_at(b, length), tile_at(b, keys)
    dos = pair_rows(do[rows, lanes], masks)
    dp = dot_t(dos, v[krows, lanes])
    pb = p[i]
    pf = pb.astype(F32)
    ds = (pf * (dp - jnp.sum(pf * dp, axis=-1, keepdims=True))).astype(BF)
    dq[rows, lanes] = dot(side_by_side(ds), pair_rows(k[krows, lanes], masks)).astype(BF)
    dk[krows, lanes] = dot_rows(ds, pair_rows(q[rows, lanes], masks)).astype(BF)
    dv[krows, lanes] = dot_rows(pb, dos).astype(BF)
    if diag is not None:
        i0 = lax.broadcasted_iota(jnp.int32, (length, length), 0)
        i1 = lax.broadcasted_iota(jnp.int32, (length, length), 1)
        flip = (i0 + i1 == length - 1).astype(F32).astype(BF)
        for h in range(2):
            u = pltpu.roll(dot(flip, ds[h * length:(h + 1) * length]), 1, 1, stride=1, stride_axis=0)
            diag[2 * pair + h] += jnp.sum(u, axis=0, keepdims=True)


def position_bias(taps, bias, length):
    def pair(i):
        for h in range(2):
            w = jnp.broadcast_to(taps[pl.ds(2 * i + h, 1), :], (length, length))
            bias[i, h * length:(h + 1) * length, :] = pltpu.roll(w, 0, 1, stride=1, stride_axis=0)
    each(bias.shape[0], pair)


def seg_masks(drow, erow, neg_self, neg_cross, length):
    for b in range(drow.shape[0]):
        row = drow[b].astype(F32)
        col = jnp.broadcast_to(row, (length, length)).T
        i = lax.broadcasted_iota(jnp.int32, (length, length), 0)
        j = lax.broadcasted_iota(jnp.int32, (length, length), 1)
        neg_self[b] = jnp.where((j <= i) & (col == row), 0.0, NEG)
        enc = erow[b].astype(F32)
        for k in range(enc.shape[1] // length):
            part = slice(k * length, (k + 1) * length)
            neg_cross[b, :, part] = jnp.where(col == enc[:, part], 0.0, NEG)


def bucket_rows(buckets, count):
    length = buckets.shape[1]
    i = lax.broadcasted_iota(jnp.int32, (count, length), 0)
    hot = (i == buckets[...]).astype(F32).astype(BF)
    m = lax.broadcasted_iota(jnp.int32, (length, length), 0)
    l = lax.broadcasted_iota(jnp.int32, (length, length), 1)
    back = ((m + l == length) | ((m == 0) & (l == 0))).astype(F32).astype(BF)
    return dot(hot, back)


def project(a, w, dst, base=None, kind=BF):
    def tile(c):
        v = dot(a[...], w[:, tile_at(c)])
        if base is not None:
            v = v + base[:, tile_at(c)].astype(F32)
        dst[:, tile_at(c)] = v.astype(kind)
    each(dst.shape[1] // TILE, tile)


def project_t(terms, dst, kind=F32, begin=0, end=None):
    def tile(c):
        v = None
        for a, w in terms:
            u = dot_t(a[...], w[tile_at(c), :])
            v = u if v is None else v + u
        dst[:, tile_at(c)] = v.astype(kind)
    lax.fori_loop(begin, dst.shape[1] // TILE if end is None else end, lambda i, carry: (tile(i), carry)[1], 0)


def feed_tile(c, h, cot, wg, wu, wd, hid, dgate, dup):
    cols = tile_at(c)
    hv = h[...]
    gate = dot(hv, wg[:, cols])
    up = dot(hv, wu[:, cols])
    dhid = dot_t(cot[...], wd[cols, :])
    sq = gate * gate
    th = jnp.tanh(C1 * gate * (1.0 + C2 * sq))
    hp = 0.5 * (1.0 + th)
    act = gate * hp
    hid[:, cols] = (act * up).astype(BF)
    slope = hp + (0.5 * C1) * gate * (1.0 - th * th) * (1.0 + (3.0 * C2) * sq)
    dgate[:, cols] = (dhid * up * slope).astype(BF)
    dup[:, cols] = (dhid * act).astype(BF)


def geometry(n):
    chips = n // 2
    side = chips // 2
    s = lax.axis_index("shard")
    rep = lax.axis_index("rep")
    core = lax.rem(s, 2)
    chip = lax.div(s, 2)
    x = lax.rem(chip, 2)
    z = lax.div(chip, 2)
    ring = z + x * (chips - 1 - 2 * z)

    def device_at(position):
        p = lax.rem(position + 2 * chips, chips)
        px = lax.div(p, side)
        pz = p + px * (chips - 1 - 2 * p)
        return (pz * 2 + px) * 2 + core

    return chips, s, rep, core, ring, device_at


def rdma(src, dst, ss, rs, dev):
    return pltpu.make_async_remote_copy(src_ref=src, dst_ref=dst, send_sem=ss, recv_sem=rs, device_id=dev, device_id_type=MESH)


class Gather:
    def __init__(self, geo, pieces, across, sems):
        self.chips, self.me, self.rep, self.core, self.ring, self.device_at = geo
        self.hops = self.chips - 1
        self.pieces, self.across = pieces, across
        self.ring_s, self.ring_r, self.sib_s, self.sib_r, self.y_s, self.y_r, self.yy_s, self.yy_r, self.own_s, self.own_r = sems
        self.other = 1 - 2 * self.core
        self.sibling = (self.me + self.other, self.rep)
        self.opposite = (self.me, 1 - self.rep)
        self.ahead = ((self.device_at(self.ring + 1), self.rep), (self.device_at(self.ring - 1), self.rep))

    def source(self, way, t):
        return self.device_at(self.ring - 1 - t) if way == 0 else self.device_at(self.ring + 1 + t)

    def each(self, rep, count=None):
        most = max(len(self.pieces(0, rep)), len(self.pieces(1, rep)))
        for p in range(most if count is None else count):
            for way in range(2):
                ps = self.pieces(way, rep)
                if p < len(ps):
                    yield way, p, ps[p]

    def ring_copy(self, way, t, p, ref):
        return rdma(ref, ref, self.ring_s.at[way, t, p], self.ring_r.at[way, t, p], self.ahead[way])

    def sib_copy(self, way, t, p, ref):
        return rdma(ref, ref, self.sib_s.at[way, t, p], self.sib_r.at[way, t, p], self.sibling)

    def y_copy(self, way, t, p, ref):
        return rdma(ref, ref, self.y_s.at[way, t, p], self.y_r.at[way, t, p], self.opposite)

    def yy_copy(self, way, t, p, ref):
        return rdma(ref, ref, self.yy_s.at[way, t, p], self.yy_r.at[way, t, p], self.sibling)

    def own_copies(self, src):
        found = []
        for rep in (self.rep, 1 - self.rep):
            for way, p, ref in self.each(rep, None if rep is self.rep else self.across):
                i = 0 if rep is self.rep else 1
                r = ref(src)
                found.append(rdma(r, r, self.own_s.at[i, way, p], self.own_r.at[i, way, p], self.sibling))
        return found

    def start(self):
        for way, p, ref in self.each(self.rep):
            self.ring_copy(way, 0, p, ref(self.me)).start()
        for c in self.own_copies(self.me):
            c.start()

    def hop(self, t, last=False):
        for way, p, ref in self.each(self.rep):
            r = ref(self.source(way, t))
            self.ring_copy(way, t, p, r).wait_recv()
            if not last:
                self.ring_copy(way, t + 1, p, r).start()
            if p < self.across:
                self.y_copy(way, t, p, r).start()
            self.sib_copy(way, t, p, r).start()

    def relay(self, t):
        for way, p, ref in self.each(1 - self.rep, self.across):
            r = ref(self.source(way, t))
            self.y_copy(way, t, p, r).wait_recv()
            self.yy_copy(way, t, p, r).start()

    def complete(self):
        def step(t):
            for way, p, ref in self.each(self.rep):
                self.sib_copy(way, t, p, ref(self.source(way, t) + self.other)).wait_recv()
            for way, p, ref in self.each(1 - self.rep, self.across):
                self.yy_copy(way, t, p, ref(self.source(way, t) + self.other)).wait_recv()
        each(self.hops, step)
        for c in self.own_copies(self.me + self.other):
            c.wait_recv()

    def drain(self):
        def step(t):
            for way, p, ref in self.each(self.rep):
                r = ref(self.source(way, t))
                self.ring_copy(way, t, p, r).wait_send()
                self.sib_copy(way, t, p, r).wait_send()
                if p < self.across:
                    self.y_copy(way, t, p, r).wait_send()
            for way, p, ref in self.each(1 - self.rep, self.across):
                self.yy_copy(way, t, p, ref(self.source(way, t))).wait_send()
        each(self.hops, step)
        for c in self.own_copies(self.me):
            c.wait_send()


def gather_sems(hops, pieces, across):
    dma = pltpu.SemaphoreType.DMA
    return [dma((2, hops, pieces))] * 4 + [dma((2, hops, across))] * 4 + [dma((2, 2, pieces))] * 2


def forward_kernel(n, dims, *refs):
    length, keys = dims
    ins, refs = refs[:11], refs[11:]
    own_gains, refs = refs[:3], refs[3:]
    x, enc, cot, drow, erow, buckets, table = refs[:7]
    w_out, kept, refs = refs[7], refs[8:23], refs[23:]
    out, xt, enct, hfft, hidt, dgu, r1, x1, qkv, cq, ckv, p1, p2, gain3, gains = held = refs[:15]
    w, gu, dn, gn, taps, bias, neg_s, neg_c, h, hid, x2, dh, o = refs[15:28]
    first_sems, second_sems = refs[28:38], refs[38:48]
    load_s, store_s = refs[48:50]

    def stored(i):
        return pltpu.make_async_copy(held[i], kept[i], store_s.at[i])

    def store(*which):
        for i in which:
            stored(i).start()
    geo = geometry(n)
    chips, me, rep, core, ring, device_at = geo
    hops = chips - 1
    rows, rows_d = ins[0].shape[0], ins[10].shape[0]
    half, half_g = w.shape[2] // 2, gu.shape[2] // 2
    count = drow.shape[0]
    pairs = w.shape[2] // 128

    def block(src):
        return pl.ds(pl.multiple_of(src * rows, rows), rows)

    def block_d(src):
        return pl.ds(pl.multiple_of(src * rows_d, rows_d), rows_d)

    def attention_pieces(way, r):
        c = pl.ds(way * half, half)
        found = [lambda s: w.at[r, block(s), c], lambda s: w.at[4 + r, block(s), c],
                 lambda s: w.at[pl.ds(2, 2), block(s), c], lambda s: w.at[pl.ds(6, 2), block(s), c]]
        return found + [lambda s: gn.at[s]] if way == 0 else found

    def feed_pieces(way, r):
        return [lambda s: gu.at[r, block(s), pl.ds(way * half_g, half_g)], lambda s: dn.at[block_d(s), pl.ds(way * half, half)]]

    first = Gather(geo, attention_pieces, 2, first_sems)
    second = Gather(geo, feed_pieces, 1, second_sems)

    width = w.shape[2]
    places = [w.at[i, block(me), :] for i in range(8)] + [gu.at[i, block(me), :] for i in range(2)] + [dn.at[block_d(me), :]]
    loads = [pltpu.make_async_copy(a, b, load_s.at[i]) for i, (a, b) in enumerate(zip(ins, places))]
    for c in loads:
        c.start()
    barrier = pltpu.get_barrier_semaphore()
    for dev in first.ahead + (first.sibling, first.opposite):
        pl.semaphore_signal(barrier, inc=1, device_id=dev, device_id_type=MESH)
    per = 128 // rows
    lane = lax.broadcasted_iota(jnp.int32, (rows, 128), 1)
    spot = lax.broadcasted_iota(jnp.int32, (rows, 128), 0)
    place = (lane == spot + lax.rem(me, per) * rows).astype(F32).astype(BF)
    gn[me] = jnp.concatenate([dot(g[...], place) for g in own_gains] + [jnp.zeros((5, 128), F32)], axis=0)
    for c in loads:
        c.wait()
    pl.semaphore_wait(barrier, 4)

    first.start()
    turn(enc, enct)
    store(2)
    first.hop(0)
    taps[...] = dot(table[...], bucket_rows(buckets, table.shape[1]).astype(BF))
    position_bias(taps, bias, length)
    seg_masks(drow, erow, neg_s, neg_c, length)

    def middle(t):
        first.hop(t)
        first.relay(t - 1)
    lax.fori_loop(1, hops - 1, lambda t, c: (middle(t), c)[1], 0)
    second.start()
    first.hop(hops - 1, True)
    first.relay(hops - 2)
    first.relay(hops - 1)
    first.complete()
    weights_out = pltpu.make_async_copy(w, w_out, store_s.at[15])
    weights_out.start()
    for j in range(w.shape[2] // 128):
        v = gn[j * per]
        for i in range(1, per):
            v = v + gn[j * per + i]
        for i in range(3):
            gains[i, :, j * 128:(j + 1) * 128] = v[i:i + 1, :]
    store(14)

    def some(begin, end, f):
        lax.fori_loop(begin, end, lambda i, c: (f(i), c)[1], 0)

    def heads():
        normed(x, gains.at[0], h)
        for i in range(3):
            project(h, w.at[i], qkv.at[i])

    def own(i):
        attend(i, qkv.at[0], qkv.at[1], qkv.at[2], p1, o, neg_s, bias, length, length)

    def cross_heads():
        store(8, 11)
        turn(h, xt.at[0])
        turn(o, xt.at[1])
        project(o, w.at[3], x1, base=x, kind=F32)
        normed(x1, gains.at[1], h)
        project(h, w.at[4], cq)

    def cross_keys():
        store(7, 9)
        turn(h, xt.at[2])
        for i in range(2):
            project(enc, w.at[6 + i], ckv.at[i])

    def cross(i):
        attend(i, cq, ckv.at[0], ckv.at[1], p2, o, neg_c, None, length, keys)

    def before_feed():
        store(10, 12)
        turn(o, xt.at[3])
        store(1)
        project(o, w.at[5], x2, base=x1, kind=F32)
        normed(x2, gains.at[2], h)
        turn(h, hfft)
        store(3)

    total = count * pairs
    mid = total // 2
    chunks = [heads, lambda: some(0, mid, own), lambda: some(mid, total, own), cross_heads, cross_keys,
              lambda: some(0, mid, cross), lambda: some(mid, total, cross)]
    for t in range(len(chunks)):
        chunks[t]()
        second.hop(t, t == hops - 1)
        if t > 0:
            second.relay(t - 1)
    if hops > len(chunks):
        def rest(t):
            second.hop(t)
            second.relay(t - 1)
        some(len(chunks), hops - 1, rest)
        second.hop(hops - 1, True)
        second.relay(hops - 2)
    before_feed()
    second.relay(hops - 1)
    second.complete()

    each(hid.shape[1] // TILE, lambda c: feed_tile(c, h, cot, gu.at[0], gu.at[1], dn, hid, dgu.at[0], dgu.at[1]))
    store(5)
    turn(hid, hidt)
    store(4)
    project_t([(dgu.at[0], gu.at[0]), (dgu.at[1], gu.at[1])], dh)
    norm_back(x2, gains.at[2], dh, cot, r1, gain3)
    store(6, 13)
    project(hid, dn, out, base=x2)
    store(0)
    first.drain()
    second.drain()
    weights_out.wait()
    for i in range(15):
        stored(i).wait()


def forward(n, weights, own_gains, x, enc, cot, drow, erow, buckets, table):
    hops = n // 2 - 1
    rows, width = weights[0].shape
    ff = weights[8].shape[1]
    tokens, etokens = x.shape[0], enc.shape[0]
    count, _, length = drow.shape
    keys = etokens // count
    pairs = width // 128
    S = jax.ShapeDtypeStruct

    def v(*shape, t=BF):
        return pltpu.VMEM(shape, t)

    kept = [
        S((tokens, width), BF), S((4, width, tokens), BF), S((width, etokens), BF),
        S((width, tokens), BF), S((ff, tokens), BF), S((2, tokens, ff), BF), S((tokens, width), F32), S((tokens, width), F32),
        S((3, tokens, width), BF), S((tokens, width), BF), S((2, etokens, width), BF),
        S((count * pairs, 2 * length, length), BF), S((count * pairs, 2 * length, keys), BF),
        S((1, width), F32), S((3, 1, width), F32),
    ]
    vm, hbm = pl.BlockSpec(memory_space=pltpu.VMEM), pl.BlockSpec(memory_space=pl.ANY)
    return pl.pallas_call(
        functools.partial(forward_kernel, n, (length, keys)),
        name="gather_forward",
        out_shape=(S((8, width, width), BF),) + tuple(kept),
        in_specs=[hbm] * 11 + [vm] * 10,
        out_specs=[hbm] * 16,
        scratch_shapes=[v(*a.shape, t=a.dtype) for a in kept] + [
            v(8, width, width), v(2, width, ff), v(ff, width), v(n, 8, 128, t=F32), v(table.shape[0], length, t=F32),
            v(pairs, 2 * length, length, t=F32), v(count, length, length, t=F32), v(count, length, keys, t=F32),
            v(tokens, width), v(tokens, ff), v(tokens, width, t=F32), v(tokens, width, t=F32), v(tokens, width),
        ] + gather_sems(hops, 5, 2) + gather_sems(hops, 2, 1) + [pltpu.SemaphoreType.DMA((11,)), pltpu.SemaphoreType.DMA((16,))],
        compiler_params=pltpu.CompilerParams(collective_id=0, has_side_effects=True, vmem_limit_bytes=67043328),
    )(*weights, *own_gains, x, enc, cot, drow, erow, buckets, table)


class Group:
    def __init__(self, left, right, size, refs):
        self.left, self.right = left, right
        self.count, self.rows, self.half, self.share = size
        self.ss, self.sr, self.ys, self.yr, self.rs, self.rr, self.own, self.got = refs

    def part(self, i, dev, start, width):
        return dot(self.left(i, dev), self.right(i, pl.ds(pl.multiple_of(start, 128), width)))


def group_shapes(size, slots):
    count, rows, half, share = size
    sib_slots, y_slots, ring_slots = slots

    def v(*shape):
        return pltpu.VMEM(shape, BF)
    return [v(2, 2, count, rows, half), v(sib_slots, 2, count, rows, half), v(2, 2, count, rows, share), v(y_slots, 2, count, rows, share),
            v(2, 2, count, rows, half - share), v(ring_slots, 2, count, rows, half - share)]


def reduce_sems(groups, slots):
    dma = pltpu.SemaphoreType.DMA
    sib_slots, y_slots, ring_slots = slots
    return [dma((2, 2, groups)), dma((sib_slots, 2, groups)), dma((2, 2, groups)), dma((y_slots, 2, groups)),
            dma((2, 2, groups)), dma((ring_slots, 2, groups)), dma((2, 2 * groups)), dma((2, 2 * groups)),
            pltpu.SemaphoreType.REGULAR((3, 2))]


class Reduce:
    def __init__(self, geo, groups, slots, sems):
        self.chips, self.me, self.rep, self.core, self.ring, self.device_at = geo
        self.groups = groups
        self.slots = slots
        self.sib_s, self.sib_r, self.y_s, self.y_r, self.ring_s, self.ring_r, self.fin_s, self.fin_r, self.free = sems
        self.other = 1 - self.rep
        self.sibling = (self.me + 1 - 2 * self.core, self.rep)
        self.opposite = (self.me, self.other)
        self.after = ((self.device_at(self.ring + 1), self.rep), (self.device_at(self.ring - 1), self.rep))

    def block(self, t, way, core):
        return self.device_at(self.ring + (2 * way - 1) * (1 + t)) + core - self.core

    def toward(self, way):
        return (self.after[0][0] + way * (self.after[1][0] - self.after[0][0]), self.rep)

    def behind(self, way):
        return (self.after[1][0] + way * (self.after[0][0] - self.after[1][0]), self.rep)

    def sib_copies(self, t, way):
        s, r = lax.rem(t, 2), lax.rem(t, self.slots[0])
        return [rdma(g.ss.at[s, way], g.sr.at[r, way], self.sib_s.at[s, way, i], self.sib_r.at[r, way, i], self.sibling)
                for i, g in enumerate(self.groups)]

    def y_copies(self, t, way):
        s, r = lax.rem(t, 2), lax.rem(t, self.slots[1])
        return [rdma(g.ys.at[s, way], g.yr.at[r, way], self.y_s.at[s, way, i], self.y_r.at[r, way, i], self.opposite)
                for i, g in enumerate(self.groups)]

    def ring_copies(self, t, way):
        s, r = lax.rem(t, 2), lax.rem(t + 1, self.slots[2])
        return [rdma(g.rs.at[s, way], g.rr.at[r, way], self.ring_s.at[s, way, i], self.ring_r.at[r, way, i], self.toward(way))
                for i, g in enumerate(self.groups)]

    def claim(self, kind, step, way):
        if self.slots[kind] < self.chips:
            @pl.when(step >= self.slots[kind])
            def _():
                pl.semaphore_wait(self.free.at[kind, way], 1)

    def release(self, kind, step, way, dev):
        if self.slots[kind] < self.chips:
            @pl.when(step + self.slots[kind] < self.chips)
            def _():
                pl.semaphore_signal(self.free.at[kind, way], inc=1, device_id=dev, device_id_type=MESH)

    def settle(self, t, copies):
        @pl.when(t >= 2)
        def _():
            for c in copies:
                c.wait_send()

    def to_sibling(self, t):
        s = lax.rem(t, 2)

        def go(way):
            dev = self.block(t, way, 1 - self.core)
            self.settle(t, self.sib_copies(t, way))
            for g in self.groups:
                for i in range(g.count):
                    g.ss[s, way, i] = g.part(i, dev, way * g.half, g.half).astype(BF)
            self.claim(0, t, way)
            for c in self.sib_copies(t, way):
                c.start()
        each(2, go)

    def to_across(self, t):
        s, r = lax.rem(t, 2), lax.rem(t, self.slots[0])

        def go(way):
            dev = self.block(t, way, self.core)
            self.settle(t, self.y_copies(t, way))
            for c in self.sib_copies(t, way):
                c.wait_recv()
            for g in self.groups:
                at = pl.multiple_of(self.other * g.share, 128)
                for i in range(g.count):
                    v = g.part(i, dev, way * g.half + at, g.share)
                    g.ys[s, way, i] = (v + g.sr[r, way, i, :, pl.ds(at, g.share)].astype(F32)).astype(BF)
            self.claim(1, t, way)
            for c in self.y_copies(t, way):
                c.start()
        each(2, go)

    def to_ring(self, t):
        s, b, y, r = lax.rem(t, 2), lax.rem(t, self.slots[0]), lax.rem(t, self.slots[1]), lax.rem(t, self.slots[2])

        for k, g in enumerate(self.groups):
            def go(way, k=k, g=g):
                dev = self.block(t, way, self.core)
                self.settle(t, self.ring_copies(t, way)[k:k + 1])
                self.y_copies(t, way)[k].wait_recv()

                @pl.when(t >= 1)
                def _():
                    self.ring_copies(t - 1, way)[k].wait_recv()
                at = pl.multiple_of(self.rep * g.share, 128)
                for i in range(g.count):
                    v = g.part(i, dev, way * g.half + at, g.share) + g.sr[b, way, i, :, pl.ds(at, g.share)].astype(F32)
                    v = v + g.yr[y, way, i].astype(F32) + g.rr[r, way, i, :, :g.share].astype(F32)
                    g.rs[s, way, i, :, :g.share] = v.astype(BF)
                    v = g.part(i, dev, way * g.half + 2 * g.share, g.half - 2 * g.share)
                    v = v + g.sr[b, way, i, :, 2 * g.share:].astype(F32) + g.rr[r, way, i, :, g.share:].astype(F32)
                    g.rs[s, way, i, :, g.share:] = v.astype(BF)

                @pl.when(t < self.chips - 1)
                def _():
                    if k == 0:
                        self.claim(2, t + 1, way)
                    self.ring_copies(t, way)[k].start()

                @pl.when(t == self.chips - 1)
                def _():
                    for c in self.final_copies(way, k):
                        c.start()
                    last = (self.chips - 1) % 2
                    cols = pl.ds(pl.multiple_of(way * g.half + self.rep * g.share, 128), g.share)
                    g.own[:, :, cols] = g.rs[last, way, :, :, :g.share]
                    rest = pl.ds(pl.multiple_of(way * g.half + 2 * g.share, 128), g.half - 2 * g.share)
                    g.own[:, :, rest] = g.rs[last, way, :, :, g.share:]
                if k == len(self.groups) - 1:
                    self.release(0, t, way, self.sibling)
                    self.release(1, t, way, self.opposite)
                    self.release(2, t, way, self.behind(way))
            each(2, go)

    def prepare(self):
        for g in self.groups:
            g.rr[0] = jnp.zeros(g.rr.shape[1:], BF)

    def final_copies(self, way, k):
        g = self.groups[k]
        mine = g.rs.at[(self.chips - 1) % 2, way]
        cols = pl.ds(pl.multiple_of(way * g.half + self.rep * g.share, 128), g.share)
        wide = g.half - 2 * g.share
        there = pl.ds(pl.multiple_of(way * wide, 128), wide)
        return [rdma(mine.at[:, :, pl.ds(0, g.share)], g.own.at[:, :, cols],
                     self.fin_s.at[way, 2 * k], self.fin_r.at[way, 2 * k], self.opposite),
                rdma(mine.at[:, :, pl.ds(g.share, wide)], g.got.at[:, :, there],
                     self.fin_s.at[way, 2 * k + 1], self.fin_r.at[way, 2 * k + 1], self.opposite)]

    def finish(self):
        def go(way):
            for k, g in enumerate(self.groups):
                wide = g.half - 2 * g.share
                ref = g.own.at[:, :, pl.ds(pl.multiple_of(way * g.half + self.other * g.share, 128), g.share)]
                rdma(ref, ref, self.fin_s.at[way, 2 * k], self.fin_r.at[way, 2 * k], self.opposite).wait_recv()
                ref = g.got.at[:, :, pl.ds(pl.multiple_of(way * wide, 128), wide)]
                rdma(ref, ref, self.fin_s.at[way, 2 * k + 1], self.fin_r.at[way, 2 * k + 1], self.opposite).wait_recv()
                for c in self.final_copies(way, k):
                    c.wait_send()
            for t in (self.chips - 2, self.chips - 1):
                for c in self.sib_copies(t, way) + self.y_copies(t, way):
                    c.wait_send()
            for c in self.ring_copies(self.chips - 2, way):
                c.wait_send()
        each(2, go)

    def at(self, t, f):
        @pl.when((t >= 0) & (t < self.chips))
        def _():
            f(t)


class Butterfly:
    def __init__(self, geo, n, buf, got, sems):
        _, self.me, self.rep, _, _, _ = geo
        self.stages = n.bit_length() - 1
        self.buf, self.got = buf, got
        self.send, self.recv = sems

    def partner(self, bit):
        return (self.me + bit - 2 * bit * lax.rem(lax.div(self.me, bit), 2), self.rep)

    def copy(self, j, dev):
        return rdma(self.buf.at[j], self.got.at[j], self.send.at[j], self.recv.at[j], dev)

    def begin(self):
        self.copy(0, (self.me, 1 - self.rep)).start()

    def stage(self, j, bit):
        self.copy(j - 1, self.partner(bit)).wait_recv()
        self.buf[j] = self.buf[j - 1] + self.got[j - 1]
        self.copy(j, self.partner(bit)).start()

    def end(self, dst):
        self.copy(self.stages, self.partner(1)).wait_recv()
        dst[...] = self.buf[self.stages] + self.got[self.stages]
        for j in range(self.stages + 1):
            self.copy(j, self.partner(1)).wait_send()


OFFSETS = (0, 0, 0, 5, 8)
CHAINS = ((2,), (3,), (4,), (0, 5), (1,))
SLOTS = (3, 3, 3)


def backward_kernel(n, sizes, dims, *refs):
    length, keys = dims
    ins, w_hbm, refs = refs[:16], refs[16], refs[17:]
    outs, (small_o, dtok, denc), refs = refs[:12], refs[12:15], refs[15:]
    held, refs = refs[:16], refs[16:]
    hfft, hidt, dgu, cot, r1, cq, ckv, p2, x1, gains, qkv, p1, x, xt, enct, gain3 = held
    bufs, refs = refs[:36], refs[36:]
    sems, refs = [refs[9 * k:9 * k + 9] for k in range(5)], refs[45:]
    sm, sm_got, sm_s, sm_r, load_s, w, w_s, dy, dye, dh, r0, do, gain12, diag = refs
    geo = geometry(n)
    chips, me, rep, core, ring, device_at = geo
    rows, rows_d = sizes[0][1], sizes[4][1]

    loads = [pltpu.make_async_copy(a, b, load_s.at[i]) for i, (a, b) in enumerate(zip(ins, held))]
    for c in loads:
        c.start()

    def fetch(i, slot):
        return pltpu.make_async_copy(w_hbm.at[i], w.at[slot], w_s.at[slot])
    for i, slot in ((5, 0), (6, 1), (7, 2), (4, 3)):
        fetch(i, slot).start()

    def block(dev, size):
        return pl.ds(pl.multiple_of(dev * size, size), size)
    lefts = [lambda i, dev: xt[(3, 2)[i], block(dev, rows), :], lambda i, dev: xt[(1, 0, 0, 0)[i], block(dev, rows), :],
             lambda i, dev: hfft[block(dev, rows), :], lambda i, dev: hfft[block(dev, rows), :],
             lambda i, dev: hidt[block(dev, rows_d), :], lambda i, dev: enct[block(dev, rows), :]]
    rights = [lambda i, c: dy[i, :, c], lambda i, c: dy[2 + i, :, c], lambda i, c: dgu[0, :, c], lambda i, c: dgu[1, :, c],
              lambda i, c: cot[:, c], lambda i, c: dye[i, :, c]]
    groups = [Group(lefts[k], rights[k], sizes[k], bufs[6 * k:6 * k + 6] + outs[2 * k:2 * k + 2]) for k in range(6)]
    chains = [Reduce(geo, [groups[k] for k in c], SLOTS, s) for c, s in zip(CHAINS, sems)]
    tree = Butterfly(geo, n, sm, sm_got, (sm_s, sm_r))
    lead = chains[0]

    barrier = pltpu.get_barrier_semaphore()
    greet = [lead.after[0], lead.after[1], lead.sibling, lead.opposite] + [tree.partner(1 << j) for j in range(tree.stages)]
    for dev in greet:
        pl.semaphore_signal(barrier, inc=1, device_id=dev, device_id_type=MESH)
    for g in groups:
        g.rr[0] = jnp.zeros(g.rr.shape[1:], BF)
    diag[...] = jnp.zeros(diag.shape, F32)
    for c in loads[:4]:
        c.wait()
    pl.semaphore_wait(barrier, len(greet))

    total = p1.shape[0]
    width = dh.shape[1]

    def start_back():
        for c in loads[4:]:
            c.wait()
        dy[0] = r1[...].astype(BF)
        fetch(5, 0).wait()
        project_t([(dy.at[0], w.at[0])], do, kind=BF)
        fetch(3, 0).start()

    def cross(begin, end):
        def f():
            lax.fori_loop(begin, end, lambda i, c: (attend_back(
                i, cq, ckv.at[0], ckv.at[1], p2, do, dy.at[1], dye.at[0], dye.at[1], None, length, keys), c)[1], 0)
        return f

    def own(begin, end):
        def f():
            lax.fori_loop(begin, end, lambda i, c: (attend_back(
                i, qkv.at[0], qkv.at[1], qkv.at[2], p1, do, dy.at[3], dy.at[4], dy.at[5], diag, length, length), c)[1], 0)
        return f

    def encoder(begin, end, last):
        def f():
            if not last:
                fetch(6, 1).wait()
                fetch(7, 2).wait()
            project_t([(dye.at[0], w.at[1]), (dye.at[1], w.at[2])], denc, begin=begin, end=end)
            if last:
                fetch(0, 1).start()
                fetch(1, 2).start()
        return f

    def cross_norm():
        norm_back(x1, gains.at[1], dh, r1, r0, gain12.at[1])
        dy[2] = r0[...].astype(BF)

    def cross_query():
        fetch(4, 3).wait()
        project_t([(dy.at[1], w.at[3])], dh)
        fetch(2, 3).start()

    def own_out():
        fetch(3, 0).wait()
        project_t([(dy.at[2], w.at[0])], do, kind=BF)

    def own_in(begin, end, last):
        def f():
            if not last:
                for i, slot in ((0, 1), (1, 2), (2, 3)):
                    fetch(i, slot).wait()
            project_t([(dy.at[3], w.at[1]), (dy.at[4], w.at[2]), (dy.at[5], w.at[3])], dh, begin=begin, end=end)
        return f

    def own_norm():
        norm_back(x, gains.at[0], dh, r0, dtok, gain12.at[0])
        for k in range(width // 128):
            for i, g in enumerate((gain12.at[0], gain12.at[1], gain3)):
                sm[0, pl.ds(i * (width // 128) + k, 1), :] = g[:, k * 128:(k + 1) * 128]
        for i in range(diag.shape[0]):
            sm[0, pl.ds(3 * (width // 128) + i, 1), :] = diag[i]

    tiles = width // TILE
    pieces = [start_back]
    pieces += [cross(total * k // 8, total * (k + 1) // 8) for k in range(8)]
    pieces += [cross_query, cross_norm, own_out]
    pieces += [own(total * k // 5, total * (k + 1) // 5) for k in range(5)]
    pieces += [encoder(0, tiles // 2, False), encoder(tiles // 2, tiles, True)]
    pieces += [own_in(0, tiles // 2, False), own_in(tiles // 2, tiles, True), own_norm]
    tree_at = 7

    def piece(u, which):
        for i in range(which, len(pieces), 3):
            pl.when(u == i // 3)(pieces[i])

    def step(v, bit):
        u = v - 3
        for k, c in enumerate(chains):
            c.at(u - OFFSETS[k], c.to_ring)
            if k < 3:
                piece(u, k)
        for k, c in enumerate(chains):
            c.at(u - OFFSETS[k] + 2, c.to_across)
        for k, c in enumerate(chains):
            c.at(u - OFFSETS[k] + 3, c.to_sibling)
        pl.when(u == tree_at)(tree.begin)
        inside = (u > tree_at) & (u <= tree_at + tree.stages)

        @pl.when(inside)
        def _():
            tree.stage(u - tree_at, bit)
        return jnp.where(inside, bit * 2, bit)

    lax.fori_loop(0, OFFSETS[-1] + chips + 3, step, jnp.int32(1))
    tree.end(small_o)
    for c in chains:
        c.finish()


def shares(half):
    return max(1, half // 512) * 128


def backward(n, w, hfft, hidt, dgu, cot, r1, cq, ckv, p2, x1, gains, qkv, p1, x, xt, enct, gain3):
    chips = n // 2
    tokens, width = x.shape
    etokens, ff = enct.shape[1], dgu.shape[2]
    length, keys = p1.shape[2], p2.shape[2]
    rows, rows_d = width // n, hidt.shape[0] // n
    half, half_g = width // 2, ff // 2
    sizes = [(2, rows, half, shares(half)), (4, rows, half, shares(half)), (1, rows, half_g, shares(half_g)),
             (1, rows, half_g, shares(half_g)), (1, rows_d, half, shares(half)), (2, rows, half, shares(half))]
    stages = n.bit_length() - 1
    dma = pltpu.SemaphoreType.DMA
    S = jax.ShapeDtypeStruct
    vm, hbm = pl.BlockSpec(memory_space=pltpu.VMEM), pl.BlockSpec(memory_space=pl.ANY)
    outs = []
    for count, r, h, share in sizes:
        outs += [S((count, r, 2 * h), BF), S((count, r, 2 * (h - 2 * share)), BF)]
    small = (3 * (width // 128) + width // 64, 128)
    ins = (hfft, hidt, dgu, cot, r1, cq, ckv, p2, x1, gains, qkv, p1, x, xt, enct, gain3)
    slots = tuple(min(s, chips) for s in SLOTS)
    return pl.pallas_call(
        functools.partial(backward_kernel, n, sizes, (length, keys)),
        name="backward_reduce",
        out_shape=tuple(outs) + (S(small, F32), S((tokens, width), F32), S((etokens, width), F32)),
        in_specs=[hbm] * 17,
        out_specs=[vm] * 15,
        scratch_shapes=[pltpu.VMEM(a.shape, a.dtype) for a in ins]
        + [b for size in sizes for b in group_shapes(size, slots)]
        + [s for c in CHAINS for s in reduce_sems(len(c), slots)]
        + [pltpu.VMEM((stages + 1,) + small, F32)] * 2 + [dma((stages + 1,))] * 2
        + [dma((16,)), pltpu.VMEM((4, width, width), BF), dma((4,)), pltpu.VMEM((6, tokens, width), BF),
           pltpu.VMEM((2, etokens, width), BF), pltpu.VMEM((tokens, width), F32), pltpu.VMEM((tokens, width), F32),
           pltpu.VMEM((tokens, width), BF), pltpu.VMEM((2, 1, width), F32), pltpu.VMEM((width // 64, 1, 128), F32)],
        compiler_params=pltpu.CompilerParams(collective_id=1, has_side_effects=True, vmem_limit_bytes=67043328),
    )(*ins, w)


def finish_kernel(sizes, passed, buckets_count, *refs):
    parts, mats = 2 * len(sizes), sum(s[0] for s in sizes)
    ins, (small, buckets), refs = refs[:parts + passed], refs[parts + passed:parts + passed + 2], refs[parts + passed + 2:]
    outs, (dtable, gain1, gain2, gain3), refs = refs[:mats + passed], refs[mats + passed:mats + passed + 4], refs[mats + passed + 4:]
    held, done, (load_s, store_s) = refs[:parts + passed], refs[parts + passed:-2], refs[-2:]
    loads = [pltpu.make_async_copy(a, b, load_s.at[i]) for i, (a, b) in enumerate(zip(ins, held))]
    stores = [pltpu.make_async_copy(a, b, store_s.at[i]) for i, (a, b) in enumerate(zip(done + held[parts:], outs))]
    for c in loads:
        c.start()
    at = 0
    for k, (count, rows, half, share) in enumerate(sizes):
        own, got = held[2 * k], held[2 * k + 1]
        loads[2 * k].wait()
        loads[2 * k + 1].wait()
        wide = half - 2 * share
        for i in range(count):
            for way in range(2):
                lo = way * half
                done[at][:, lo:lo + 2 * share] = own[i, :, lo:lo + 2 * share].astype(F32)
                v = own[i, :, lo + 2 * share:lo + half].astype(F32) + got[i, :, way * wide:(way + 1) * wide].astype(F32)
                done[at][:, lo + 2 * share:lo + half] = v
            stores[at].start()
            at += 1
    for i in range(passed):
        loads[parts + i].wait()
        stores[mats + i].start()
    me = lax.axis_index("shard")
    rows = gain1.shape[1]
    per = 128 // rows
    heads = dtable.shape[0]
    tiles = (small.shape[0] - heads) // 3
    tile = lax.broadcasted_iota(jnp.int32, (tiles, 128), 0)
    for i, dst in enumerate((gain1, gain2, gain3)):
        v = jnp.where(tile == lax.div(me, per), small[i * tiles:(i + 1) * tiles, :], 0.0)
        v = pltpu.roll(v, lax.rem(128 - lax.rem(me, per) * rows, 128), 1)
        dst[...] = jnp.sum(v, axis=0, keepdims=True)[:, :rows]
    dtable[...] = lax.dot_general(small[3 * tiles:, :], bucket_rows(buckets, buckets_count), (((1,), (1,)), ((), ())),
                                  precision=lax.Precision.HIGHEST, preferred_element_type=F32)
    for c in stores:
        c.wait()


def finish(parts, passed, small, buckets, shape, rows):
    sizes, outs = [], []
    S = jax.ShapeDtypeStruct
    for own, got in zip(parts[0::2], parts[1::2]):
        count, r, width = own.shape
        half = width // 2
        sizes.append((count, r, half, (half - got.shape[2] // 2) // 2))
        outs += [S((r, width), F32)] * count
    vm, hbm = pl.BlockSpec(memory_space=pltpu.VMEM), pl.BlockSpec(memory_space=pl.ANY)
    ins = list(parts) + list(passed)
    dma = pltpu.SemaphoreType.DMA
    return pl.pallas_call(
        functools.partial(finish_kernel, sizes, len(passed), shape[1]),
        name="finish",
        out_shape=tuple(outs) + tuple(S(a.shape, a.dtype) for a in passed) + (S(shape, F32),) + (S((1, rows), F32),) * 3,
        in_specs=[hbm] * len(ins) + [vm] * 2,
        out_specs=[hbm] * (len(outs) + len(passed)) + [vm] * 4,
        scratch_shapes=[pltpu.VMEM(a.shape, a.dtype) for a in ins] + [pltpu.VMEM(a.shape, a.dtype) for a in outs]
        + [dma((len(ins),)), dma((len(outs) + len(passed),))],
        compiler_params=pltpu.CompilerParams(vmem_limit_bytes=67043328),
    )(*ins, small, buckets)


def body(hidden_in, encoded, dec_segments, enc_segments, buckets, out_cot, norm_self, self_query, self_key, self_value,
         self_out, table, norm_cross, cross_query, cross_key, cross_value, cross_out, norm_ff, ff_gate, ff_up, ff_down, *, n):
    micro, per, length, width = hidden_in.shape
    keys = encoded.shape[2]
    count = micro * per
    rows, rows_d, ff = self_query.shape[0], ff_down.shape[0], ff_gate.shape[1]
    spare = -rows_d % 16
    if spare:
        ff_down = jnp.pad(ff_down, ((0, spare), (0, 0)))
        ff_gate, ff_up = [jnp.pad(w.reshape(rows, n, rows_d), ((0, 0), (0, 0), (0, spare))).reshape(rows, -1) for w in (ff_gate, ff_up)]
    x = hidden_in.reshape(count * length, width)
    enc = encoded.reshape(count * keys, width)
    cot = out_cot.reshape(count * length, width)
    buckets = buckets.reshape(1, length)
    weights = (self_query, self_key, self_value, self_out, cross_query, cross_out, cross_key, cross_value, ff_gate, ff_up, ff_down)
    own_gains = [g.reshape(1, rows) for g in (norm_self, norm_cross, norm_ff)]
    w, out, xt, enct, hfft, hidt, dgu, r1, x1, qkv, cq, ckv, p1, p2, gain3, gains = forward(
        n, weights, own_gains, x, enc, cot, dec_segments.reshape(count, 1, length), enc_segments.reshape(count, 1, keys), buckets, table.T)
    *parts, small, dtok, denc = backward(n, w, hfft, hidt, dgu, cot, r1, cq, ckv, p2, x1, gains, qkv, p1, x, xt, enct, gain3)
    gco, gcq, gso, gq, gk, gv, gg, gup, gd, gck, gcv, out, dtok, denc, dtable, g1, g2, g3 = finish(
        parts, (out, dtok, denc), small, buckets, table.T.shape, rows)
    if spare:
        gd = gd[:rows_d]
        gg, gup = [g.reshape(rows, n, -1)[:, :, :rows_d].reshape(rows, ff) for g in (gg, gup)]
    return (
        out.reshape(hidden_in.shape), dtok.reshape(hidden_in.shape), denc.reshape(encoded.shape),
        g1.reshape(rows), gq, gk, gv, gso, dtable.T, g2.reshape(rows), gcq, gck, gcv, gco, g3.reshape(rows), gg, gup, gd,
    )


def solution(mesh):
    tok = P(None, ("shard", "rep"), None, None)
    seg = P(None, ("shard", "rep"), None)
    vec, mat, rep = P("shard"), P("shard", None), P()
    return jax.shard_map(
        functools.partial(body, n=mesh.shape["shard"]),
        mesh=mesh,
        in_specs=(tok, tok, seg, seg, rep, tok, vec, mat, mat, mat, mat, rep, vec, mat, mat, mat, mat, vec, mat, mat, mat),
        out_specs=(tok, tok, tok, vec, mat, mat, mat, mat, rep, vec, mat, mat, mat, mat, vec, mat, mat, mat),
        check_vma=False,
    )
```

```python
import functools
import math

import jax
import jax.numpy as jnp
from jax import lax
from jax.experimental import pallas as pl
from jax.experimental.pallas import tpu as pltpu
from jax.sharding import PartitionSpec as P

MESH = pl.DeviceIdType.MESH
BF = jnp.bfloat16
F32 = jnp.float32
EPS = 1e-06
NEG = -1e30
C1 = math.sqrt(2.0 / math.pi)
C2 = 0.044715
TILE = 256


def each(count, f):
    def step(i, carry):
        f(i)
        return carry
    lax.fori_loop(0, count, step, 0)


def tile_at(i, size=TILE):
    return pl.ds(pl.multiple_of(i * size, size), size)


def dot(a, b):
    return jnp.dot(a, b, preferred_element_type=F32)


def dot_t(a, b):
    return lax.dot_general(a, b, (((1,), (1,)), ((), ())), preferred_element_type=F32)


def dot_rows(a, b):
    return lax.dot_general(a, b, (((0,), (0,)), ((), ())), preferred_element_type=F32)


def normed(src, gain, dst):
    def rows(i):
        r = tile_at(i, 32)
        v = src[r, :].astype(F32)
        t = lax.rsqrt(jnp.mean(v * v, axis=-1, keepdims=True) + EPS)
        dst[r, :] = (v * t * gain[...]).astype(BF)
    each(src.shape[0] // 32, rows)


def norm_back(src, gain, grad, base, dst, gain_sum):
    gain_sum[...] = jnp.zeros(gain_sum.shape, F32)

    def rows(i):
        r = tile_at(i, 16)
        v = src[r, :].astype(F32)
        dy = grad[r, :]
        g = gain[...]
        t = lax.rsqrt(jnp.mean(v * v, axis=-1, keepdims=True) + EPS)
        vt = v * t
        gdy = g * dy
        inner = jnp.mean(vt * gdy, axis=-1, keepdims=True)
        dst[r, :] = base[r, :].astype(F32) + t * (gdy - vt * inner)
        gain_sum[...] += jnp.sum(vt * dy, axis=0, keepdims=True)
    each(src.shape[0] // 16, rows)


def turn(src, dst):
    for b in range(src.shape[0] // 128):
        def block(c, b=b):
            dst[tile_at(c), b * 128:(b + 1) * 128] = src[b * 128:(b + 1) * 128, tile_at(c)].T
        each(src.shape[1] // TILE, block)


def head_masks():
    lane = lax.broadcasted_iota(jnp.int32, (1, 128), 1)
    even = (lane < 64).astype(F32).astype(BF)
    return even, (lane >= 64).astype(F32).astype(BF)


def pair_rows(x, masks):
    return jnp.concatenate([x * masks[0], x * masks[1]], axis=0)


def side_by_side(x):
    half = x.shape[0] // 2
    return jnp.concatenate([x[:half], x[half:]], axis=1)


def attend(i, q, k, v, p, o, neg, bias, length, keys):
    masks = head_masks()
    pairs = q.shape[1] // 128
    b, pair = lax.div(i, pairs), lax.rem(i, pairs)
    lanes = tile_at(pair, 128)
    rows, krows = tile_at(b, length), tile_at(b, keys)
    s = dot_t(pair_rows(q[rows, lanes], masks), k[krows, lanes])
    if bias is not None:
        s = s + bias[pair]
    n = neg[b]
    s = s + jnp.concatenate([n, n], axis=0)
    e = jnp.exp(s - jnp.max(s, axis=-1, keepdims=True))
    pb = (e * (1.0 / jnp.sum(e, axis=-1, keepdims=True))).astype(BF)
    p[i] = pb
    o[rows, lanes] = dot(side_by_side(pb), pair_rows(v[krows, lanes], masks)).astype(BF)


def attend_back(i, q, k, v, p, do, dq, dk, dv, diag, length, keys):
    masks = head_masks()
    pairs = q.shape[1] // 128
    b, pair = lax.div(i, pairs), lax.rem(i, pairs)
    lanes = tile_at(pair, 128)
    rows, krows = tile_at(b, length), tile_at(b, keys)
    dos = pair_rows(do[rows, lanes], masks)
    dp = dot_t(dos, v[krows, lanes])
    pb = p[i]
    pf = pb.astype(F32)
    ds = (pf * (dp - jnp.sum(pf * dp, axis=-1, keepdims=True))).astype(BF)
    dq[rows, lanes] = dot(side_by_side(ds), pair_rows(k[krows, lanes], masks)).astype(BF)
    dk[krows, lanes] = dot_rows(ds, pair_rows(q[rows, lanes], masks)).astype(BF)
    dv[krows, lanes] = dot_rows(pb, dos).astype(BF)
    if diag is not None:
        i0 = lax.broadcasted_iota(jnp.int32, (length, length), 0)
        i1 = lax.broadcasted_iota(jnp.int32, (length, length), 1)
        flip = (i0 + i1 == length - 1).astype(F32).astype(BF)
        for h in range(2):
            u = pltpu.roll(dot(flip, ds[h * length:(h + 1) * length]), 1, 1, stride=1, stride_axis=0)
            diag[2 * pair + h] += jnp.sum(u, axis=0, keepdims=True)


def position_bias(taps, bias, length):
    def pair(i):
        for h in range(2):
            w = jnp.broadcast_to(taps[pl.ds(2 * i + h, 1), :], (length, length))
            bias[i, h * length:(h + 1) * length, :] = pltpu.roll(w, 0, 1, stride=1, stride_axis=0)
    each(bias.shape[0], pair)


def seg_masks(drow, erow, neg_self, neg_cross, length):
    for b in range(drow.shape[0]):
        row = drow[b].astype(F32)
        col = jnp.broadcast_to(row, (length, length)).T
        i = lax.broadcasted_iota(jnp.int32, (length, length), 0)
        j = lax.broadcasted_iota(jnp.int32, (length, length), 1)
        neg_self[b] = jnp.where((j <= i) & (col == row), 0.0, NEG)
        enc = erow[b].astype(F32)
        for k in range(enc.shape[1] // length):
            part = slice(k * length, (k + 1) * length)
            neg_cross[b, :, part] = jnp.where(col == enc[:, part], 0.0, NEG)


def bucket_rows(buckets, count):
    length = buckets.shape[1]
    i = lax.broadcasted_iota(jnp.int32, (count, length), 0)
    hot = (i == buckets[...]).astype(F32).astype(BF)
    m = lax.broadcasted_iota(jnp.int32, (length, length), 0)
    l = lax.broadcasted_iota(jnp.int32, (length, length), 1)
    back = ((m + l == length) | ((m == 0) & (l == 0))).astype(F32).astype(BF)
    return dot(hot, back)


def project(a, w, dst, base=None, kind=BF):
    def tile(c):
        v = dot(a[...], w[:, tile_at(c)])
        if base is not None:
            v = v + base[:, tile_at(c)].astype(F32)
        dst[:, tile_at(c)] = v.astype(kind)
    each(dst.shape[1] // TILE, tile)


def project_t(terms, dst, kind=F32, begin=0, end=None):
    def tile(c):
        v = None
        for a, w in terms:
            u = dot_t(a[...], w[tile_at(c), :])
            v = u if v is None else v + u
        dst[:, tile_at(c)] = v.astype(kind)
    lax.fori_loop(begin, dst.shape[1] // TILE if end is None else end, lambda i, carry: (tile(i), carry)[1], 0)


def feed_tile(c, h, cot, wg, wu, wd, hid, dgate, dup):
    cols = tile_at(c)
    hv = h[...]
    gate = dot(hv, wg[:, cols])
    up = dot(hv, wu[:, cols])
    dhid = dot_t(cot[...], wd[cols, :])
    sq = gate * gate
    th = jnp.tanh(C1 * gate * (1.0 + C2 * sq))
    hp = 0.5 * (1.0 + th)
    act = gate * hp
    hid[:, cols] = (act * up).astype(BF)
    slope = hp + (0.5 * C1) * gate * (1.0 - th * th) * (1.0 + (3.0 * C2) * sq)
    dgate[:, cols] = (dhid * up * slope).astype(BF)
    dup[:, cols] = (dhid * act).astype(BF)


def geometry(n):
    chips = n // 2
    side = chips // 2
    s = lax.axis_index("shard")
    rep = lax.axis_index("rep")
    core = lax.rem(s, 2)
    chip = lax.div(s, 2)
    x = lax.rem(chip, 2)
    z = lax.div(chip, 2)
    ring = z + x * (chips - 1 - 2 * z)

    def device_at(position):
        p = lax.rem(position + 2 * chips, chips)
        px = lax.div(p, side)
        pz = p + px * (chips - 1 - 2 * p)
        return (pz * 2 + px) * 2 + core

    return chips, s, rep, core, ring, device_at


def rdma(src, dst, ss, rs, dev):
    return pltpu.make_async_remote_copy(src_ref=src, dst_ref=dst, send_sem=ss, recv_sem=rs, device_id=dev, device_id_type=MESH)


class Gather:
    def __init__(self, geo, pieces, across, sems):
        self.chips, self.me, self.rep, self.core, self.ring, self.device_at = geo
        self.hops = self.chips - 1
        self.pieces, self.across = pieces, across
        self.ring_s, self.ring_r, self.sib_s, self.sib_r, self.y_s, self.y_r, self.yy_s, self.yy_r, self.own_s, self.own_r = sems
        self.other = 1 - 2 * self.core
        self.sibling = (self.me + self.other, self.rep)
        self.opposite = (self.me, 1 - self.rep)
        self.ahead = ((self.device_at(self.ring + 1), self.rep), (self.device_at(self.ring - 1), self.rep))

    def source(self, way, t):
        return self.device_at(self.ring - 1 - t) if way == 0 else self.device_at(self.ring + 1 + t)

    def each(self, rep, count=None):
        most = max(len(self.pieces(0, rep)), len(self.pieces(1, rep)))
        for p in range(most if count is None else count):
            for way in range(2):
                ps = self.pieces(way, rep)
                if p < len(ps):
                    yield way, p, ps[p]

    def ring_copy(self, way, t, p, ref):
        return rdma(ref, ref, self.ring_s.at[way, t, p], self.ring_r.at[way, t, p], self.ahead[way])

    def sib_copy(self, way, t, p, ref):
        return rdma(ref, ref, self.sib_s.at[way, t, p], self.sib_r.at[way, t, p], self.sibling)

    def y_copy(self, way, t, p, ref):
        return rdma(ref, ref, self.y_s.at[way, t, p], self.y_r.at[way, t, p], self.opposite)

    def yy_copy(self, way, t, p, ref):
        return rdma(ref, ref, self.yy_s.at[way, t, p], self.yy_r.at[way, t, p], self.sibling)

    def own_copies(self, src):
        found = []
        for rep in (self.rep, 1 - self.rep):
            for way, p, ref in self.each(rep, None if rep is self.rep else self.across):
                i = 0 if rep is self.rep else 1
                r = ref(src)
                found.append(rdma(r, r, self.own_s.at[i, way, p], self.own_r.at[i, way, p], self.sibling))
        return found

    def start(self):
        for way, p, ref in self.each(self.rep):
            self.ring_copy(way, 0, p, ref(self.me)).start()
        for c in self.own_copies(self.me):
            c.start()

    def hop(self, t, last=False):
        for way, p, ref in self.each(self.rep):
            r = ref(self.source(way, t))
            self.ring_copy(way, t, p, r).wait_recv()
            if not last:
                self.ring_copy(way, t + 1, p, r).start()
            if p < self.across:
                self.y_copy(way, t, p, r).start()
            self.sib_copy(way, t, p, r).start()

    def relay(self, t):
        for way, p, ref in self.each(1 - self.rep, self.across):
            r = ref(self.source(way, t))
            self.y_copy(way, t, p, r).wait_recv()
            self.yy_copy(way, t, p, r).start()

    def complete(self):
        def step(t):
            for way, p, ref in self.each(self.rep):
                self.sib_copy(way, t, p, ref(self.source(way, t) + self.other)).wait_recv()
            for way, p, ref in self.each(1 - self.rep, self.across):
                self.yy_copy(way, t, p, ref(self.source(way, t) + self.other)).wait_recv()
        each(self.hops, step)
        for c in self.own_copies(self.me + self.other):
            c.wait_recv()

    def drain(self):
        def step(t):
            for way, p, ref in self.each(self.rep):
                r = ref(self.source(way, t))
                self.ring_copy(way, t, p, r).wait_send()
                self.sib_copy(way, t, p, r).wait_send()
                if p < self.across:
                    self.y_copy(way, t, p, r).wait_send()
            for way, p, ref in self.each(1 - self.rep, self.across):
                self.yy_copy(way, t, p, ref(self.source(way, t))).wait_send()
        each(self.hops, step)
        for c in self.own_copies(self.me):
            c.wait_send()


def gather_sems(hops, pieces, across):
    dma = pltpu.SemaphoreType.DMA
    return [dma((2, hops, pieces))] * 4 + [dma((2, hops, across))] * 4 + [dma((2, 2, pieces))] * 2


def forward_kernel(n, dims, *refs):
    length, keys = dims
    ins, refs = refs[:11], refs[11:]
    own_gains, refs = refs[:3], refs[3:]
    x, enc, cot, drow, erow, buckets, table = refs[:7]
    w_out, kept, refs = refs[7], refs[8:23], refs[23:]
    out, xt, enct, hfft, hidt, dgu, r1, x1, qkv, cq, ckv, p1, p2, gain3, gains = held = refs[:15]
    w, gu, dn, gn, taps, bias, neg_s, neg_c, h, hid, x2, dh, o = refs[15:28]
    first_sems, second_sems = refs[28:38], refs[38:48]
    load_s, store_s = refs[48:50]

    def stored(i):
        return pltpu.make_async_copy(held[i], kept[i], store_s.at[i])

    def store(*which):
        for i in which:
            stored(i).start()
    geo = geometry(n)
    chips, me, rep, core, ring, device_at = geo
    hops = chips - 1
    rows, rows_d = ins[0].shape[0], ins[10].shape[0]
    half, half_g = w.shape[2] // 2, gu.shape[2] // 2
    count = drow.shape[0]
    pairs = w.shape[2] // 128

    def block(src):
        return pl.ds(pl.multiple_of(src * rows, rows), rows)

    def block_d(src):
        return pl.ds(pl.multiple_of(src * rows_d, rows_d), rows_d)

    def attention_pieces(way, r):
        c = pl.ds(way * half, half)
        near, far = pl.ds(way * half, half // 2), pl.ds(way * half + half // 2, half // 2)
        found = [lambda s: w.at[r, block(s), c], lambda s: w.at[4 + r, block(s), c], lambda s: w.at[2 + r, block(s), near],
                 lambda s: w.at[pl.ds(2, 2), block(s), far], lambda s: w.at[pl.ds(6, 2), block(s), c]]
        return found + [lambda s: gn.at[s]] if way == 0 else found

    def feed_pieces(way, r):
        return [lambda s: gu.at[r, block(s), pl.ds(way * half_g, half_g)], lambda s: dn.at[block_d(s), pl.ds(way * half, half)]]

    first = Gather(geo, attention_pieces, 3, first_sems)
    second = Gather(geo, feed_pieces, 1, second_sems)

    width = w.shape[2]
    places = [w.at[i, block(me), :] for i in range(8)] + [gu.at[i, block(me), :] for i in range(2)] + [dn.at[block_d(me), :]]
    loads = [pltpu.make_async_copy(a, b, load_s.at[i]) for i, (a, b) in enumerate(zip(ins, places))]
    for c in loads:
        c.start()
    barrier = pltpu.get_barrier_semaphore()
    for dev in first.ahead + (first.sibling, first.opposite):
        pl.semaphore_signal(barrier, inc=1, device_id=dev, device_id_type=MESH)
    per = 128 // rows
    lane = lax.broadcasted_iota(jnp.int32, (rows, 128), 1)
    spot = lax.broadcasted_iota(jnp.int32, (rows, 128), 0)
    place = (lane == spot + lax.rem(me, per) * rows).astype(F32).astype(BF)
    gn[me] = jnp.concatenate([dot(g[...], place) for g in own_gains] + [jnp.zeros((5, 128), F32)], axis=0)
    for c in loads[:8]:
        c.wait()
    pl.semaphore_wait(barrier, 4)

    first.start()
    turn(enc, enct)
    store(2)
    first.hop(0)
    taps[...] = dot(table[...], bucket_rows(buckets, table.shape[1]).astype(BF))
    position_bias(taps, bias, length)
    seg_masks(drow, erow, neg_s, neg_c, length)

    def middle(t):
        first.hop(t)
        first.relay(t - 1)
    lax.fori_loop(1, hops - 1, lambda t, c: (middle(t), c)[1], 0)
    for c in loads[8:]:
        c.wait()
    second.start()
    first.hop(hops - 1, True)
    first.relay(hops - 2)
    first.relay(hops - 1)
    first.complete()
    weights_out = pltpu.make_async_copy(w, w_out, store_s.at[15])
    weights_out.start()
    for j in range(w.shape[2] // 128):
        v = gn[j * per]
        for i in range(1, per):
            v = v + gn[j * per + i]
        for i in range(3):
            gains[i, :, j * 128:(j + 1) * 128] = v[i:i + 1, :]
    store(14)

    def some(begin, end, f):
        lax.fori_loop(begin, end, lambda i, c: (f(i), c)[1], 0)

    def heads():
        normed(x, gains.at[0], h)
        for i in range(3):
            project(h, w.at[i], qkv.at[i])

    def own(i):
        attend(i, qkv.at[0], qkv.at[1], qkv.at[2], p1, o, neg_s, bias, length, length)

    def cross_heads():
        store(8, 11)
        turn(h, xt.at[0])
        turn(o, xt.at[1])
        project(o, w.at[3], x1, base=x, kind=F32)
        normed(x1, gains.at[1], h)
        project(h, w.at[4], cq)

    def cross_keys():
        store(7, 9)
        turn(h, xt.at[2])
        for i in range(2):
            project(enc, w.at[6 + i], ckv.at[i])

    def cross(i):
        attend(i, cq, ckv.at[0], ckv.at[1], p2, o, neg_c, None, length, keys)

    def before_feed():
        store(10, 12)
        turn(o, xt.at[3])
        store(1)
        project(o, w.at[5], x2, base=x1, kind=F32)
        normed(x2, gains.at[2], h)
        turn(h, hfft)
        store(3)

    total = count * pairs
    mid = total // 2
    chunks = [heads, lambda: some(0, mid, own), lambda: some(mid, total, own), cross_heads, cross_keys,
              lambda: some(0, mid, cross), lambda: some(mid, total, cross)]
    for t in range(len(chunks)):
        chunks[t]()
        second.hop(t, t == hops - 1)
        if t > 0:
            second.relay(t - 1)
    if hops > len(chunks):
        def rest(t):
            second.hop(t)
            second.relay(t - 1)
        some(len(chunks), hops - 1, rest)
        second.hop(hops - 1, True)
        second.relay(hops - 2)
    before_feed()
    second.relay(hops - 1)
    second.complete()

    each(hid.shape[1] // TILE, lambda c: feed_tile(c, h, cot, gu.at[0], gu.at[1], dn, hid, dgu.at[0], dgu.at[1]))
    store(5)
    turn(hid, hidt)
    store(4)
    project_t([(dgu.at[0], gu.at[0]), (dgu.at[1], gu.at[1])], dh)
    norm_back(x2, gains.at[2], dh, cot, r1, gain3)
    store(6, 13)
    project(hid, dn, out, base=x2)
    store(0)
    first.drain()
    second.drain()
    weights_out.wait()
    for i in range(15):
        stored(i).wait()


def forward(n, weights, own_gains, x, enc, cot, drow, erow, buckets, table):
    hops = n // 2 - 1
    rows, width = weights[0].shape
    ff = weights[8].shape[1]
    tokens, etokens = x.shape[0], enc.shape[0]
    count, _, length = drow.shape
    keys = etokens // count
    pairs = width // 128
    S = jax.ShapeDtypeStruct

    def v(*shape, t=BF):
        return pltpu.VMEM(shape, t)

    kept = [
        S((tokens, width), BF), S((4, width, tokens), BF), S((width, etokens), BF),
        S((width, tokens), BF), S((ff, tokens), BF), S((2, tokens, ff), BF), S((tokens, width), F32), S((tokens, width), F32),
        S((3, tokens, width), BF), S((tokens, width), BF), S((2, etokens, width), BF),
        S((count * pairs, 2 * length, length), BF), S((count * pairs, 2 * length, keys), BF),
        S((1, width), F32), S((3, 1, width), F32),
    ]
    vm, hbm = pl.BlockSpec(memory_space=pltpu.VMEM), pl.BlockSpec(memory_space=pl.ANY)
    return pl.pallas_call(
        functools.partial(forward_kernel, n, (length, keys)),
        name="gather_forward",
        out_shape=(S((8, width, width), BF),) + tuple(kept),
        in_specs=[hbm] * 11 + [vm] * 10,
        out_specs=[hbm] * 16,
        scratch_shapes=[v(*a.shape, t=a.dtype) for a in kept] + [
            v(8, width, width), v(2, width, ff), v(ff, width), v(n, 8, 128, t=F32), v(table.shape[0], length, t=F32),
            v(pairs, 2 * length, length, t=F32), v(count, length, length, t=F32), v(count, length, keys, t=F32),
            v(tokens, width), v(tokens, ff), v(tokens, width, t=F32), v(tokens, width, t=F32), v(tokens, width),
        ] + gather_sems(hops, 6, 3) + gather_sems(hops, 2, 1) + [pltpu.SemaphoreType.DMA((11,)), pltpu.SemaphoreType.DMA((16,))],
        compiler_params=pltpu.CompilerParams(collective_id=0, has_side_effects=True, vmem_limit_bytes=67043328),
    )(*weights, *own_gains, x, enc, cot, drow, erow, buckets, table)


class Group:
    def __init__(self, left, right, size, refs):
        self.left, self.right = left, right
        self.count, self.rows, self.half, self.share = size
        self.ss, self.sr, self.ys, self.yr, self.rs, self.rr, self.own, self.got = refs

    def part(self, i, dev, start, width):
        return dot(self.left(i, dev), self.right(i, pl.ds(pl.multiple_of(start, 128), width)))


def group_shapes(size, slots):
    count, rows, half, share = size
    sib_slots, y_slots, ring_slots = slots

    def v(*shape):
        return pltpu.VMEM(shape, BF)
    crossing = [v(2, 2, count, rows, share), v(y_slots, 2, count, rows, share)] if share else [v(16, 128), v(16, 128)]
    return [v(2, 2, count, rows, half), v(sib_slots, 2, count, rows, half)] + crossing + [
        v(2, 2, count, rows, half - share), v(ring_slots, 2, count, rows, half - share)]


def reduce_sems(groups, slots):
    dma = pltpu.SemaphoreType.DMA
    sib_slots, y_slots, ring_slots = slots
    return [dma((2, 2, groups)), dma((sib_slots, 2, groups)), dma((2, 2, groups)), dma((y_slots, 2, groups)),
            dma((2, 2, groups)), dma((ring_slots, 2, groups)), dma((2, 2 * groups)), dma((2, 2 * groups)),
            pltpu.SemaphoreType.REGULAR((3, 2))]


class Reduce:
    def __init__(self, geo, groups, slots, sems):
        self.chips, self.me, self.rep, self.core, self.ring, self.device_at = geo
        self.groups = groups
        self.shared = groups[0].share > 0
        self.slots = slots
        self.sib_s, self.sib_r, self.y_s, self.y_r, self.ring_s, self.ring_r, self.fin_s, self.fin_r, self.free = sems
        self.other = 1 - self.rep
        self.sibling = (self.me + 1 - 2 * self.core, self.rep)
        self.opposite = (self.me, self.other)
        self.after = ((self.device_at(self.ring + 1), self.rep), (self.device_at(self.ring - 1), self.rep))

    def block(self, t, way, core):
        return self.device_at(self.ring + (2 * way - 1) * (1 + t)) + core - self.core

    def toward(self, way):
        return (self.after[0][0] + way * (self.after[1][0] - self.after[0][0]), self.rep)

    def behind(self, way):
        return (self.after[1][0] + way * (self.after[0][0] - self.after[1][0]), self.rep)

    def sib_copies(self, t, way):
        s, r = lax.rem(t, 2), lax.rem(t, self.slots[0])
        return [rdma(g.ss.at[s, way], g.sr.at[r, way], self.sib_s.at[s, way, i], self.sib_r.at[r, way, i], self.sibling)
                for i, g in enumerate(self.groups)]

    def y_copies(self, t, way):
        s, r = lax.rem(t, 2), lax.rem(t, self.slots[1])
        return [rdma(g.ys.at[s, way], g.yr.at[r, way], self.y_s.at[s, way, i], self.y_r.at[r, way, i], self.opposite)
                for i, g in enumerate(self.groups)]

    def ring_copies(self, t, way):
        s, r = lax.rem(t, 2), lax.rem(t + 1, self.slots[2])
        return [rdma(g.rs.at[s, way], g.rr.at[r, way], self.ring_s.at[s, way, i], self.ring_r.at[r, way, i], self.toward(way))
                for i, g in enumerate(self.groups)]

    def claim(self, kind, step, way):
        if self.slots[kind] < self.chips:
            @pl.when(step >= self.slots[kind])
            def _():
                pl.semaphore_wait(self.free.at[kind, way], 1)

    def release(self, kind, step, way, dev):
        if self.slots[kind] < self.chips:
            @pl.when(step + self.slots[kind] < self.chips)
            def _():
                pl.semaphore_signal(self.free.at[kind, way], inc=1, device_id=dev, device_id_type=MESH)

    def settle(self, t, copies):
        @pl.when(t >= 2)
        def _():
            for c in copies:
                c.wait_send()

    def to_sibling(self, t):
        s = lax.rem(t, 2)

        def go(way):
            dev = self.block(t, way, 1 - self.core)
            self.settle(t, self.sib_copies(t, way))
            for g in self.groups:
                for i in range(g.count):
                    g.ss[s, way, i] = g.part(i, dev, way * g.half, g.half).astype(BF)
            self.claim(0, t, way)
            for c in self.sib_copies(t, way):
                c.start()
        each(2, go)

    def to_across(self, t):
        s, r = lax.rem(t, 2), lax.rem(t, self.slots[0])

        def go(way):
            dev = self.block(t, way, self.core)
            self.settle(t, self.y_copies(t, way))
            for c in self.sib_copies(t, way):
                c.wait_recv()
            for g in self.groups:
                at = pl.multiple_of(self.other * g.share, 128)
                for i in range(g.count):
                    v = g.part(i, dev, way * g.half + at, g.share)
                    g.ys[s, way, i] = (v + g.sr[r, way, i, :, pl.ds(at, g.share)].astype(F32)).astype(BF)
            self.claim(1, t, way)
            for c in self.y_copies(t, way):
                c.start()
        each(2, go)

    def to_ring(self, t, at_once):
        s, b, y, r = lax.rem(t, 2), lax.rem(t, self.slots[0]), lax.rem(t, self.slots[1]), lax.rem(t, self.slots[2])

        for k, g in enumerate(self.groups):
            def go(way, k=k, g=g):
                dev = self.block(t, way, self.core)
                if not self.shared:
                    self.sib_copies(t, way)[k].wait_recv()
                lo, wide = 2 * g.share, g.half - 2 * g.share
                at = pl.multiple_of(self.rep * g.share, 128)
                common, apart = [], []
                for i in range(g.count):
                    if self.shared:
                        v = g.part(i, dev, way * g.half + at, g.share)
                        common.append(v + g.sr[b, way, i, :, pl.ds(at, g.share)].astype(F32))
                    v = g.part(i, dev, way * g.half + lo, wide)
                    apart.append(v + g.sr[b, way, i, :, lo:].astype(F32))
                self.settle(t, self.ring_copies(t, way)[k:k + 1])
                if self.shared:
                    self.y_copies(t, way)[k].wait_recv()

                @pl.when(t >= 1)
                def _():
                    self.ring_copies(t - 1, way)[k].wait_recv()
                for i in range(g.count):
                    if self.shared:
                        v = common[i] + g.yr[y, way, i].astype(F32) + g.rr[r, way, i, :, :g.share].astype(F32)
                        g.rs[s, way, i, :, :g.share] = v.astype(BF)
                    g.rs[s, way, i, :, g.share:] = (apart[i] + g.rr[r, way, i, :, g.share:].astype(F32)).astype(BF)

                @pl.when(t < self.chips - 1)
                def _():
                    if k == 0:
                        self.claim(2, t + 1, way)
                    self.ring_copies(t, way)[k].start()

                @pl.when(t == self.chips - 1)
                def _():
                    if at_once:
                        self.send_final(way, k)
                    last = (self.chips - 1) % 2
                    if self.shared:
                        cols = pl.ds(pl.multiple_of(way * g.half + self.rep * g.share, 128), g.share)
                        g.own[:, :, cols] = g.rs[last, way, :, :, :g.share]
                    rest = pl.ds(pl.multiple_of(way * g.half + lo, 128), wide)
                    g.own[:, :, rest] = g.rs[last, way, :, :, g.share:]
                if k == len(self.groups) - 1:
                    self.release(0, t, way, self.sibling)
                    if self.shared:
                        self.release(1, t, way, self.opposite)
                    self.release(2, t, way, self.behind(way))
            each(2, go)

    def send_final(self, way, k):
        for c in self.final_copies(way, k):
            c.start()

    def final_copies(self, way, k):
        g = self.groups[k]
        mine = g.rs.at[(self.chips - 1) % 2, way]
        cols = pl.ds(pl.multiple_of(way * g.half + self.rep * g.share, 128), g.share) if g.share else None
        wide = g.half - 2 * g.share
        there = pl.ds(pl.multiple_of(way * wide, 128), wide)
        found = [rdma(mine.at[:, :, pl.ds(g.share, wide)], g.got.at[:, :, there],
                      self.fin_s.at[way, 2 * k + 1], self.fin_r.at[way, 2 * k + 1], self.opposite)]
        if self.shared:
            found.append(rdma(mine.at[:, :, pl.ds(0, g.share)], g.own.at[:, :, cols],
                              self.fin_s.at[way, 2 * k], self.fin_r.at[way, 2 * k], self.opposite))
        return found

    def finish(self):
        def go(way):
            for k, g in enumerate(self.groups):
                wide = g.half - 2 * g.share
                if self.shared:
                    ref = g.own.at[:, :, pl.ds(pl.multiple_of(way * g.half + self.other * g.share, 128), g.share)]
                    rdma(ref, ref, self.fin_s.at[way, 2 * k], self.fin_r.at[way, 2 * k], self.opposite).wait_recv()
                ref = g.got.at[:, :, pl.ds(pl.multiple_of(way * wide, 128), wide)]
                rdma(ref, ref, self.fin_s.at[way, 2 * k + 1], self.fin_r.at[way, 2 * k + 1], self.opposite).wait_recv()
                for c in self.final_copies(way, k):
                    c.wait_send()
            for t in (self.chips - 2, self.chips - 1):
                for c in self.sib_copies(t, way) + (self.y_copies(t, way) if self.shared else []):
                    c.wait_send()
            for c in self.ring_copies(self.chips - 2, way):
                c.wait_send()
        each(2, go)

    def at(self, t, f, *more):
        @pl.when((t >= 0) & (t < self.chips))
        def _():
            f(t, *more)


class Butterfly:
    def __init__(self, geo, n, buf, got, sems):
        _, self.me, self.rep, _, _, _ = geo
        self.stages = n.bit_length() - 1
        self.buf, self.got = buf, got
        self.send, self.recv = sems

    def partner(self, bit):
        return (self.me + bit - 2 * bit * lax.rem(lax.div(self.me, bit), 2), self.rep)

    def copy(self, j, dev):
        return rdma(self.buf.at[j], self.got.at[j], self.send.at[j], self.recv.at[j], dev)

    def begin(self):
        self.copy(0, (self.me, 1 - self.rep)).start()

    def stage(self, j, bit):
        self.copy(j - 1, self.partner(bit)).wait_recv()
        self.buf[j] = self.buf[j - 1] + self.got[j - 1]
        self.copy(j, self.partner(bit)).start()

    def end(self, dst):
        self.copy(self.stages, self.partner(1)).wait_recv()
        dst[...] = self.buf[self.stages] + self.got[self.stages]
        for j in range(self.stages + 1):
            self.copy(j, self.partner(1)).wait_send()


OFFSETS = (0, 0, 0, 5, 8)
FINALS = (1, 2, 3, 1, 0)
CHAINS = ((2,), (3,), (4,), (0, 5), (1, 6))
SLOTS = (3, 3, 3)
FIRST_PIECE = 0


def backward_kernel(n, sizes, dims, *refs):
    length, keys = dims
    ins, w_hbm, refs = refs[:16], refs[16], refs[17:]
    outs, (small_o, dtok, denc), refs = refs[:14], refs[14:17], refs[17:]
    held, refs = refs[:16], refs[16:]
    hfft, hidt, dgu, cot, r1, cq, ckv, p2, x1, gains, qkv, p1, x, xt, enct, gain3 = held
    bufs, refs = refs[:42], refs[42:]
    sems, refs = [refs[9 * k:9 * k + 9] for k in range(5)], refs[45:]
    sm, sm_got, sm_s, sm_r, load_s, w, w_s, dy, dye, dh, r0, do, gain12, diag = refs
    geo = geometry(n)
    chips, me, rep, core, ring, device_at = geo
    rows, rows_d = sizes[0][1], sizes[4][1]

    loads = [pltpu.make_async_copy(a, b, load_s.at[i]) for i, (a, b) in enumerate(zip(ins, held))]
    for c in loads[:4]:
        c.start()

    def fetch(i, slot):
        return pltpu.make_async_copy(w_hbm.at[i], w.at[slot], w_s.at[slot])

    def block(dev, size):
        return pl.ds(pl.multiple_of(dev * size, size), size)
    lefts = [lambda i, dev: xt[(3, 2)[i], block(dev, rows), :], lambda i, dev: xt[(1, 0)[i], block(dev, rows), :],
             lambda i, dev: hfft[block(dev, rows), :], lambda i, dev: hfft[block(dev, rows), :],
             lambda i, dev: hidt[block(dev, rows_d), :], lambda i, dev: enct[block(dev, rows), :], lambda i, dev: xt[0, block(dev, rows), :]]
    rights = [lambda i, c: dy[i, :, c], lambda i, c: dy[2 + i, :, c], lambda i, c: dgu[0, :, c], lambda i, c: dgu[1, :, c],
              lambda i, c: cot[:, c], lambda i, c: dye[i, :, c], lambda i, c: dy[4 + i, :, c]]
    groups = [Group(lefts[k], rights[k], sizes[k], bufs[6 * k:6 * k + 6] + outs[2 * k:2 * k + 2]) for k in range(7)]
    chains = [Reduce(geo, [groups[k] for k in c], SLOTS, s) for c, s in zip(CHAINS, sems)]
    tree = Butterfly(geo, n, sm, sm_got, (sm_s, sm_r))
    lead = chains[0]

    barrier = pltpu.get_barrier_semaphore()
    greet = [lead.after[0], lead.after[1], lead.sibling, lead.opposite] + [tree.partner(1 << j) for j in range(tree.stages)]
    for dev in greet:
        pl.semaphore_signal(barrier, inc=1, device_id=dev, device_id_type=MESH)
    for g in groups:
        g.rr[0] = jnp.zeros(g.rr.shape[1:], BF)
    diag[...] = jnp.zeros(diag.shape, F32)
    for c in loads[:4]:
        c.wait()
    for c in loads[4:]:
        c.start()
    for i, slot in ((5, 0), (6, 1), (7, 2), (4, 3)):
        fetch(i, slot).start()
    pl.semaphore_wait(barrier, len(greet))

    total = p1.shape[0]
    width = dh.shape[1]

    def start_back():
        for c in loads[4:]:
            c.wait()
        dy[0] = r1[...].astype(BF)
        fetch(5, 0).wait()
        project_t([(dy.at[0], w.at[0])], do, kind=BF)
        fetch(3, 0).start()

    def cross(begin, end):
        def f():
            lax.fori_loop(begin, end, lambda i, c: (attend_back(
                i, cq, ckv.at[0], ckv.at[1], p2, do, dy.at[1], dye.at[0], dye.at[1], None, length, keys), c)[1], 0)
        return f

    def own(begin, end):
        def f():
            lax.fori_loop(begin, end, lambda i, c: (attend_back(
                i, qkv.at[0], qkv.at[1], qkv.at[2], p1, do, dy.at[3], dy.at[4], dy.at[5], diag, length, length), c)[1], 0)
        return f

    def encoder(begin, end, last):
        def f():
            if not last:
                fetch(6, 1).wait()
                fetch(7, 2).wait()
            project_t([(dye.at[0], w.at[1]), (dye.at[1], w.at[2])], denc, begin=begin, end=end)
            if last:
                fetch(0, 1).start()
                fetch(1, 2).start()
        return f

    def cross_norm():
        norm_back(x1, gains.at[1], dh, r1, r0, gain12.at[1])
        dy[2] = r0[...].astype(BF)

    def cross_query():
        fetch(4, 3).wait()
        project_t([(dy.at[1], w.at[3])], dh)
        fetch(2, 3).start()

    def own_out():
        fetch(3, 0).wait()
        project_t([(dy.at[2], w.at[0])], do, kind=BF)

    def own_in(begin, end, last):
        def f():
            if not last:
                for i, slot in ((0, 1), (1, 2), (2, 3)):
                    fetch(i, slot).wait()
            project_t([(dy.at[3], w.at[1]), (dy.at[4], w.at[2]), (dy.at[5], w.at[3])], dh, begin=begin, end=end)
        return f

    def own_norm():
        norm_back(x, gains.at[0], dh, r0, dtok, gain12.at[0])
        for k in range(width // 128):
            for i, g in enumerate((gain12.at[0], gain12.at[1], gain3)):
                sm[0, pl.ds(i * (width // 128) + k, 1), :] = g[:, k * 128:(k + 1) * 128]
        for i in range(diag.shape[0]):
            sm[0, pl.ds(3 * (width // 128) + i, 1), :] = diag[i]

    tiles = width // TILE
    pieces = [start_back]
    pieces += [cross(total * k // 8, total * (k + 1) // 8) for k in range(8)]
    pieces += [cross_query, cross_norm, own_out]
    pieces += [own(total * k // 5, total * (k + 1) // 5) for k in range(5)]
    pieces += [encoder(0, tiles // 2, False), encoder(tiles // 2, tiles, True)]
    pieces += [own_in(0, tiles // 2, False), own_in(tiles // 2, tiles, True), own_norm]
    tree_at = 7

    def piece(u, which):
        for i in range(which, len(pieces), 3):
            pl.when(u == i // 3 + FIRST_PIECE)(pieces[i])

    def step(v, bit):
        u = v - 3
        for k, c in enumerate(chains):
            t = u - OFFSETS[k]
            c.at(t, c.to_ring, FINALS[k] == 0)
            if k < 3:
                piece(u, k)
            if FINALS[k]:
                for way in range(2):
                    for j in range(len(c.groups)):
                        pl.when(t == chips - 1 + FINALS[k] + way)(functools.partial(c.send_final, way, j))
        for k, c in enumerate(chains):
            if c.shared:
                c.at(u - OFFSETS[k] + 2, c.to_across)
        for k, c in enumerate(chains):
            c.at(u - OFFSETS[k] + 3, c.to_sibling)
        pl.when(u == tree_at)(tree.begin)
        inside = (u > tree_at) & (u <= tree_at + tree.stages)

        @pl.when(inside)
        def _():
            tree.stage(u - tree_at, bit)
        return jnp.where(inside, bit * 2, bit)

    lax.fori_loop(0, OFFSETS[-1] + chips + 3, step, jnp.int32(1))
    tree.end(small_o)
    for c in chains:
        c.finish()


def shares(half, part):
    return half * part // 1408 * 128


def backward(n, w, hfft, hidt, dgu, cot, r1, cq, ckv, p2, x1, gains, qkv, p1, x, xt, enct, gain3):
    chips = n // 2
    tokens, width = x.shape
    etokens, ff = enct.shape[1], dgu.shape[2]
    length, keys = p1.shape[2], p2.shape[2]
    rows, rows_d = width // n, hidt.shape[0] // n
    half, half_g = width // 2, ff // 2
    part = shares(half, 3)
    sizes = [(2, rows, half, part), (2, rows, half, part), (1, rows, half_g, shares(half_g, 3)),
             (1, rows, half_g, shares(half_g, 3)), (1, rows_d, half, part), (2, rows, half, part), (2, rows, half, part)]
    stages = n.bit_length() - 1
    dma = pltpu.SemaphoreType.DMA
    S = jax.ShapeDtypeStruct
    vm, hbm = pl.BlockSpec(memory_space=pltpu.VMEM), pl.BlockSpec(memory_space=pl.ANY)
    outs = []
    for count, r, h, share in sizes:
        outs += [S((count, r, 2 * h), BF), S((count, r, 2 * (h - 2 * share)), BF)]
    small = (3 * (width // 128) + width // 64, 128)
    ins = (hfft, hidt, dgu, cot, r1, cq, ckv, p2, x1, gains, qkv, p1, x, xt, enct, gain3)
    slots = tuple(min(s, chips) for s in SLOTS)
    return pl.pallas_call(
        functools.partial(backward_kernel, n, sizes, (length, keys)),
        name="backward_reduce",
        out_shape=tuple(outs) + (S(small, F32), S((tokens, width), F32), S((etokens, width), F32)),
        in_specs=[hbm] * 17,
        out_specs=[vm] * 17,
        scratch_shapes=[pltpu.VMEM(a.shape, a.dtype) for a in ins]
        + [b for size in sizes for b in group_shapes(size, slots)]
        + [s for c in CHAINS for s in reduce_sems(len(c), slots)]
        + [pltpu.VMEM((stages + 1,) + small, F32)] * 2 + [dma((stages + 1,))] * 2
        + [dma((16,)), pltpu.VMEM((4, width, width), BF), dma((4,)), pltpu.VMEM((6, tokens, width), BF),
           pltpu.VMEM((2, etokens, width), BF), pltpu.VMEM((tokens, width), F32), pltpu.VMEM((tokens, width), F32),
           pltpu.VMEM((tokens, width), BF), pltpu.VMEM((2, 1, width), F32), pltpu.VMEM((width // 64, 1, 128), F32)],
        compiler_params=pltpu.CompilerParams(collective_id=1, has_side_effects=True, vmem_limit_bytes=67043328),
    )(*ins, w)


def finish_kernel(sizes, passed, buckets_count, *refs):
    parts, mats = 2 * len(sizes), sum(s[0] for s in sizes)
    ins, (small, buckets), refs = refs[:parts + passed], refs[parts + passed:parts + passed + 2], refs[parts + passed + 2:]
    outs, (dtable, gain1, gain2, gain3), refs = refs[:mats + passed], refs[mats + passed:mats + passed + 4], refs[mats + passed + 4:]
    held, done, (load_s, store_s) = refs[:parts + passed], refs[parts + passed:-2], refs[-2:]
    loads = [pltpu.make_async_copy(a, b, load_s.at[i]) for i, (a, b) in enumerate(zip(ins, held))]
    stores = [pltpu.make_async_copy(a, b, store_s.at[i]) for i, (a, b) in enumerate(zip(done + held[parts:], outs))]
    for c in loads:
        c.start()
    at = 0
    for k, (count, rows, half, share) in enumerate(sizes):
        own, got = held[2 * k], held[2 * k + 1]
        loads[2 * k].wait()
        loads[2 * k + 1].wait()
        wide = half - 2 * share
        for i in range(count):
            for way in range(2):
                lo = way * half
                if share:
                    done[at][:, lo:lo + 2 * share] = own[i, :, lo:lo + 2 * share].astype(F32)
                v = own[i, :, lo + 2 * share:lo + half].astype(F32) + got[i, :, way * wide:(way + 1) * wide].astype(F32)
                done[at][:, lo + 2 * share:lo + half] = v
            stores[at].start()
            at += 1
    for i in range(passed):
        loads[parts + i].wait()
        stores[mats + i].start()
    me = lax.axis_index("shard")
    rows = gain1.shape[1]
    per = 128 // rows
    heads = dtable.shape[0]
    tiles = (small.shape[0] - heads) // 3
    tile = lax.broadcasted_iota(jnp.int32, (tiles, 128), 0)
    for i, dst in enumerate((gain1, gain2, gain3)):
        v = jnp.where(tile == lax.div(me, per), small[i * tiles:(i + 1) * tiles, :], 0.0)
        v = pltpu.roll(v, lax.rem(128 - lax.rem(me, per) * rows, 128), 1)
        dst[...] = jnp.sum(v, axis=0, keepdims=True)[:, :rows]
    dtable[...] = lax.dot_general(small[3 * tiles:, :], bucket_rows(buckets, buckets_count), (((1,), (1,)), ((), ())),
                                  precision=lax.Precision.HIGHEST, preferred_element_type=F32)
    for c in stores:
        c.wait()


def finish(parts, passed, small, buckets, shape, rows):
    sizes, outs = [], []
    S = jax.ShapeDtypeStruct
    for own, got in zip(parts[0::2], parts[1::2]):
        count, r, width = own.shape
        half = width // 2
        sizes.append((count, r, half, (half - got.shape[2] // 2) // 2))
        outs += [S((r, width), F32)] * count
    vm, hbm = pl.BlockSpec(memory_space=pltpu.VMEM), pl.BlockSpec(memory_space=pl.ANY)
    ins = list(parts) + list(passed)
    dma = pltpu.SemaphoreType.DMA
    return pl.pallas_call(
        functools.partial(finish_kernel, sizes, len(passed), shape[1]),
        name="finish",
        out_shape=tuple(outs) + tuple(S(a.shape, a.dtype) for a in passed) + (S(shape, F32),) + (S((1, rows), F32),) * 3,
        in_specs=[hbm] * len(ins) + [vm] * 2,
        out_specs=[hbm] * (len(outs) + len(passed)) + [vm] * 4,
        scratch_shapes=[pltpu.VMEM(a.shape, a.dtype) for a in ins] + [pltpu.VMEM(a.shape, a.dtype) for a in outs]
        + [dma((len(ins),)), dma((len(outs) + len(passed),))],
        compiler_params=pltpu.CompilerParams(vmem_limit_bytes=67043328),
    )(*ins, small, buckets)


def body(hidden_in, encoded, dec_segments, enc_segments, buckets, out_cot, norm_self, self_query, self_key, self_value,
         self_out, table, norm_cross, cross_query, cross_key, cross_value, cross_out, norm_ff, ff_gate, ff_up, ff_down, *, n):
    micro, per, length, width = hidden_in.shape
    keys = encoded.shape[2]
    count = micro * per
    rows, rows_d, ff = self_query.shape[0], ff_down.shape[0], ff_gate.shape[1]
    spare = -rows_d % 16
    if spare:
        ff_down = jnp.pad(ff_down, ((0, spare), (0, 0)))
        ff_gate, ff_up = [jnp.pad(w.reshape(rows, n, rows_d), ((0, 0), (0, 0), (0, spare))).reshape(rows, -1) for w in (ff_gate, ff_up)]
    x = hidden_in.reshape(count * length, width)
    enc = encoded.reshape(count * keys, width)
    cot = out_cot.reshape(count * length, width)
    buckets = buckets.reshape(1, length)
    weights = (self_query, self_key, self_value, self_out, cross_query, cross_out, cross_key, cross_value, ff_gate, ff_up, ff_down)
    own_gains = [g.reshape(1, rows) for g in (norm_self, norm_cross, norm_ff)]
    w, out, xt, enct, hfft, hidt, dgu, r1, x1, qkv, cq, ckv, p1, p2, gain3, gains = forward(
        n, weights, own_gains, x, enc, cot, dec_segments.reshape(count, 1, length), enc_segments.reshape(count, 1, keys), buckets, table.T)
    *parts, small, dtok, denc = backward(n, w, hfft, hidt, dgu, cot, r1, cq, ckv, p2, x1, gains, qkv, p1, x, xt, enct, gain3)
    gco, gcq, gso, gq, gg, gup, gd, gck, gcv, gk, gv, out, dtok, denc, dtable, g1, g2, g3 = finish(
        parts, (out, dtok, denc), small, buckets, table.T.shape, rows)
    if spare:
        gd = gd[:rows_d]
        gg, gup = [g.reshape(rows, n, -1)[:, :, :rows_d].reshape(rows, ff) for g in (gg, gup)]
    return (
        out.reshape(hidden_in.shape), dtok.reshape(hidden_in.shape), denc.reshape(encoded.shape),
        g1.reshape(rows), gq, gk, gv, gso, dtable.T, g2.reshape(rows), gcq, gck, gcv, gco, g3.reshape(rows), gg, gup, gd,
    )


def solution(mesh):
    tok = P(None, ("shard", "rep"), None, None)
    seg = P(None, ("shard", "rep"), None)
    vec, mat, rep = P("shard"), P("shard", None), P()
    return jax.shard_map(
        functools.partial(body, n=mesh.shape["shard"]),
        mesh=mesh,
        in_specs=(tok, tok, seg, seg, rep, tok, vec, mat, mat, mat, mat, rep, vec, mat, mat, mat, mat, vec, mat, mat, mat),
        out_specs=(tok, tok, tok, vec, mat, mat, mat, mat, rep, vec, mat, mat, mat, mat, vec, mat, mat, mat),
        check_vma=False,
    )
```

```python
import functools
import math

import jax
import jax.numpy as jnp
from jax import lax
from jax.experimental import pallas as pl
from jax.experimental.pallas import tpu as pltpu
from jax.sharding import PartitionSpec as P

MESH = pl.DeviceIdType.MESH
BF = jnp.bfloat16
F32 = jnp.float32
EPS = 1e-06
NEG = -1e30
C1 = math.sqrt(2.0 / math.pi)
C2 = 0.044715
TILE = 256


def each(count, f):
    def step(i, carry):
        f(i)
        return carry
    lax.fori_loop(0, count, step, 0)


def tile_at(i, size=TILE):
    return pl.ds(pl.multiple_of(i * size, size), size)


def dot(a, b):
    return jnp.dot(a, b, preferred_element_type=F32)


def dot_t(a, b):
    return lax.dot_general(a, b, (((1,), (1,)), ((), ())), preferred_element_type=F32)


def dot_rows(a, b):
    return lax.dot_general(a, b, (((0,), (0,)), ((), ())), preferred_element_type=F32)


def normed(src, gain, dst):
    def rows(i):
        r = tile_at(i, 32)
        v = src[r, :].astype(F32)
        t = lax.rsqrt(jnp.mean(v * v, axis=-1, keepdims=True) + EPS)
        dst[r, :] = (v * t * gain[...]).astype(BF)
    each(src.shape[0] // 32, rows)


def norm_back(src, gain, grad, base, dst, gain_sum):
    gain_sum[...] = jnp.zeros(gain_sum.shape, F32)

    def rows(i):
        r = tile_at(i, 16)
        v = src[r, :].astype(F32)
        dy = grad[r, :]
        g = gain[...]
        t = lax.rsqrt(jnp.mean(v * v, axis=-1, keepdims=True) + EPS)
        vt = v * t
        gdy = g * dy
        inner = jnp.mean(vt * gdy, axis=-1, keepdims=True)
        dst[r, :] = base[r, :].astype(F32) + t * (gdy - vt * inner)
        gain_sum[...] += jnp.sum(vt * dy, axis=0, keepdims=True)
    each(src.shape[0] // 16, rows)


def turn(src, dst):
    for b in range(src.shape[0] // 128):
        def block(c, b=b):
            dst[tile_at(c), b * 128:(b + 1) * 128] = src[b * 128:(b + 1) * 128, tile_at(c)].T
        each(src.shape[1] // TILE, block)


def head_masks():
    lane = lax.broadcasted_iota(jnp.int32, (1, 128), 1)
    even = (lane < 64).astype(F32).astype(BF)
    return even, (lane >= 64).astype(F32).astype(BF)


def pair_rows(x, masks):
    return jnp.concatenate([x * masks[0], x * masks[1]], axis=0)


def side_by_side(x):
    half = x.shape[0] // 2
    return jnp.concatenate([x[:half], x[half:]], axis=1)


def attend(i, q, k, v, p, o, neg, bias, length, keys):
    masks = head_masks()
    pairs = q.shape[1] // 128
    b, pair = lax.div(i, pairs), lax.rem(i, pairs)
    lanes = tile_at(pair, 128)
    rows, krows = tile_at(b, length), tile_at(b, keys)
    s = dot_t(pair_rows(q[rows, lanes], masks), k[krows, lanes])
    if bias is not None:
        s = s + bias[pair]
    n = neg[b]
    s = s + jnp.concatenate([n, n], axis=0)
    e = jnp.exp(s - jnp.max(s, axis=-1, keepdims=True))
    pb = (e * (1.0 / jnp.sum(e, axis=-1, keepdims=True))).astype(BF)
    p[i] = pb
    o[rows, lanes] = dot(side_by_side(pb), pair_rows(v[krows, lanes], masks)).astype(BF)


def attend_back(i, q, k, v, p, do, dq, dk, dv, diag, length, keys):
    masks = head_masks()
    pairs = q.shape[1] // 128
    b, pair = lax.div(i, pairs), lax.rem(i, pairs)
    lanes = tile_at(pair, 128)
    rows, krows = tile_at(b, length), tile_at(b, keys)
    dos = pair_rows(do[rows, lanes], masks)
    dp = dot_t(dos, v[krows, lanes])
    pb = p[i]
    pf = pb.astype(F32)
    ds = (pf * (dp - jnp.sum(pf * dp, axis=-1, keepdims=True))).astype(BF)
    dq[rows, lanes] = dot(side_by_side(ds), pair_rows(k[krows, lanes], masks)).astype(BF)
    dk[krows, lanes] = dot_rows(ds, pair_rows(q[rows, lanes], masks)).astype(BF)
    dv[krows, lanes] = dot_rows(pb, dos).astype(BF)
    if diag is not None:
        i0 = lax.broadcasted_iota(jnp.int32, (length, length), 0)
        i1 = lax.broadcasted_iota(jnp.int32, (length, length), 1)
        flip = (i0 + i1 == length - 1).astype(F32).astype(BF)
        for h in range(2):
            u = pltpu.roll(dot(flip, ds[h * length:(h + 1) * length]), 1, 1, stride=1, stride_axis=0)
            diag[2 * pair + h] += jnp.sum(u, axis=0, keepdims=True)


def position_bias(taps, bias, length):
    def pair(i):
        for h in range(2):
            w = jnp.broadcast_to(taps[pl.ds(2 * i + h, 1), :], (length, length))
            bias[i, h * length:(h + 1) * length, :] = pltpu.roll(w, 0, 1, stride=1, stride_axis=0)
    each(bias.shape[0], pair)


def seg_masks(drow, erow, neg_self, neg_cross, length):
    for b in range(drow.shape[0]):
        row = drow[b].astype(F32)
        col = jnp.broadcast_to(row, (length, length)).T
        i = lax.broadcasted_iota(jnp.int32, (length, length), 0)
        j = lax.broadcasted_iota(jnp.int32, (length, length), 1)
        neg_self[b] = jnp.where((j <= i) & (col == row), 0.0, NEG)
        enc = erow[b].astype(F32)
        for k in range(enc.shape[1] // length):
            part = slice(k * length, (k + 1) * length)
            neg_cross[b, :, part] = jnp.where(col == enc[:, part], 0.0, NEG)


def bucket_rows(buckets, count):
    length = buckets.shape[1]
    i = lax.broadcasted_iota(jnp.int32, (count, length), 0)
    hot = (i == buckets[...]).astype(F32).astype(BF)
    m = lax.broadcasted_iota(jnp.int32, (length, length), 0)
    l = lax.broadcasted_iota(jnp.int32, (length, length), 1)
    back = ((m + l == length) | ((m == 0) & (l == 0))).astype(F32).astype(BF)
    return dot(hot, back)


def project(a, w, dst, base=None, kind=BF):
    def tile(c):
        v = dot(a[...], w[:, tile_at(c)])
        if base is not None:
            v = v + base[:, tile_at(c)].astype(F32)
        dst[:, tile_at(c)] = v.astype(kind)
    each(dst.shape[1] // TILE, tile)


def project_t(terms, dst, kind=F32, begin=0, end=None):
    def tile(c):
        v = None
        for a, w in terms:
            u = dot_t(a[...], w[tile_at(c), :])
            v = u if v is None else v + u
        dst[:, tile_at(c)] = v.astype(kind)
    lax.fori_loop(begin, dst.shape[1] // TILE if end is None else end, lambda i, carry: (tile(i), carry)[1], 0)


def feed_tile(c, h, cot, wg, wu, wd, hid, dgate, dup):
    cols = tile_at(c)
    hv = h[...]
    gate = dot(hv, wg[:, cols])
    up = dot(hv, wu[:, cols])
    dhid = dot_t(cot[...], wd[cols, :])
    sq = gate * gate
    th = jnp.tanh(C1 * gate * (1.0 + C2 * sq))
    hp = 0.5 * (1.0 + th)
    act = gate * hp
    hid[:, cols] = (act * up).astype(BF)
    slope = hp + (0.5 * C1) * gate * (1.0 - th * th) * (1.0 + (3.0 * C2) * sq)
    dgate[:, cols] = (dhid * up * slope).astype(BF)
    dup[:, cols] = (dhid * act).astype(BF)


def geometry(n):
    chips = n // 2
    side = chips // 2
    s = lax.axis_index("shard")
    rep = lax.axis_index("rep")
    core = lax.rem(s, 2)
    chip = lax.div(s, 2)
    x = lax.rem(chip, 2)
    z = lax.div(chip, 2)
    ring = z + x * (chips - 1 - 2 * z)

    def device_at(position):
        p = lax.rem(position + 2 * chips, chips)
        px = lax.div(p, side)
        pz = p + px * (chips - 1 - 2 * p)
        return (pz * 2 + px) * 2 + core

    return chips, s, rep, core, ring, device_at


def rdma(src, dst, ss, rs, dev):
    return pltpu.make_async_remote_copy(src_ref=src, dst_ref=dst, send_sem=ss, recv_sem=rs, device_id=dev, device_id_type=MESH)


class Gather:
    def __init__(self, geo, pieces, across, sems):
        self.chips, self.me, self.rep, self.core, self.ring, self.device_at = geo
        self.hops = self.chips - 1
        self.pieces, self.across = pieces, across
        self.ring_s, self.ring_r, self.sib_s, self.sib_r, self.y_s, self.y_r, self.yy_s, self.yy_r, self.own_s, self.own_r = sems
        self.other = 1 - 2 * self.core
        self.sibling = (self.me + self.other, self.rep)
        self.opposite = (self.me, 1 - self.rep)
        self.ahead = ((self.device_at(self.ring + 1), self.rep), (self.device_at(self.ring - 1), self.rep))

    def source(self, way, t):
        return self.device_at(self.ring - 1 - t) if way == 0 else self.device_at(self.ring + 1 + t)

    def each(self, rep, count=None):
        most = max(len(self.pieces(0, rep)), len(self.pieces(1, rep)))
        for p in range(most if count is None else count):
            for way in range(2):
                ps = self.pieces(way, rep)
                if p < len(ps):
                    yield way, p, ps[p]

    def ring_copy(self, way, t, p, ref):
        return rdma(ref, ref, self.ring_s.at[way, t, p], self.ring_r.at[way, t, p], self.ahead[way])

    def sib_copy(self, way, t, p, ref):
        return rdma(ref, ref, self.sib_s.at[way, t, p], self.sib_r.at[way, t, p], self.sibling)

    def y_copy(self, way, t, p, ref):
        return rdma(ref, ref, self.y_s.at[way, t, p], self.y_r.at[way, t, p], self.opposite)

    def yy_copy(self, way, t, p, ref):
        return rdma(ref, ref, self.yy_s.at[way, t, p], self.yy_r.at[way, t, p], self.sibling)

    def own_copies(self, src):
        found = []
        for rep in (self.rep, 1 - self.rep):
            for way, p, ref in self.each(rep, None if rep is self.rep else self.across):
                i = 0 if rep is self.rep else 1
                r = ref(src)
                found.append(rdma(r, r, self.own_s.at[i, way, p], self.own_r.at[i, way, p], self.sibling))
        return found

    def start(self):
        for way, p, ref in self.each(self.rep):
            self.ring_copy(way, 0, p, ref(self.me)).start()
        for c in self.own_copies(self.me):
            c.start()

    def hop(self, t, last=False, which=None):
        for way, p, ref in self.each(self.rep):
            if which is not None and p != which:
                continue
            r = ref(self.source(way, t))
            self.ring_copy(way, t, p, r).wait_recv()
            if not last:
                self.ring_copy(way, t + 1, p, r).start()
            if p < self.across:
                self.y_copy(way, t, p, r).start()
            self.sib_copy(way, t, p, r).start()

    def relay(self, t):
        for way, p, ref in self.each(1 - self.rep, self.across):
            r = ref(self.source(way, t))
            self.y_copy(way, t, p, r).wait_recv()
            self.yy_copy(way, t, p, r).start()

    def complete(self):
        def step(t):
            for way, p, ref in self.each(self.rep):
                self.sib_copy(way, t, p, ref(self.source(way, t) + self.other)).wait_recv()
            for way, p, ref in self.each(1 - self.rep, self.across):
                self.yy_copy(way, t, p, ref(self.source(way, t) + self.other)).wait_recv()
        each(self.hops, step)
        for c in self.own_copies(self.me + self.other):
            c.wait_recv()

    def drain(self):
        def step(t):
            for way, p, ref in self.each(self.rep):
                r = ref(self.source(way, t))
                self.ring_copy(way, t, p, r).wait_send()
                self.sib_copy(way, t, p, r).wait_send()
                if p < self.across:
                    self.y_copy(way, t, p, r).wait_send()
            for way, p, ref in self.each(1 - self.rep, self.across):
                self.yy_copy(way, t, p, ref(self.source(way, t))).wait_send()
        each(self.hops, step)
        for c in self.own_copies(self.me):
            c.wait_send()


def gather_sems(hops, pieces, across):
    dma = pltpu.SemaphoreType.DMA
    return [dma((2, hops, pieces))] * 4 + [dma((2, hops, across))] * 4 + [dma((2, 2, pieces))] * 2


def forward_kernel(n, dims, *refs):
    length, keys = dims
    ins, refs = refs[:11], refs[11:]
    own_gains, refs = refs[:3], refs[3:]
    x, enc, cot, drow, erow, buckets, table = refs[:7]
    w_out, kept, refs = refs[7], refs[8:23], refs[23:]
    out, xt, enct, hfft, hidt, dgu, r1, x1, qkv, cq, ckv, p1, p2, gain3, gains = held = refs[:15]
    w, gu, dn, gn, taps, bias, neg_s, neg_c, h, hid, x2, dh, o = refs[15:28]
    first_sems, second_sems = refs[28:38], refs[38:48]
    load_s, store_s = refs[48:50]

    def stored(i):
        return pltpu.make_async_copy(held[i], kept[i], store_s.at[i])

    def store(*which):
        for i in which:
            stored(i).start()
    geo = geometry(n)
    chips, me, rep, core, ring, device_at = geo
    hops = chips - 1
    rows, rows_d = ins[0].shape[0], ins[10].shape[0]
    half, half_g = w.shape[2] // 2, gu.shape[2] // 2
    count = drow.shape[0]
    pairs = w.shape[2] // 128

    def block(src):
        return pl.ds(pl.multiple_of(src * rows, rows), rows)

    def block_d(src):
        return pl.ds(pl.multiple_of(src * rows_d, rows_d), rows_d)

    def attention_pieces(way, r):
        c = pl.ds(way * half, half)
        near, far = pl.ds(way * half, half // 2), pl.ds(way * half + half // 2, half // 2)
        found = [lambda s: w.at[r, block(s), c], lambda s: w.at[4 + r, block(s), c], lambda s: w.at[2 + r, block(s), near],
                 lambda s: w.at[pl.ds(2, 2), block(s), far], lambda s: w.at[pl.ds(6, 2), block(s), c]]
        return found + [lambda s: gn.at[s]] if way == 0 else found

    def feed_pieces(way, r):
        return [lambda s: gu.at[r, block(s), pl.ds(way * half_g, half_g)], lambda s: dn.at[block_d(s), pl.ds(way * half, half)]]

    first = Gather(geo, attention_pieces, 3, first_sems)
    second = Gather(geo, feed_pieces, 1, second_sems)

    width = w.shape[2]
    places = [w.at[i, block(me), :] for i in range(8)] + [gu.at[i, block(me), :] for i in range(2)] + [dn.at[block_d(me), :]]
    loads = [pltpu.make_async_copy(a, b, load_s.at[i]) for i, (a, b) in enumerate(zip(ins, places))]
    for c in loads:
        c.start()
    barrier = pltpu.get_barrier_semaphore()
    for dev in first.ahead + (first.sibling, first.opposite):
        pl.semaphore_signal(barrier, inc=1, device_id=dev, device_id_type=MESH)
    per = 128 // rows
    lane = lax.broadcasted_iota(jnp.int32, (rows, 128), 1)
    spot = lax.broadcasted_iota(jnp.int32, (rows, 128), 0)
    place = (lane == spot + lax.rem(me, per) * rows).astype(F32).astype(BF)
    gn[me] = jnp.concatenate([dot(g[...], place) for g in own_gains] + [jnp.zeros((5, 128), F32)], axis=0)
    for c in loads[:8]:
        c.wait()
    pl.semaphore_wait(barrier, 4)

    first.start()
    turn(enc, enct)
    store(2)
    first.hop(0)
    taps[...] = dot(table[...], bucket_rows(buckets, table.shape[1]).astype(BF))
    position_bias(taps, bias, length)
    seg_masks(drow, erow, neg_s, neg_c, length)

    def middle(t):
        first.hop(t)
        first.relay(t - 1)
    lax.fori_loop(1, hops - 1, lambda t, c: (middle(t), c)[1], 0)
    for c in loads[8:]:
        c.wait()
    second.start()
    first.hop(hops - 1, True)
    first.relay(hops - 2)
    first.relay(hops - 1)
    first.complete()
    weights_out = pltpu.make_async_copy(w, w_out, store_s.at[15])
    weights_out.start()
    for j in range(w.shape[2] // 128):
        v = gn[j * per]
        for i in range(1, per):
            v = v + gn[j * per + i]
        for i in range(3):
            gains[i, :, j * 128:(j + 1) * 128] = v[i:i + 1, :]
    store(14)

    def some(begin, end, f):
        lax.fori_loop(begin, end, lambda i, c: (f(i), c)[1], 0)

    def heads():
        normed(x, gains.at[0], h)
        project(h, w.at[0], qkv.at[0])

    def keys_values():
        for i in range(1, 3):
            project(h, w.at[i], qkv.at[i])

    def own(i):
        attend(i, qkv.at[0], qkv.at[1], qkv.at[2], p1, o, neg_s, bias, length, length)

    def own_result():
        store(8, 11)
        turn(h, xt.at[0])
        turn(o, xt.at[1])
        project(o, w.at[3], x1, base=x, kind=F32)

    def cross_heads():
        normed(x1, gains.at[1], h)
        project(h, w.at[4], cq)

    def cross_keys():
        store(7, 9)
        turn(h, xt.at[2])
        project(enc, w.at[6], ckv.at[0])

    def cross(i):
        attend(i, cq, ckv.at[0], ckv.at[1], p2, o, neg_c, None, length, keys)

    def before_feed():
        store(10, 12)
        turn(o, xt.at[3])
        store(1)
        project(o, w.at[5], x2, base=x1, kind=F32)
        normed(x2, gains.at[2], h)
        turn(h, hfft)
        store(3)

    total = count * pairs
    def quarters(f):
        return [functools.partial(some, total * k // 4, total * (k + 1) // 4, f) for k in range(4)]
    halves = [heads, keys_values] + quarters(own) + [own_result, cross_heads, cross_keys, lambda: project(enc, w.at[7], ckv.at[1])] + quarters(cross)
    chunks = list(zip(halves[0::2], halves[1::2]))
    for t in range(len(chunks)):
        chunks[t][0]()
        second.hop(t, t == hops - 1, 0)
        if t > 0:
            second.relay(t - 1)
        chunks[t][1]()
        second.hop(t, t == hops - 1, 1)
    if hops > len(chunks):
        def rest(t):
            second.hop(t)
            second.relay(t - 1)
        some(len(chunks), hops - 1, rest)
        second.hop(hops - 1, True)
        second.relay(hops - 2)
    before_feed()
    second.relay(hops - 1)
    second.complete()

    each(hid.shape[1] // TILE, lambda c: feed_tile(c, h, cot, gu.at[0], gu.at[1], dn, hid, dgu.at[0], dgu.at[1]))
    store(5)
    turn(hid, hidt)
    store(4)
    project_t([(dgu.at[0], gu.at[0]), (dgu.at[1], gu.at[1])], dh)
    norm_back(x2, gains.at[2], dh, cot, r1, gain3)
    store(6, 13)
    project(hid, dn, out, base=x2)
    store(0)
    first.drain()
    second.drain()
    weights_out.wait()
    for i in range(15):
        stored(i).wait()


def forward(n, weights, own_gains, x, enc, cot, drow, erow, buckets, table):
    hops = n // 2 - 1
    rows, width = weights[0].shape
    ff = weights[8].shape[1]
    tokens, etokens = x.shape[0], enc.shape[0]
    count, _, length = drow.shape
    keys = etokens // count
    pairs = width // 128
    S = jax.ShapeDtypeStruct

    def v(*shape, t=BF):
        return pltpu.VMEM(shape, t)

    kept = [
        S((tokens, width), BF), S((4, width, tokens), BF), S((width, etokens), BF),
        S((width, tokens), BF), S((ff, tokens), BF), S((2, tokens, ff), BF), S((tokens, width), F32), S((tokens, width), F32),
        S((3, tokens, width), BF), S((tokens, width), BF), S((2, etokens, width), BF),
        S((count * pairs, 2 * length, length), BF), S((count * pairs, 2 * length, keys), BF),
        S((1, width), F32), S((3, 1, width), F32),
    ]
    vm, hbm = pl.BlockSpec(memory_space=pltpu.VMEM), pl.BlockSpec(memory_space=pl.ANY)
    return pl.pallas_call(
        functools.partial(forward_kernel, n, (length, keys)),
        name="gather_forward",
        out_shape=(S((8, width, width), BF),) + tuple(kept),
        in_specs=[hbm] * 11 + [vm] * 10,
        out_specs=[hbm] * 16,
        scratch_shapes=[v(*a.shape, t=a.dtype) for a in kept] + [
            v(8, width, width), v(2, width, ff), v(ff, width), v(n, 8, 128, t=F32), v(table.shape[0], length, t=F32),
            v(pairs, 2 * length, length, t=F32), v(count, length, length, t=F32), v(count, length, keys, t=F32),
            v(tokens, width), v(tokens, ff), v(tokens, width, t=F32), v(tokens, width, t=F32), v(tokens, width),
        ] + gather_sems(hops, 6, 3) + gather_sems(hops, 2, 1) + [pltpu.SemaphoreType.DMA((11,)), pltpu.SemaphoreType.DMA((16,))],
        compiler_params=pltpu.CompilerParams(collective_id=0, has_side_effects=True, vmem_limit_bytes=67043328),
    )(*weights, *own_gains, x, enc, cot, drow, erow, buckets, table)


class Group:
    def __init__(self, left, right, size, refs):
        self.left, self.right = left, right
        self.count, self.rows, self.half, self.share = size
        self.ss, self.sr, self.ys, self.yr, self.rs, self.rr, self.own, self.got = refs

    def part(self, i, dev, start, width):
        return dot(self.left(i, dev), self.right(i, pl.ds(pl.multiple_of(start, 128), width)))


def group_shapes(size, slots):
    count, rows, half, share = size
    sib_slots, y_slots, ring_slots = slots

    def v(*shape):
        return pltpu.VMEM(shape, BF)
    crossing = [v(2, 2, count, rows, share), v(y_slots, 2, count, rows, share)] if share else [v(16, 128), v(16, 128)]
    return [v(2, 2, count, rows, half), v(sib_slots, 2, count, rows, half)] + crossing + [
        v(2, 2, count, rows, half - share), v(ring_slots, 2, count, rows, half - share)]


def reduce_sems(groups, slots):
    dma = pltpu.SemaphoreType.DMA
    sib_slots, y_slots, ring_slots = slots
    return [dma((2, 2, groups)), dma((sib_slots, 2, groups)), dma((2, 2, groups)), dma((y_slots, 2, groups)),
            dma((2, 2, groups)), dma((ring_slots, 2, groups)), dma((2, 2 * groups)), dma((2, 2 * groups)),
            pltpu.SemaphoreType.REGULAR((3, 2))]


class Reduce:
    def __init__(self, geo, groups, slots, sems):
        self.chips, self.me, self.rep, self.core, self.ring, self.device_at = geo
        self.groups = groups
        self.shared = groups[0].share > 0
        self.slots = slots
        self.sib_s, self.sib_r, self.y_s, self.y_r, self.ring_s, self.ring_r, self.fin_s, self.fin_r, self.free = sems
        self.other = 1 - self.rep
        self.sibling = (self.me + 1 - 2 * self.core, self.rep)
        self.opposite = (self.me, self.other)
        self.after = ((self.device_at(self.ring + 1), self.rep), (self.device_at(self.ring - 1), self.rep))

    def block(self, t, way, core):
        return self.device_at(self.ring + (2 * way - 1) * (1 + t)) + core - self.core

    def toward(self, way):
        return (self.after[0][0] + way * (self.after[1][0] - self.after[0][0]), self.rep)

    def behind(self, way):
        return (self.after[1][0] + way * (self.after[0][0] - self.after[1][0]), self.rep)

    def sib_copies(self, t, way):
        s, r = lax.rem(t, 2), lax.rem(t, self.slots[0])
        return [rdma(g.ss.at[s, way], g.sr.at[r, way], self.sib_s.at[s, way, i], self.sib_r.at[r, way, i], self.sibling)
                for i, g in enumerate(self.groups)]

    def y_copies(self, t, way):
        s, r = lax.rem(t, 2), lax.rem(t, self.slots[1])
        return [rdma(g.ys.at[s, way], g.yr.at[r, way], self.y_s.at[s, way, i], self.y_r.at[r, way, i], self.opposite)
                for i, g in enumerate(self.groups)]

    def ring_copies(self, t, way):
        s, r = lax.rem(t, 2), lax.rem(t + 1, self.slots[2])
        return [rdma(g.rs.at[s, way], g.rr.at[r, way], self.ring_s.at[s, way, i], self.ring_r.at[r, way, i], self.toward(way))
                for i, g in enumerate(self.groups)]

    def claim(self, kind, step, way):
        if self.slots[kind] < self.chips:
            @pl.when(step >= self.slots[kind])
            def _():
                pl.semaphore_wait(self.free.at[kind, way], 1)

    def release(self, kind, step, way, dev):
        if self.slots[kind] < self.chips:
            @pl.when(step + self.slots[kind] < self.chips)
            def _():
                pl.semaphore_signal(self.free.at[kind, way], inc=1, device_id=dev, device_id_type=MESH)

    def settle(self, t, copies):
        @pl.when(t >= 2)
        def _():
            for c in copies:
                c.wait_send()

    def to_sibling(self, t):
        s = lax.rem(t, 2)

        def go(way):
            dev = self.block(t, way, 1 - self.core)
            self.settle(t, self.sib_copies(t, way))
            for g in self.groups:
                for i in range(g.count):
                    g.ss[s, way, i] = g.part(i, dev, way * g.half, g.half).astype(BF)
            self.claim(0, t, way)
            for c in self.sib_copies(t, way):
                c.start()
        each(2, go)

    def to_across(self, t):
        s, r = lax.rem(t, 2), lax.rem(t, self.slots[0])

        def go(way):
            dev = self.block(t, way, self.core)
            self.settle(t, self.y_copies(t, way))
            for c in self.sib_copies(t, way):
                c.wait_recv()
            for g in self.groups:
                at = pl.multiple_of(self.other * g.share, 128)
                for i in range(g.count):
                    v = g.part(i, dev, way * g.half + at, g.share)
                    g.ys[s, way, i] = (v + g.sr[r, way, i, :, pl.ds(at, g.share)].astype(F32)).astype(BF)
            self.claim(1, t, way)
            for c in self.y_copies(t, way):
                c.start()
        each(2, go)

    def to_ring(self, t, at_once):
        s, b, y, r = lax.rem(t, 2), lax.rem(t, self.slots[0]), lax.rem(t, self.slots[1]), lax.rem(t, self.slots[2])

        for k, g in enumerate(self.groups):
            def go(way, k=k, g=g):
                dev = self.block(t, way, self.core)
                if not self.shared:
                    self.sib_copies(t, way)[k].wait_recv()
                lo, wide = 2 * g.share, g.half - 2 * g.share
                at = pl.multiple_of(self.rep * g.share, 128)
                common, apart = [], []
                for i in range(g.count):
                    if self.shared:
                        v = g.part(i, dev, way * g.half + at, g.share)
                        common.append(v + g.sr[b, way, i, :, pl.ds(at, g.share)].astype(F32))
                    v = g.part(i, dev, way * g.half + lo, wide)
                    apart.append(v + g.sr[b, way, i, :, lo:].astype(F32))
                self.settle(t, self.ring_copies(t, way)[k:k + 1])
                if self.shared:
                    self.y_copies(t, way)[k].wait_recv()

                @pl.when(t >= 1)
                def _():
                    self.ring_copies(t - 1, way)[k].wait_recv()
                for i in range(g.count):
                    if self.shared:
                        v = common[i] + g.yr[y, way, i].astype(F32) + g.rr[r, way, i, :, :g.share].astype(F32)
                        g.rs[s, way, i, :, :g.share] = v.astype(BF)
                    g.rs[s, way, i, :, g.share:] = (apart[i] + g.rr[r, way, i, :, g.share:].astype(F32)).astype(BF)

                @pl.when(t < self.chips - 1)
                def _():
                    if k == 0:
                        self.claim(2, t + 1, way)
                    self.ring_copies(t, way)[k].start()

                @pl.when(t == self.chips - 1)
                def _():
                    if at_once:
                        self.send_final(way, k)
                    last = (self.chips - 1) % 2
                    if self.shared:
                        cols = pl.ds(pl.multiple_of(way * g.half + self.rep * g.share, 128), g.share)
                        g.own[:, :, cols] = g.rs[last, way, :, :, :g.share]
                    rest = pl.ds(pl.multiple_of(way * g.half + lo, 128), wide)
                    g.own[:, :, rest] = g.rs[last, way, :, :, g.share:]
                if k == len(self.groups) - 1:
                    self.release(0, t, way, self.sibling)
                    if self.shared:
                        self.release(1, t, way, self.opposite)
                    self.release(2, t, way, self.behind(way))
            each(2, go)

    def send_final(self, way, k):
        for c in self.final_copies(way, k):
            c.start()

    def final_copies(self, way, k):
        g = self.groups[k]
        mine = g.rs.at[(self.chips - 1) % 2, way]
        cols = pl.ds(pl.multiple_of(way * g.half + self.rep * g.share, 128), g.share) if g.share else None
        wide = g.half - 2 * g.share
        there = pl.ds(pl.multiple_of(way * wide, 128), wide)
        found = [rdma(mine.at[:, :, pl.ds(g.share, wide)], g.got.at[:, :, there],
                      self.fin_s.at[way, 2 * k + 1], self.fin_r.at[way, 2 * k + 1], self.opposite)]
        if self.shared:
            found.append(rdma(mine.at[:, :, pl.ds(0, g.share)], g.own.at[:, :, cols],
                              self.fin_s.at[way, 2 * k], self.fin_r.at[way, 2 * k], self.opposite))
        return found

    def finish(self):
        def go(way):
            for k, g in enumerate(self.groups):
                wide = g.half - 2 * g.share
                if self.shared:
                    ref = g.own.at[:, :, pl.ds(pl.multiple_of(way * g.half + self.other * g.share, 128), g.share)]
                    rdma(ref, ref, self.fin_s.at[way, 2 * k], self.fin_r.at[way, 2 * k], self.opposite).wait_recv()
                ref = g.got.at[:, :, pl.ds(pl.multiple_of(way * wide, 128), wide)]
                rdma(ref, ref, self.fin_s.at[way, 2 * k + 1], self.fin_r.at[way, 2 * k + 1], self.opposite).wait_recv()
                for c in self.final_copies(way, k):
                    c.wait_send()
            for t in (self.chips - 2, self.chips - 1):
                for c in self.sib_copies(t, way) + (self.y_copies(t, way) if self.shared else []):
                    c.wait_send()
            for c in self.ring_copies(self.chips - 2, way):
                c.wait_send()
        each(2, go)

    def at(self, t, f, *more):
        @pl.when((t >= 0) & (t < self.chips))
        def _():
            f(t, *more)


class Butterfly:
    def __init__(self, geo, n, buf, got, sems):
        _, self.me, self.rep, _, _, _ = geo
        self.stages = n.bit_length() - 1
        self.buf, self.got = buf, got
        self.send, self.recv = sems

    def partner(self, bit):
        return (self.me + bit - 2 * bit * lax.rem(lax.div(self.me, bit), 2), self.rep)

    def copy(self, j, dev):
        return rdma(self.buf.at[j], self.got.at[j], self.send.at[j], self.recv.at[j], dev)

    def begin(self):
        self.copy(0, (self.me, 1 - self.rep)).start()

    def stage(self, j, bit):
        self.copy(j - 1, self.partner(bit)).wait_recv()
        self.buf[j] = self.buf[j - 1] + self.got[j - 1]
        self.copy(j, self.partner(bit)).start()

    def end(self, dst):
        self.copy(self.stages, self.partner(1)).wait_recv()
        dst[...] = self.buf[self.stages] + self.got[self.stages]
        for j in range(self.stages + 1):
            self.copy(j, self.partner(1)).wait_send()


OFFSETS = (0, 0, 0, 5, 8)
FINALS = (0, 1, 2, 0, 0)
CHAINS = ((2,), (3,), (4,), (0, 5), (1, 6))
SLOTS = (3, 3, 3)
FIRST_PIECE = 0


def backward_kernel(n, sizes, dims, *refs):
    length, keys = dims
    ins, w_hbm, refs = refs[:16], refs[16], refs[17:]
    kept, (small_o,), refs = refs[:16], refs[16:17], refs[17:]
    done, refs = refs[:16], refs[16:]
    outs, (dtok, denc) = done[:14], done[14:]
    held, refs = refs[:16], refs[16:]
    hfft, hidt, dgu, cot, r1, cq, ckv, p2, x1, gains, qkv, p1, x, xt, enct, gain3 = held
    bufs, refs = refs[:42], refs[42:]
    sems, refs = [refs[9 * k:9 * k + 9] for k in range(5)], refs[45:]
    sm, sm_got, sm_s, sm_r, load_s, w, w_s, dy, dye, dh, r0, do, gain12, diag, store_s = refs
    geo = geometry(n)
    chips, me, rep, core, ring, device_at = geo
    rows, rows_d = sizes[0][1], sizes[4][1]

    loads = [pltpu.make_async_copy(a, b, load_s.at[i]) for i, (a, b) in enumerate(zip(ins, held))]
    for c in loads[:4]:
        c.start()

    def stored(i):
        return pltpu.make_async_copy(done[i], kept[i], store_s.at[i])

    def fetch(i, slot):
        return pltpu.make_async_copy(w_hbm.at[i], w.at[slot], w_s.at[slot])

    def block(dev, size):
        return pl.ds(pl.multiple_of(dev * size, size), size)
    lefts = [lambda i, dev: xt[(3, 2)[i], block(dev, rows), :], lambda i, dev: xt[(1, 0)[i], block(dev, rows), :],
             lambda i, dev: hfft[block(dev, rows), :], lambda i, dev: hfft[block(dev, rows), :],
             lambda i, dev: hidt[block(dev, rows_d), :], lambda i, dev: enct[block(dev, rows), :], lambda i, dev: xt[0, block(dev, rows), :]]
    rights = [lambda i, c: dy[i, :, c], lambda i, c: dy[2 + i, :, c], lambda i, c: dgu[0, :, c], lambda i, c: dgu[1, :, c],
              lambda i, c: cot[:, c], lambda i, c: dye[i, :, c], lambda i, c: dy[4 + i, :, c]]
    groups = [Group(lefts[k], rights[k], sizes[k], bufs[6 * k:6 * k + 6] + outs[2 * k:2 * k + 2]) for k in range(7)]
    chains = [Reduce(geo, [groups[k] for k in c], SLOTS, s) for c, s in zip(CHAINS, sems)]
    tree = Butterfly(geo, n, sm, sm_got, (sm_s, sm_r))
    lead = chains[0]

    barrier = pltpu.get_barrier_semaphore()
    greet = [lead.after[0], lead.after[1], lead.sibling, lead.opposite] + [tree.partner(1 << j) for j in range(tree.stages)]
    for dev in greet:
        pl.semaphore_signal(barrier, inc=1, device_id=dev, device_id_type=MESH)
    for g in groups:
        g.rr[0] = jnp.zeros(g.rr.shape[1:], BF)
    diag[...] = jnp.zeros(diag.shape, F32)
    for c in loads[:4]:
        c.wait()
    for c in loads[4:]:
        c.start()
    for i, slot in ((5, 0), (6, 1), (7, 2), (4, 3)):
        fetch(i, slot).start()
    pl.semaphore_wait(barrier, len(greet))

    total = p1.shape[0]
    width = dh.shape[1]

    def start_back():
        for c in loads[4:]:
            c.wait()
        dy[0] = r1[...].astype(BF)
        fetch(5, 0).wait()
        project_t([(dy.at[0], w.at[0])], do, kind=BF)
        fetch(3, 0).start()

    def cross(begin, end):
        def f():
            lax.fori_loop(begin, end, lambda i, c: (attend_back(
                i, cq, ckv.at[0], ckv.at[1], p2, do, dy.at[1], dye.at[0], dye.at[1], None, length, keys), c)[1], 0)
        return f

    def own(begin, end):
        def f():
            lax.fori_loop(begin, end, lambda i, c: (attend_back(
                i, qkv.at[0], qkv.at[1], qkv.at[2], p1, do, dy.at[3], dy.at[4], dy.at[5], diag, length, length), c)[1], 0)
        return f

    def encoder(begin, end, last):
        def f():
            if not last:
                fetch(6, 1).wait()
                fetch(7, 2).wait()
            project_t([(dye.at[0], w.at[1]), (dye.at[1], w.at[2])], denc, begin=begin, end=end)
            if last:
                stored(15).start()
                fetch(0, 1).start()
                fetch(1, 2).start()
        return f

    def cross_norm():
        norm_back(x1, gains.at[1], dh, r1, r0, gain12.at[1])
        dy[2] = r0[...].astype(BF)

    def cross_query():
        fetch(4, 3).wait()
        project_t([(dy.at[1], w.at[3])], dh)
        fetch(2, 3).start()

    def own_out():
        fetch(3, 0).wait()
        project_t([(dy.at[2], w.at[0])], do, kind=BF)

    def own_in(begin, end, last):
        def f():
            if not last:
                for i, slot in ((0, 1), (1, 2), (2, 3)):
                    fetch(i, slot).wait()
            project_t([(dy.at[3], w.at[1]), (dy.at[4], w.at[2]), (dy.at[5], w.at[3])], dh, begin=begin, end=end)
        return f

    def own_norm():
        norm_back(x, gains.at[0], dh, r0, dtok, gain12.at[0])
        stored(14).start()
        for k in range(width // 128):
            for i, g in enumerate((gain12.at[0], gain12.at[1], gain3)):
                sm[0, pl.ds(i * (width // 128) + k, 1), :] = g[:, k * 128:(k + 1) * 128]
        for i in range(diag.shape[0]):
            sm[0, pl.ds(3 * (width // 128) + i, 1), :] = diag[i]

    tiles = width // TILE
    pieces = [start_back]
    pieces += [cross(total * k // 8, total * (k + 1) // 8) for k in range(8)]
    pieces += [cross_query, cross_norm, own_out]
    pieces += [own(total * k // 5, total * (k + 1) // 5) for k in range(5)]
    pieces += [encoder(0, tiles // 2, False), encoder(tiles // 2, tiles, True)]
    pieces += [own_in(0, tiles // 2, False), own_in(tiles // 2, tiles, True), own_norm]
    tree_at = 7

    def piece(u, which):
        for i in range(which, len(pieces), 3):
            pl.when(u == i // 3 + FIRST_PIECE)(pieces[i])

    def step(v, bit):
        u = v - 3
        for k, c in enumerate(chains):
            t = u - OFFSETS[k]
            c.at(t, c.to_ring, FINALS[k] == 0)
            if k < 3:
                piece(u, k)
            if FINALS[k]:
                for way in range(2):
                    for j in range(len(c.groups)):
                        pl.when(t == chips - 1 + FINALS[k] + way)(functools.partial(c.send_final, way, j))
        for k, c in enumerate(chains):
            if c.shared:
                c.at(u - OFFSETS[k] + 2, c.to_across)
        for k, c in enumerate(chains):
            c.at(u - OFFSETS[k] + 3, c.to_sibling)
        pl.when(u == tree_at)(tree.begin)
        inside = (u > tree_at) & (u <= tree_at + tree.stages)

        @pl.when(inside)
        def _():
            tree.stage(u - tree_at, bit)
        return jnp.where(inside, bit * 2, bit)

    lax.fori_loop(0, OFFSETS[-1] + chips + 3, step, jnp.int32(1))
    tree.end(small_o)
    for k, c in enumerate(chains):
        c.finish()
        for g in CHAINS[k]:
            stored(2 * g).start()
            stored(2 * g + 1).start()
    for i in range(16):
        stored(i).wait()


def shares(half, part):
    return half * part // 1408 * 128


def backward(n, w, hfft, hidt, dgu, cot, r1, cq, ckv, p2, x1, gains, qkv, p1, x, xt, enct, gain3):
    chips = n // 2
    tokens, width = x.shape
    etokens, ff = enct.shape[1], dgu.shape[2]
    length, keys = p1.shape[2], p2.shape[2]
    rows, rows_d = width // n, hidt.shape[0] // n
    half, half_g = width // 2, ff // 2
    part = shares(half, 3)
    sizes = [(2, rows, half, part), (2, rows, half, part), (1, rows, half_g, shares(half_g, 3)),
             (1, rows, half_g, shares(half_g, 3)), (1, rows_d, half, part), (2, rows, half, part), (2, rows, half, part)]
    stages = n.bit_length() - 1
    dma = pltpu.SemaphoreType.DMA
    S = jax.ShapeDtypeStruct
    vm, hbm = pl.BlockSpec(memory_space=pltpu.VMEM), pl.BlockSpec(memory_space=pl.ANY)
    outs = []
    for count, r, h, share in sizes:
        outs += [S((count, r, 2 * h), BF), S((count, r, 2 * (h - 2 * share)), BF)]
    outs += [S((tokens, width), F32), S((etokens, width), F32)]
    small = (3 * (width // 128) + width // 64, 128)
    ins = (hfft, hidt, dgu, cot, r1, cq, ckv, p2, x1, gains, qkv, p1, x, xt, enct, gain3)
    slots = tuple(min(s, chips) for s in SLOTS)
    return pl.pallas_call(
        functools.partial(backward_kernel, n, sizes, (length, keys)),
        name="backward_reduce",
        out_shape=tuple(outs) + (S(small, F32),),
        in_specs=[hbm] * 17,
        out_specs=[hbm] * 16 + [vm],
        scratch_shapes=[pltpu.VMEM(a.shape, a.dtype) for a in outs] + [pltpu.VMEM(a.shape, a.dtype) for a in ins]
        + [b for size in sizes for b in group_shapes(size, slots)]
        + [s for c in CHAINS for s in reduce_sems(len(c), slots)]
        + [pltpu.VMEM((stages + 1,) + small, F32)] * 2 + [dma((stages + 1,))] * 2
        + [dma((16,)), pltpu.VMEM((4, width, width), BF), dma((4,)), pltpu.VMEM((6, tokens, width), BF),
           pltpu.VMEM((2, etokens, width), BF), pltpu.VMEM((tokens, width), F32), pltpu.VMEM((tokens, width), F32),
           pltpu.VMEM((tokens, width), BF), pltpu.VMEM((2, 1, width), F32), pltpu.VMEM((width // 64, 1, 128), F32),
           dma((16,))],
        compiler_params=pltpu.CompilerParams(collective_id=1, has_side_effects=True, vmem_limit_bytes=67043328),
    )(*ins, w)


def finish_kernel(sizes, passed, buckets_count, *refs):
    parts, mats = 2 * len(sizes), sum(s[0] for s in sizes)
    ins, (small, buckets), refs = refs[:parts + passed], refs[parts + passed:parts + passed + 2], refs[parts + passed + 2:]
    outs, (dtable, gain1, gain2, gain3), refs = refs[:mats + passed], refs[mats + passed:mats + passed + 4], refs[mats + passed + 4:]
    held, done, (load_s, store_s) = refs[:parts + passed], refs[parts + passed:-2], refs[-2:]
    loads = [pltpu.make_async_copy(a, b, load_s.at[i]) for i, (a, b) in enumerate(zip(ins, held))]
    stores = [pltpu.make_async_copy(a, b, store_s.at[i]) for i, (a, b) in enumerate(zip(done + held[parts:], outs))]
    for c in loads:
        c.start()
    at = 0
    for k, (count, rows, half, share) in enumerate(sizes):
        own, got = held[2 * k], held[2 * k + 1]
        loads[2 * k].wait()
        loads[2 * k + 1].wait()
        wide = half - 2 * share
        for i in range(count):
            for way in range(2):
                lo = way * half
                if share:
                    done[at][:, lo:lo + 2 * share] = own[i, :, lo:lo + 2 * share].astype(F32)
                v = own[i, :, lo + 2 * share:lo + half].astype(F32) + got[i, :, way * wide:(way + 1) * wide].astype(F32)
                done[at][:, lo + 2 * share:lo + half] = v
            stores[at].start()
            at += 1
    for i in range(passed):
        loads[parts + i].wait()
        stores[mats + i].start()
    me = lax.axis_index("shard")
    rows = gain1.shape[1]
    per = 128 // rows
    heads = dtable.shape[0]
    tiles = (small.shape[0] - heads) // 3
    tile = lax.broadcasted_iota(jnp.int32, (tiles, 128), 0)
    for i, dst in enumerate((gain1, gain2, gain3)):
        v = jnp.where(tile == lax.div(me, per), small[i * tiles:(i + 1) * tiles, :], 0.0)
        v = pltpu.roll(v, lax.rem(128 - lax.rem(me, per) * rows, 128), 1)
        dst[...] = jnp.sum(v, axis=0, keepdims=True)[:, :rows]
    dtable[...] = lax.dot_general(small[3 * tiles:, :], bucket_rows(buckets, buckets_count), (((1,), (1,)), ((), ())),
                                  precision=lax.Precision.HIGHEST, preferred_element_type=F32)
    for c in stores:
        c.wait()


def finish(parts, passed, small, buckets, shape, rows):
    sizes, outs = [], []
    S = jax.ShapeDtypeStruct
    for own, got in zip(parts[0::2], parts[1::2]):
        count, r, width = own.shape
        half = width // 2
        sizes.append((count, r, half, (half - got.shape[2] // 2) // 2))
        outs += [S((r, width), F32)] * count
    vm, hbm = pl.BlockSpec(memory_space=pltpu.VMEM), pl.BlockSpec(memory_space=pl.ANY)
    ins = list(parts) + list(passed)
    dma = pltpu.SemaphoreType.DMA
    return pl.pallas_call(
        functools.partial(finish_kernel, sizes, len(passed), shape[1]),
        name="finish",
        out_shape=tuple(outs) + tuple(S(a.shape, a.dtype) for a in passed) + (S(shape, F32),) + (S((1, rows), F32),) * 3,
        in_specs=[hbm] * len(ins) + [vm] * 2,
        out_specs=[hbm] * (len(outs) + len(passed)) + [vm] * 4,
        scratch_shapes=[pltpu.VMEM(a.shape, a.dtype) for a in ins] + [pltpu.VMEM(a.shape, a.dtype) for a in outs]
        + [dma((len(ins),)), dma((len(outs) + len(passed),))],
        compiler_params=pltpu.CompilerParams(vmem_limit_bytes=67043328),
    )(*ins, small, buckets)


def body(hidden_in, encoded, dec_segments, enc_segments, buckets, out_cot, norm_self, self_query, self_key, self_value,
         self_out, table, norm_cross, cross_query, cross_key, cross_value, cross_out, norm_ff, ff_gate, ff_up, ff_down, *, n):
    micro, per, length, width = hidden_in.shape
    keys = encoded.shape[2]
    count = micro * per
    rows, rows_d, ff = self_query.shape[0], ff_down.shape[0], ff_gate.shape[1]
    spare = -rows_d % 16
    if spare:
        ff_down = jnp.pad(ff_down, ((0, spare), (0, 0)))
        ff_gate, ff_up = [jnp.pad(w.reshape(rows, n, rows_d), ((0, 0), (0, 0), (0, spare))).reshape(rows, -1) for w in (ff_gate, ff_up)]
    x = hidden_in.reshape(count * length, width)
    enc = encoded.reshape(count * keys, width)
    cot = out_cot.reshape(count * length, width)
    buckets = buckets.reshape(1, length)
    weights = (self_query, self_key, self_value, self_out, cross_query, cross_out, cross_key, cross_value, ff_gate, ff_up, ff_down)
    own_gains = [g.reshape(1, rows) for g in (norm_self, norm_cross, norm_ff)]
    w, out, xt, enct, hfft, hidt, dgu, r1, x1, qkv, cq, ckv, p1, p2, gain3, gains = forward(
        n, weights, own_gains, x, enc, cot, dec_segments.reshape(count, 1, length), enc_segments.reshape(count, 1, keys), buckets, table.T)
    *parts, dtok, denc, small = backward(n, w, hfft, hidt, dgu, cot, r1, cq, ckv, p2, x1, gains, qkv, p1, x, xt, enct, gain3)
    gco, gcq, gso, gq, gg, gup, gd, gck, gcv, gk, gv, out, dtok, denc, dtable, g1, g2, g3 = finish(
        parts, (out, dtok, denc), small, buckets, table.T.shape, rows)
    if spare:
        gd = gd[:rows_d]
        gg, gup = [g.reshape(rows, n, -1)[:, :, :rows_d].reshape(rows, ff) for g in (gg, gup)]
    return (
        out.reshape(hidden_in.shape), dtok.reshape(hidden_in.shape), denc.reshape(encoded.shape),
        g1.reshape(rows), gq, gk, gv, gso, dtable.T, g2.reshape(rows), gcq, gck, gcv, gco, g3.reshape(rows), gg, gup, gd,
    )


def solution(mesh):
    tok = P(None, ("shard", "rep"), None, None)
    seg = P(None, ("shard", "rep"), None)
    vec, mat, rep = P("shard"), P("shard", None), P()
    return jax.shard_map(
        functools.partial(body, n=mesh.shape["shard"]),
        mesh=mesh,
        in_specs=(tok, tok, seg, seg, rep, tok, vec, mat, mat, mat, mat, rep, vec, mat, mat, mat, mat, vec, mat, mat, mat),
        out_specs=(tok, tok, tok, vec, mat, mat, mat, mat, rep, vec, mat, mat, mat, mat, vec, mat, mat, mat),
        check_vma=False,
    )
```

```python
import functools
import math

import jax
import jax.numpy as jnp
from jax import lax
from jax.experimental import pallas as pl
from jax.experimental.pallas import tpu as pltpu
from jax.sharding import PartitionSpec as P

MESH = pl.DeviceIdType.MESH
BF = jnp.bfloat16
F32 = jnp.float32
EPS = 1e-06
NEG = -1e30
C1 = math.sqrt(2.0 / math.pi)
C2 = 0.044715
TILE = 256


def each(count, f):
    def step(i, carry):
        f(i)
        return carry
    lax.fori_loop(0, count, step, 0)


def tile_at(i, size=TILE):
    return pl.ds(pl.multiple_of(i * size, size), size)


def dot(a, b):
    return jnp.dot(a, b, preferred_element_type=F32)


def dot_t(a, b):
    return lax.dot_general(a, b, (((1,), (1,)), ((), ())), preferred_element_type=F32)


def dot_rows(a, b):
    return lax.dot_general(a, b, (((0,), (0,)), ((), ())), preferred_element_type=F32)


def normed(src, gain, dst):
    def rows(i):
        r = tile_at(i, 32)
        v = src[r, :].astype(F32)
        t = lax.rsqrt(jnp.mean(v * v, axis=-1, keepdims=True) + EPS)
        dst[r, :] = (v * t * gain[...]).astype(BF)
    each(src.shape[0] // 32, rows)


def norm_back(src, gain, grad, base, dst, gain_sum):
    gain_sum[...] = jnp.zeros(gain_sum.shape, F32)

    def rows(i):
        r = tile_at(i, 16)
        v = src[r, :].astype(F32)
        dy = grad[r, :]
        g = gain[...]
        t = lax.rsqrt(jnp.mean(v * v, axis=-1, keepdims=True) + EPS)
        vt = v * t
        gdy = g * dy
        inner = jnp.mean(vt * gdy, axis=-1, keepdims=True)
        dst[r, :] = base[r, :].astype(F32) + t * (gdy - vt * inner)
        gain_sum[...] += jnp.sum(vt * dy, axis=0, keepdims=True)
    each(src.shape[0] // 16, rows)


def turn(src, dst):
    for b in range(src.shape[0] // 128):
        def block(c, b=b):
            dst[tile_at(c), b * 128:(b + 1) * 128] = src[b * 128:(b + 1) * 128, tile_at(c)].T
        each(src.shape[1] // TILE, block)


def head_masks():
    lane = lax.broadcasted_iota(jnp.int32, (1, 128), 1)
    even = (lane < 64).astype(F32).astype(BF)
    return even, (lane >= 64).astype(F32).astype(BF)


def pair_rows(x, masks):
    return jnp.concatenate([x * masks[0], x * masks[1]], axis=0)


def side_by_side(x):
    half = x.shape[0] // 2
    return jnp.concatenate([x[:half], x[half:]], axis=1)


def attend(i, q, k, v, p, o, neg, bias, length, keys):
    masks = head_masks()
    pairs = q.shape[1] // 128
    b, pair = lax.div(i, pairs), lax.rem(i, pairs)
    lanes = tile_at(pair, 128)
    rows, krows = tile_at(b, length), tile_at(b, keys)
    s = dot_t(pair_rows(q[rows, lanes], masks), k[krows, lanes])
    if bias is not None:
        s = s + bias[pair]
    n = neg[b]
    s = s + jnp.concatenate([n, n], axis=0)
    e = jnp.exp(s - jnp.max(s, axis=-1, keepdims=True))
    pb = (e * (1.0 / jnp.sum(e, axis=-1, keepdims=True))).astype(BF)
    p[i] = pb
    o[rows, lanes] = dot(side_by_side(pb), pair_rows(v[krows, lanes], masks)).astype(BF)


def attend_back(i, q, k, v, p, do, dq, dk, dv, diag, length, keys):
    masks = head_masks()
    pairs = q.shape[1] // 128
    b, pair = lax.div(i, pairs), lax.rem(i, pairs)
    lanes = tile_at(pair, 128)
    rows, krows = tile_at(b, length), tile_at(b, keys)
    dos = pair_rows(do[rows, lanes], masks)
    dp = dot_t(dos, v[krows, lanes])
    pb = p[i]
    pf = pb.astype(F32)
    ds = (pf * (dp - jnp.sum(pf * dp, axis=-1, keepdims=True))).astype(BF)
    dq[rows, lanes] = dot(side_by_side(ds), pair_rows(k[krows, lanes], masks)).astype(BF)
    dk[krows, lanes] = dot_rows(ds, pair_rows(q[rows, lanes], masks)).astype(BF)
    dv[krows, lanes] = dot_rows(pb, dos).astype(BF)
    if diag is not None:
        i0 = lax.broadcasted_iota(jnp.int32, (length, length), 0)
        i1 = lax.broadcasted_iota(jnp.int32, (length, length), 1)
        flip = (i0 + i1 == length - 1).astype(F32).astype(BF)
        for h in range(2):
            u = pltpu.roll(dot(flip, ds[h * length:(h + 1) * length]), 1, 1, stride=1, stride_axis=0)
            diag[2 * pair + h] += jnp.sum(u, axis=0, keepdims=True)


def position_bias(taps, bias, length):
    def pair(i):
        for h in range(2):
            w = jnp.broadcast_to(taps[pl.ds(2 * i + h, 1), :], (length, length))
            bias[i, h * length:(h + 1) * length, :] = pltpu.roll(w, 0, 1, stride=1, stride_axis=0)
    each(bias.shape[0], pair)


def seg_masks(drow, erow, neg_self, neg_cross, length):
    for b in range(drow.shape[0]):
        row = drow[b].astype(F32)
        col = jnp.broadcast_to(row, (length, length)).T
        i = lax.broadcasted_iota(jnp.int32, (length, length), 0)
        j = lax.broadcasted_iota(jnp.int32, (length, length), 1)
        neg_self[b] = jnp.where((j <= i) & (col == row), 0.0, NEG)
        enc = erow[b].astype(F32)
        for k in range(enc.shape[1] // length):
            part = slice(k * length, (k + 1) * length)
            neg_cross[b, :, part] = jnp.where(col == enc[:, part], 0.0, NEG)


def bucket_rows(buckets, count):
    length = buckets.shape[1]
    i = lax.broadcasted_iota(jnp.int32, (count, length), 0)
    hot = (i == buckets[...]).astype(F32).astype(BF)
    m = lax.broadcasted_iota(jnp.int32, (length, length), 0)
    l = lax.broadcasted_iota(jnp.int32, (length, length), 1)
    back = ((m + l == length) | ((m == 0) & (l == 0))).astype(F32).astype(BF)
    return dot(hot, back)


def project(a, w, dst, base=None, kind=BF):
    def tile(c):
        v = dot(a[...], w[:, tile_at(c)])
        if base is not None:
            v = v + base[:, tile_at(c)].astype(F32)
        dst[:, tile_at(c)] = v.astype(kind)
    each(dst.shape[1] // TILE, tile)


def project_t(terms, dst, kind=F32, begin=0, end=None):
    def tile(c):
        v = None
        for a, w in terms:
            u = dot_t(a[...], w[tile_at(c), :])
            v = u if v is None else v + u
        dst[:, tile_at(c)] = v.astype(kind)
    lax.fori_loop(begin, dst.shape[1] // TILE if end is None else end, lambda i, carry: (tile(i), carry)[1], 0)


def feed_tile(c, h, cot, wg, wu, wd, hid, dgate, dup):
    cols = tile_at(c)
    hv = h[...]
    gate = dot(hv, wg[:, cols])
    up = dot(hv, wu[:, cols])
    dhid = dot_t(cot[...], wd[cols, :])
    sq = gate * gate
    th = jnp.tanh(C1 * gate * (1.0 + C2 * sq))
    hp = 0.5 * (1.0 + th)
    act = gate * hp
    hid[:, cols] = (act * up).astype(BF)
    slope = hp + (0.5 * C1) * gate * (1.0 - th * th) * (1.0 + (3.0 * C2) * sq)
    dgate[:, cols] = (dhid * up * slope).astype(BF)
    dup[:, cols] = (dhid * act).astype(BF)


def geometry(n):
    chips = n // 2
    side = chips // 2
    s = lax.axis_index("shard")
    rep = lax.axis_index("rep")
    core = lax.rem(s, 2)
    chip = lax.div(s, 2)
    x = lax.rem(chip, 2)
    z = lax.div(chip, 2)
    ring = z + x * (chips - 1 - 2 * z)

    def device_at(position):
        p = lax.rem(position + 2 * chips, chips)
        px = lax.div(p, side)
        pz = p + px * (chips - 1 - 2 * p)
        return (pz * 2 + px) * 2 + core

    return chips, s, rep, core, ring, device_at


def rdma(src, dst, ss, rs, dev):
    return pltpu.make_async_remote_copy(src_ref=src, dst_ref=dst, send_sem=ss, recv_sem=rs, device_id=dev, device_id_type=MESH)


class Gather:
    def __init__(self, geo, pieces, across, sems):
        self.chips, self.me, self.rep, self.core, self.ring, self.device_at = geo
        self.hops = self.chips - 1
        self.pieces, self.across = pieces, across
        self.ring_s, self.ring_r, self.sib_s, self.sib_r, self.y_s, self.y_r, self.yy_s, self.yy_r, self.own_s, self.own_r = sems
        self.other = 1 - 2 * self.core
        self.sibling = (self.me + self.other, self.rep)
        self.opposite = (self.me, 1 - self.rep)
        self.ahead = ((self.device_at(self.ring + 1), self.rep), (self.device_at(self.ring - 1), self.rep))

    def source(self, way, t):
        return self.device_at(self.ring - 1 - t) if way == 0 else self.device_at(self.ring + 1 + t)

    def each(self, rep, count=None):
        most = max(len(self.pieces(0, rep)), len(self.pieces(1, rep)))
        for p in range(most if count is None else count):
            for way in range(2):
                ps = self.pieces(way, rep)
                if p < len(ps):
                    yield way, p, ps[p]

    def ring_copy(self, way, t, p, ref):
        return rdma(ref, ref, self.ring_s.at[way, t, p], self.ring_r.at[way, t, p], self.ahead[way])

    def sib_copy(self, way, t, p, ref):
        return rdma(ref, ref, self.sib_s.at[way, t, p], self.sib_r.at[way, t, p], self.sibling)

    def y_copy(self, way, t, p, ref):
        return rdma(ref, ref, self.y_s.at[way, t, p], self.y_r.at[way, t, p], self.opposite)

    def yy_copy(self, way, t, p, ref):
        return rdma(ref, ref, self.yy_s.at[way, t, p], self.yy_r.at[way, t, p], self.sibling)

    def own_copies(self, src):
        found = []
        for rep in (self.rep, 1 - self.rep):
            for way, p, ref in self.each(rep, None if rep is self.rep else self.across):
                i = 0 if rep is self.rep else 1
                r = ref(src)
                found.append(rdma(r, r, self.own_s.at[i, way, p], self.own_r.at[i, way, p], self.sibling))
        return found

    def start(self):
        for way, p, ref in self.each(self.rep):
            self.ring_copy(way, 0, p, ref(self.me)).start()
        for c in self.own_copies(self.me):
            c.start()

    def hop(self, t, last=False, which=None):
        for way, p, ref in self.each(self.rep):
            if which is not None and p != which:
                continue
            r = ref(self.source(way, t))
            self.ring_copy(way, t, p, r).wait_recv()
            if not last:
                self.ring_copy(way, t + 1, p, r).start()
            if p < self.across:
                self.y_copy(way, t, p, r).start()
            self.sib_copy(way, t, p, r).start()

    def relay(self, t):
        for way, p, ref in self.each(1 - self.rep, self.across):
            r = ref(self.source(way, t))
            self.y_copy(way, t, p, r).wait_recv()
            self.yy_copy(way, t, p, r).start()

    def complete(self):
        def step(t):
            for way, p, ref in self.each(self.rep):
                self.sib_copy(way, t, p, ref(self.source(way, t) + self.other)).wait_recv()
            for way, p, ref in self.each(1 - self.rep, self.across):
                self.yy_copy(way, t, p, ref(self.source(way, t) + self.other)).wait_recv()
        each(self.hops, step)
        for c in self.own_copies(self.me + self.other):
            c.wait_recv()

    def drain(self):
        def step(t):
            for way, p, ref in self.each(self.rep):
                r = ref(self.source(way, t))
                self.ring_copy(way, t, p, r).wait_send()
                self.sib_copy(way, t, p, r).wait_send()
                if p < self.across:
                    self.y_copy(way, t, p, r).wait_send()
            for way, p, ref in self.each(1 - self.rep, self.across):
                self.yy_copy(way, t, p, ref(self.source(way, t))).wait_send()
        each(self.hops, step)
        for c in self.own_copies(self.me):
            c.wait_send()


def gather_sems(hops, pieces, across):
    dma = pltpu.SemaphoreType.DMA
    return [dma((2, hops, pieces))] * 4 + [dma((2, hops, across))] * 4 + [dma((2, 2, pieces))] * 2


def forward_kernel(n, dims, *refs):
    length, keys = dims
    ins, refs = refs[:11], refs[11:]
    own_gains, refs = refs[:3], refs[3:]
    x, enc, cot, drow, erow, buckets, table = refs[:7]
    w_out, kept, refs = refs[7], refs[8:23], refs[23:]
    out, xt, enct, hfft, hidt, dgu, r1, x1, qkv, cq, ckv, p1, p2, gain3, gains = held = refs[:15]
    w, gu, dn, gn, taps, bias, neg_s, neg_c, h, hid, x2, dh, o = refs[15:28]
    first_sems, second_sems = refs[28:38], refs[38:48]
    load_s, store_s = refs[48:50]

    def stored(i):
        return pltpu.make_async_copy(held[i], kept[i], store_s.at[i])

    def store(*which):
        for i in which:
            stored(i).start()
    geo = geometry(n)
    chips, me, rep, core, ring, device_at = geo
    hops = chips - 1
    rows, rows_d = ins[0].shape[0], ins[10].shape[0]
    half, half_g = w.shape[2] // 2, gu.shape[2] // 2
    count = drow.shape[0]
    pairs = w.shape[2] // 128

    def block(src):
        return pl.ds(pl.multiple_of(src * rows, rows), rows)

    def block_d(src):
        return pl.ds(pl.multiple_of(src * rows_d, rows_d), rows_d)

    def attention_pieces(way, r):
        c = pl.ds(way * half, half)
        near, far = pl.ds(way * half, half // 2), pl.ds(way * half + half // 2, half // 2)
        found = [lambda s: w.at[r, block(s), c], lambda s: w.at[4 + r, block(s), c], lambda s: w.at[2 + r, block(s), near],
                 lambda s: w.at[pl.ds(2, 2), block(s), far], lambda s: w.at[pl.ds(6, 2), block(s), c]]
        return found + [lambda s: gn.at[s]] if way == 0 else found

    def feed_pieces(way, r):
        return [lambda s: gu.at[r, block(s), pl.ds(way * half_g, half_g)], lambda s: dn.at[block_d(s), pl.ds(way * half, half)]]

    first = Gather(geo, attention_pieces, 3, first_sems)
    second = Gather(geo, feed_pieces, 1, second_sems)

    width = w.shape[2]
    places = [w.at[i, block(me), :] for i in range(8)] + [gu.at[i, block(me), :] for i in range(2)] + [dn.at[block_d(me), :]]
    loads = [pltpu.make_async_copy(a, b, load_s.at[i]) for i, (a, b) in enumerate(zip(ins, places))]
    for c in loads:
        c.start()
    barrier = pltpu.get_barrier_semaphore()
    for dev in first.ahead + (first.sibling, first.opposite):
        pl.semaphore_signal(barrier, inc=1, device_id=dev, device_id_type=MESH)
    per = 128 // rows
    lane = lax.broadcasted_iota(jnp.int32, (rows, 128), 1)
    spot = lax.broadcasted_iota(jnp.int32, (rows, 128), 0)
    place = (lane == spot + lax.rem(me, per) * rows).astype(F32).astype(BF)
    gn[me] = jnp.concatenate([dot(g[...], place) for g in own_gains] + [jnp.zeros((5, 128), F32)], axis=0)
    for c in loads[:8]:
        c.wait()
    pl.semaphore_wait(barrier, 4)

    first.start()
    turn(enc, enct)
    store(2)
    first.hop(0)
    taps[...] = dot(table[...], bucket_rows(buckets, table.shape[1]).astype(BF))
    position_bias(taps, bias, length)
    seg_masks(drow, erow, neg_s, neg_c, length)

    def middle(t):
        first.hop(t)
        first.relay(t - 1)
    lax.fori_loop(1, hops - 1, lambda t, c: (middle(t), c)[1], 0)
    for c in loads[8:]:
        c.wait()
    second.start()
    first.hop(hops - 1, True)
    first.relay(hops - 2)
    first.relay(hops - 1)
    first.complete()
    weights_out = pltpu.make_async_copy(w, w_out, store_s.at[15])
    weights_out.start()
    for j in range(w.shape[2] // 128):
        v = gn[j * per]
        for i in range(1, per):
            v = v + gn[j * per + i]
        for i in range(3):
            gains[i, :, j * 128:(j + 1) * 128] = v[i:i + 1, :]
    store(14)

    def some(begin, end, f):
        lax.fori_loop(begin, end, lambda i, c: (f(i), c)[1], 0)

    def heads():
        normed(x, gains.at[0], h)
        project(h, w.at[0], qkv.at[0])

    def keys_values():
        for i in range(1, 3):
            project(h, w.at[i], qkv.at[i])

    def own(i):
        attend(i, qkv.at[0], qkv.at[1], qkv.at[2], p1, o, neg_s, bias, length, length)

    def own_result():
        store(8, 11)
        turn(h, xt.at[0])
        turn(o, xt.at[1])
        project(o, w.at[3], x1, base=x, kind=F32)

    def cross_heads():
        normed(x1, gains.at[1], h)
        project(h, w.at[4], cq)

    def cross_keys():
        store(7, 9)
        turn(h, xt.at[2])
        project(enc, w.at[6], ckv.at[0])

    def cross(i):
        attend(i, cq, ckv.at[0], ckv.at[1], p2, o, neg_c, None, length, keys)

    def before_feed():
        store(10, 12)
        turn(o, xt.at[3])
        store(1)
        project(o, w.at[5], x2, base=x1, kind=F32)
        normed(x2, gains.at[2], h)
        turn(h, hfft)
        store(3)

    total = count * pairs
    def quarters(f):
        return [functools.partial(some, total * k // 4, total * (k + 1) // 4, f) for k in range(4)]
    halves = [heads, keys_values] + quarters(own) + [own_result, cross_heads, cross_keys, lambda: project(enc, w.at[7], ckv.at[1])] + quarters(cross)
    chunks = list(zip(halves[0::2], halves[1::2]))
    for t in range(len(chunks)):
        chunks[t][0]()
        second.hop(t, t == hops - 1, 0)
        if t > 0:
            second.relay(t - 1)
        chunks[t][1]()
        second.hop(t, t == hops - 1, 1)
    if hops > len(chunks):
        def rest(t):
            second.hop(t)
            second.relay(t - 1)
        some(len(chunks), hops - 1, rest)
        second.hop(hops - 1, True)
        second.relay(hops - 2)
    before_feed()
    second.relay(hops - 1)
    second.complete()

    each(hid.shape[1] // TILE, lambda c: feed_tile(c, h, cot, gu.at[0], gu.at[1], dn, hid, dgu.at[0], dgu.at[1]))
    store(5)
    turn(hid, hidt)
    store(4)
    project_t([(dgu.at[0], gu.at[0]), (dgu.at[1], gu.at[1])], dh)
    norm_back(x2, gains.at[2], dh, cot, r1, gain3)
    store(6, 13)
    project(hid, dn, out, base=x2)
    store(0)
    first.drain()
    second.drain()
    weights_out.wait()
    for i in range(15):
        stored(i).wait()


def forward(n, weights, own_gains, x, enc, cot, drow, erow, buckets, table):
    hops = n // 2 - 1
    rows, width = weights[0].shape
    ff = weights[8].shape[1]
    tokens, etokens = x.shape[0], enc.shape[0]
    count, _, length = drow.shape
    keys = etokens // count
    pairs = width // 128
    S = jax.ShapeDtypeStruct

    def v(*shape, t=BF):
        return pltpu.VMEM(shape, t)

    kept = [
        S((tokens, width), BF), S((4, width, tokens), BF), S((width, etokens), BF),
        S((width, tokens), BF), S((ff, tokens), BF), S((2, tokens, ff), BF), S((tokens, width), F32), S((tokens, width), F32),
        S((3, tokens, width), BF), S((tokens, width), BF), S((2, etokens, width), BF),
        S((count * pairs, 2 * length, length), BF), S((count * pairs, 2 * length, keys), BF),
        S((1, width), F32), S((3, 1, width), F32),
    ]
    vm, hbm = pl.BlockSpec(memory_space=pltpu.VMEM), pl.BlockSpec(memory_space=pl.ANY)
    return pl.pallas_call(
        functools.partial(forward_kernel, n, (length, keys)),
        name="gather_forward",
        out_shape=(S((8, width, width), BF),) + tuple(kept),
        in_specs=[hbm] * 11 + [vm] * 10,
        out_specs=[hbm] * 16,
        scratch_shapes=[v(*a.shape, t=a.dtype) for a in kept] + [
            v(8, width, width), v(2, width, ff), v(ff, width), v(n, 8, 128, t=F32), v(table.shape[0], length, t=F32),
            v(pairs, 2 * length, length, t=F32), v(count, length, length, t=F32), v(count, length, keys, t=F32),
            v(tokens, width), v(tokens, ff), v(tokens, width, t=F32), v(tokens, width, t=F32), v(tokens, width),
        ] + gather_sems(hops, 6, 3) + gather_sems(hops, 2, 1) + [pltpu.SemaphoreType.DMA((11,)), pltpu.SemaphoreType.DMA((16,))],
        compiler_params=pltpu.CompilerParams(collective_id=0, has_side_effects=True, vmem_limit_bytes=67043328),
    )(*weights, *own_gains, x, enc, cot, drow, erow, buckets, table)


class Group:
    def __init__(self, left, right, size, refs):
        self.left, self.right = left, right
        self.count, self.rows, self.half, self.share = size
        self.ss, self.sr, self.ys, self.yr, self.rs, self.rr, self.own, self.got = refs

    def part(self, i, dev, start, width):
        return dot(self.left(i, dev), self.right(i, pl.ds(pl.multiple_of(start, 128), width)))


def group_shapes(size, slots):
    count, rows, half, share = size
    sib_slots, y_slots, ring_slots = slots

    def v(*shape):
        return pltpu.VMEM(shape, BF)
    crossing = [v(2, 2, count, rows, share), v(y_slots, 2, count, rows, share)] if share else [v(16, 128), v(16, 128)]
    return [v(2, 2, count, rows, half), v(sib_slots, 2, count, rows, half)] + crossing + [
        v(2, 2, count, rows, half - share), v(ring_slots, 2, count, rows, half - share)]


def reduce_sems(groups, slots):
    dma = pltpu.SemaphoreType.DMA
    sib_slots, y_slots, ring_slots = slots
    return [dma((2, 2, groups)), dma((sib_slots, 2, groups)), dma((2, 2, groups)), dma((y_slots, 2, groups)),
            dma((2, 2, groups)), dma((ring_slots, 2, groups)), dma((2, 2 * groups)), dma((2, 2 * groups)),
            pltpu.SemaphoreType.REGULAR((3, 2))]


class Reduce:
    def __init__(self, geo, groups, slots, sems):
        self.chips, self.me, self.rep, self.core, self.ring, self.device_at = geo
        self.groups = groups
        self.shared = groups[0].share > 0
        self.slots = slots
        self.sib_s, self.sib_r, self.y_s, self.y_r, self.ring_s, self.ring_r, self.fin_s, self.fin_r, self.free = sems
        self.other = 1 - self.rep
        self.sibling = (self.me + 1 - 2 * self.core, self.rep)
        self.opposite = (self.me, self.other)
        self.after = ((self.device_at(self.ring + 1), self.rep), (self.device_at(self.ring - 1), self.rep))

    def block(self, t, way, core):
        return self.device_at(self.ring + (2 * way - 1) * (1 + t)) + core - self.core

    def toward(self, way):
        return (self.after[0][0] + way * (self.after[1][0] - self.after[0][0]), self.rep)

    def behind(self, way):
        return (self.after[1][0] + way * (self.after[0][0] - self.after[1][0]), self.rep)

    def sib_copies(self, t, way):
        s, r = lax.rem(t, 2), lax.rem(t, self.slots[0])
        return [rdma(g.ss.at[s, way], g.sr.at[r, way], self.sib_s.at[s, way, i], self.sib_r.at[r, way, i], self.sibling)
                for i, g in enumerate(self.groups)]

    def y_copies(self, t, way):
        s, r = lax.rem(t, 2), lax.rem(t, self.slots[1])
        return [rdma(g.ys.at[s, way], g.yr.at[r, way], self.y_s.at[s, way, i], self.y_r.at[r, way, i], self.opposite)
                for i, g in enumerate(self.groups)]

    def ring_copies(self, t, way):
        s, r = lax.rem(t, 2), lax.rem(t + 1, self.slots[2])
        return [rdma(g.rs.at[s, way], g.rr.at[r, way], self.ring_s.at[s, way, i], self.ring_r.at[r, way, i], self.toward(way))
                for i, g in enumerate(self.groups)]

    def claim(self, kind, step, way):
        if self.slots[kind] < self.chips:
            @pl.when(step >= self.slots[kind])
            def _():
                pl.semaphore_wait(self.free.at[kind, way], 1)

    def release(self, kind, step, way, dev):
        if self.slots[kind] < self.chips:
            @pl.when(step + self.slots[kind] < self.chips)
            def _():
                pl.semaphore_signal(self.free.at[kind, way], inc=1, device_id=dev, device_id_type=MESH)

    def settle(self, t, copies):
        @pl.when(t >= 2)
        def _():
            for c in copies:
                c.wait_send()

    def to_sibling(self, t):
        s = lax.rem(t, 2)

        def go(way):
            dev = self.block(t, way, 1 - self.core)
            self.settle(t, self.sib_copies(t, way))
            for g in self.groups:
                for i in range(g.count):
                    g.ss[s, way, i] = g.part(i, dev, way * g.half, g.half).astype(BF)
            self.claim(0, t, way)
            for c in self.sib_copies(t, way):
                c.start()
        each(2, go)

    def to_across(self, t):
        s, r = lax.rem(t, 2), lax.rem(t, self.slots[0])

        def go(way):
            dev = self.block(t, way, self.core)
            self.settle(t, self.y_copies(t, way))
            for c in self.sib_copies(t, way):
                c.wait_recv()
            for g in self.groups:
                at = pl.multiple_of(self.other * g.share, 128)
                for i in range(g.count):
                    v = g.part(i, dev, way * g.half + at, g.share)
                    g.ys[s, way, i] = (v + g.sr[r, way, i, :, pl.ds(at, g.share)].astype(F32)).astype(BF)
            self.claim(1, t, way)
            for c in self.y_copies(t, way):
                c.start()
        each(2, go)

    def to_ring(self, t, at_once):
        s, b, y, r = lax.rem(t, 2), lax.rem(t, self.slots[0]), lax.rem(t, self.slots[1]), lax.rem(t, self.slots[2])

        for k, g in enumerate(self.groups):
            def go(way, k=k, g=g):
                dev = self.block(t, way, self.core)
                if not self.shared:
                    self.sib_copies(t, way)[k].wait_recv()
                lo, wide = 2 * g.share, g.half - 2 * g.share
                at = pl.multiple_of(self.rep * g.share, 128)
                common, apart = [], []
                for i in range(g.count):
                    if self.shared:
                        v = g.part(i, dev, way * g.half + at, g.share)
                        common.append(v + g.sr[b, way, i, :, pl.ds(at, g.share)].astype(F32))
                    v = g.part(i, dev, way * g.half + lo, wide)
                    apart.append(v + g.sr[b, way, i, :, lo:].astype(F32))
                self.settle(t, self.ring_copies(t, way)[k:k + 1])
                if self.shared:
                    self.y_copies(t, way)[k].wait_recv()

                @pl.when(t >= 1)
                def _():
                    self.ring_copies(t - 1, way)[k].wait_recv()
                for i in range(g.count):
                    if self.shared:
                        v = common[i] + g.yr[y, way, i].astype(F32) + g.rr[r, way, i, :, :g.share].astype(F32)
                        g.rs[s, way, i, :, :g.share] = v.astype(BF)
                    g.rs[s, way, i, :, g.share:] = (apart[i] + g.rr[r, way, i, :, g.share:].astype(F32)).astype(BF)

                @pl.when(t < self.chips - 1)
                def _():
                    if k == 0:
                        self.claim(2, t + 1, way)
                    self.ring_copies(t, way)[k].start()

                @pl.when(t == self.chips - 1)
                def _():
                    if at_once:
                        self.send_final(way, k)
                    last = (self.chips - 1) % 2
                    if self.shared:
                        cols = pl.ds(pl.multiple_of(way * g.half + self.rep * g.share, 128), g.share)
                        g.own[:, :, cols] = g.rs[last, way, :, :, :g.share]
                    rest = pl.ds(pl.multiple_of(way * g.half + lo, 128), wide)
                    g.own[:, :, rest] = g.rs[last, way, :, :, g.share:]
                if k == len(self.groups) - 1:
                    self.release(0, t, way, self.sibling)
                    if self.shared:
                        self.release(1, t, way, self.opposite)
                    self.release(2, t, way, self.behind(way))
            each(2, go)

    def send_final(self, way, k):
        for c in self.final_copies(way, k):
            c.start()

    def final_copies(self, way, k):
        g = self.groups[k]
        mine = g.rs.at[(self.chips - 1) % 2, way]
        cols = pl.ds(pl.multiple_of(way * g.half + self.rep * g.share, 128), g.share) if g.share else None
        wide = g.half - 2 * g.share
        there = pl.ds(pl.multiple_of(way * wide, 128), wide)
        found = [rdma(mine.at[:, :, pl.ds(g.share, wide)], g.got.at[:, :, there],
                      self.fin_s.at[way, 2 * k + 1], self.fin_r.at[way, 2 * k + 1], self.opposite)]
        if self.shared:
            found.append(rdma(mine.at[:, :, pl.ds(0, g.share)], g.own.at[:, :, cols],
                              self.fin_s.at[way, 2 * k], self.fin_r.at[way, 2 * k], self.opposite))
        return found

    def finish(self):
        def go(way):
            for k, g in enumerate(self.groups):
                wide = g.half - 2 * g.share
                if self.shared:
                    ref = g.own.at[:, :, pl.ds(pl.multiple_of(way * g.half + self.other * g.share, 128), g.share)]
                    rdma(ref, ref, self.fin_s.at[way, 2 * k], self.fin_r.at[way, 2 * k], self.opposite).wait_recv()
                ref = g.got.at[:, :, pl.ds(pl.multiple_of(way * wide, 128), wide)]
                rdma(ref, ref, self.fin_s.at[way, 2 * k + 1], self.fin_r.at[way, 2 * k + 1], self.opposite).wait_recv()
                for c in self.final_copies(way, k):
                    c.wait_send()
            for t in (self.chips - 2, self.chips - 1):
                for c in self.sib_copies(t, way) + (self.y_copies(t, way) if self.shared else []):
                    c.wait_send()
            for c in self.ring_copies(self.chips - 2, way):
                c.wait_send()
        each(2, go)

    def at(self, t, f, *more):
        @pl.when((t >= 0) & (t < self.chips))
        def _():
            f(t, *more)


class Butterfly:
    def __init__(self, geo, n, buf, got, sems):
        _, self.me, self.rep, _, _, _ = geo
        self.stages = n.bit_length() - 1
        self.buf, self.got = buf, got
        self.send, self.recv = sems

    def partner(self, bit):
        return (self.me + bit - 2 * bit * lax.rem(lax.div(self.me, bit), 2), self.rep)

    def copy(self, j, dev):
        return rdma(self.buf.at[j], self.got.at[j], self.send.at[j], self.recv.at[j], dev)

    def begin(self):
        self.copy(0, (self.me, 1 - self.rep)).start()

    def stage(self, j, bit):
        self.copy(j - 1, self.partner(bit)).wait_recv()
        self.buf[j] = self.buf[j - 1] + self.got[j - 1]
        self.copy(j, self.partner(bit)).start()

    def end(self, dst):
        self.copy(self.stages, self.partner(1)).wait_recv()
        dst[...] = self.buf[self.stages] + self.got[self.stages]
        for j in range(self.stages + 1):
            self.copy(j, self.partner(1)).wait_send()


OFFSETS = (0, 0, 0, 5, 8)
FINALS = (0, 1, 2, 0, 0)
CHAINS = ((2,), (3,), (4,), (0, 5), (1, 6))
SLOTS = (3, 3, 3)
FIRST_PIECE = 0


def backward_kernel(n, sizes, dims, *refs):
    length, keys = dims
    ins, w_hbm, refs = refs[:16], refs[16], refs[17:]
    kept, (small_o,), refs = refs[:16], refs[16:17], refs[17:]
    done, refs = refs[:16], refs[16:]
    outs, (dtok, denc) = done[:14], done[14:]
    held, refs = refs[:16], refs[16:]
    hfft, hidt, dgu, cot, r1, cq, ckv, p2, x1, gains, qkv, p1, x, xt, enct, gain3 = held
    bufs, refs = refs[:42], refs[42:]
    sems, refs = [refs[9 * k:9 * k + 9] for k in range(5)], refs[45:]
    sm, sm_got, sm_s, sm_r, load_s, w, w_s, dy, dye, dh, r0, do, gain12, diag, store_s = refs
    geo = geometry(n)
    chips, me, rep, core, ring, device_at = geo
    rows, rows_d = sizes[0][1], sizes[4][1]

    loads = [pltpu.make_async_copy(a, b, load_s.at[i]) for i, (a, b) in enumerate(zip(ins, held))]
    for c in loads[:4]:
        c.start()

    def stored(i):
        return pltpu.make_async_copy(done[i], kept[i], store_s.at[i])

    def fetch(i, slot):
        return pltpu.make_async_copy(w_hbm.at[i], w.at[slot], w_s.at[slot])

    def block(dev, size):
        return pl.ds(pl.multiple_of(dev * size, size), size)
    lefts = [lambda i, dev: xt[(3, 2)[i], block(dev, rows), :], lambda i, dev: xt[(1, 0)[i], block(dev, rows), :],
             lambda i, dev: hfft[block(dev, rows), :], lambda i, dev: hfft[block(dev, rows), :],
             lambda i, dev: hidt[block(dev, rows_d), :], lambda i, dev: enct[block(dev, rows), :], lambda i, dev: xt[0, block(dev, rows), :]]
    rights = [lambda i, c: dy[i, :, c], lambda i, c: dy[2 + i, :, c], lambda i, c: dgu[0, :, c], lambda i, c: dgu[1, :, c],
              lambda i, c: cot[:, c], lambda i, c: dye[i, :, c], lambda i, c: dy[4 + i, :, c]]
    groups = [Group(lefts[k], rights[k], sizes[k], bufs[6 * k:6 * k + 6] + outs[2 * k:2 * k + 2]) for k in range(7)]
    chains = [Reduce(geo, [groups[k] for k in c], SLOTS, s) for c, s in zip(CHAINS, sems)]
    tree = Butterfly(geo, n, sm, sm_got, (sm_s, sm_r))
    lead = chains[0]

    barrier = pltpu.get_barrier_semaphore()
    greet = [lead.after[0], lead.after[1], lead.sibling, lead.opposite] + [tree.partner(1 << j) for j in range(tree.stages)]
    for dev in greet:
        pl.semaphore_signal(barrier, inc=1, device_id=dev, device_id_type=MESH)
    for g in groups:
        g.rr[0] = jnp.zeros(g.rr.shape[1:], BF)
    diag[...] = jnp.zeros(diag.shape, F32)
    for c in loads[4:]:
        c.start()
    for i, slot in ((5, 0), (6, 1), (7, 2), (4, 3)):
        fetch(i, slot).start()
    for c in loads[:4]:
        c.wait()
    pl.semaphore_wait(barrier, len(greet))

    total = p1.shape[0]
    width = dh.shape[1]

    def start_back():
        for c in loads[4:]:
            c.wait()
        dy[0] = r1[...].astype(BF)
        fetch(5, 0).wait()
        project_t([(dy.at[0], w.at[0])], do, kind=BF)
        fetch(3, 0).start()

    def cross(begin, end):
        def f():
            lax.fori_loop(begin, end, lambda i, c: (attend_back(
                i, cq, ckv.at[0], ckv.at[1], p2, do, dy.at[1], dye.at[0], dye.at[1], None, length, keys), c)[1], 0)
        return f

    def own(begin, end):
        def f():
            lax.fori_loop(begin, end, lambda i, c: (attend_back(
                i, qkv.at[0], qkv.at[1], qkv.at[2], p1, do, dy.at[3], dy.at[4], dy.at[5], diag, length, length), c)[1], 0)
        return f

    def encoder(begin, end, last):
        def f():
            if not last:
                fetch(6, 1).wait()
                fetch(7, 2).wait()
            project_t([(dye.at[0], w.at[1]), (dye.at[1], w.at[2])], denc, begin=begin, end=end)
            if last:
                stored(15).start()
                fetch(0, 1).start()
                fetch(1, 2).start()
        return f

    def cross_norm():
        norm_back(x1, gains.at[1], dh, r1, r0, gain12.at[1])
        dy[2] = r0[...].astype(BF)

    def cross_query():
        fetch(4, 3).wait()
        project_t([(dy.at[1], w.at[3])], dh)
        fetch(2, 3).start()

    def own_out():
        fetch(3, 0).wait()
        project_t([(dy.at[2], w.at[0])], do, kind=BF)

    def own_in(begin, end, last):
        def f():
            if not last:
                for i, slot in ((0, 1), (1, 2), (2, 3)):
                    fetch(i, slot).wait()
            project_t([(dy.at[3], w.at[1]), (dy.at[4], w.at[2]), (dy.at[5], w.at[3])], dh, begin=begin, end=end)
        return f

    def own_norm():
        norm_back(x, gains.at[0], dh, r0, dtok, gain12.at[0])
        stored(14).start()
        for k in range(width // 128):
            for i, g in enumerate((gain12.at[0], gain12.at[1], gain3)):
                sm[0, pl.ds(i * (width // 128) + k, 1), :] = g[:, k * 128:(k + 1) * 128]
        for i in range(diag.shape[0]):
            sm[0, pl.ds(3 * (width // 128) + i, 1), :] = diag[i]

    tiles = width // TILE
    pieces = [start_back]
    pieces += [cross(total * k // 8, total * (k + 1) // 8) for k in range(8)]
    pieces += [cross_query, cross_norm, own_out]
    pieces += [own(total * k // 5, total * (k + 1) // 5) for k in range(5)]
    pieces += [encoder(0, tiles // 2, False), encoder(tiles // 2, tiles, True)]
    pieces += [own_in(0, tiles // 2, False), own_in(tiles // 2, tiles, True), own_norm]
    tree_at = 7

    def piece(u, which):
        for i in range(which, len(pieces), 3):
            pl.when(u == i // 3 + FIRST_PIECE)(pieces[i])

    def step(v, bit):
        u = v - 3
        for k, c in enumerate(chains):
            t = u - OFFSETS[k]
            c.at(t, c.to_ring, FINALS[k] == 0)
            if k < 3:
                piece(u, k)
            if FINALS[k]:
                for way in range(2):
                    for j in range(len(c.groups)):
                        pl.when(t == chips - 1 + FINALS[k] + way)(functools.partial(c.send_final, way, j))
        for k, c in enumerate(chains):
            if c.shared:
                c.at(u - OFFSETS[k] + 2, c.to_across)
        for k, c in enumerate(chains):
            c.at(u - OFFSETS[k] + 3, c.to_sibling)
        pl.when(u == tree_at)(tree.begin)
        inside = (u > tree_at) & (u <= tree_at + tree.stages)

        @pl.when(inside)
        def _():
            tree.stage(u - tree_at, bit)
        return jnp.where(inside, bit * 2, bit)

    lax.fori_loop(0, OFFSETS[-1] + chips + 3, step, jnp.int32(1))
    tree.end(small_o)
    for k, c in enumerate(chains):
        c.finish()
        for g in CHAINS[k]:
            stored(2 * g).start()
            stored(2 * g + 1).start()
    for i in range(16):
        stored(i).wait()


def shares(half, part):
    return half * part // 1408 * 128


def backward(n, w, hfft, hidt, dgu, cot, r1, cq, ckv, p2, x1, gains, qkv, p1, x, xt, enct, gain3):
    chips = n // 2
    tokens, width = x.shape
    etokens, ff = enct.shape[1], dgu.shape[2]
    length, keys = p1.shape[2], p2.shape[2]
    rows, rows_d = width // n, hidt.shape[0] // n
    half, half_g = width // 2, ff // 2
    part = shares(half, 3)
    sizes = [(2, rows, half, part), (2, rows, half, part), (1, rows, half_g, shares(half_g, 3)),
             (1, rows, half_g, shares(half_g, 3)), (1, rows_d, half, part), (2, rows, half, part), (2, rows, half, part)]
    stages = n.bit_length() - 1
    dma = pltpu.SemaphoreType.DMA
    S = jax.ShapeDtypeStruct
    vm, hbm = pl.BlockSpec(memory_space=pltpu.VMEM), pl.BlockSpec(memory_space=pl.ANY)
    outs = []
    for count, r, h, share in sizes:
        outs += [S((count, r, 2 * h), BF), S((count, r, 2 * (h - 2 * share)), BF)]
    outs += [S((tokens, width), F32), S((etokens, width), F32)]
    small = (3 * (width // 128) + width // 64, 128)
    ins = (hfft, hidt, dgu, cot, r1, cq, ckv, p2, x1, gains, qkv, p1, x, xt, enct, gain3)
    slots = tuple(min(s, chips) for s in SLOTS)
    return pl.pallas_call(
        functools.partial(backward_kernel, n, sizes, (length, keys)),
        name="backward_reduce",
        out_shape=tuple(outs) + (S(small, F32),),
        in_specs=[hbm] * 17,
        out_specs=[hbm] * 16 + [vm],
        scratch_shapes=[pltpu.VMEM(a.shape, a.dtype) for a in outs] + [pltpu.VMEM(a.shape, a.dtype) for a in ins]
        + [b for size in sizes for b in group_shapes(size, slots)]
        + [s for c in CHAINS for s in reduce_sems(len(c), slots)]
        + [pltpu.VMEM((stages + 1,) + small, F32)] * 2 + [dma((stages + 1,))] * 2
        + [dma((16,)), pltpu.VMEM((4, width, width), BF), dma((4,)), pltpu.VMEM((6, tokens, width), BF),
           pltpu.VMEM((2, etokens, width), BF), pltpu.VMEM((tokens, width), F32), pltpu.VMEM((tokens, width), F32),
           pltpu.VMEM((tokens, width), BF), pltpu.VMEM((2, 1, width), F32), pltpu.VMEM((width // 64, 1, 128), F32),
           dma((16,))],
        compiler_params=pltpu.CompilerParams(collective_id=1, has_side_effects=True, vmem_limit_bytes=67043328),
    )(*ins, w)


def finish_kernel(sizes, passed, buckets_count, *refs):
    parts, mats = 2 * len(sizes), sum(s[0] for s in sizes)
    ins, (small, buckets), refs = refs[:parts + passed], refs[parts + passed:parts + passed + 2], refs[parts + passed + 2:]
    outs, (dtable, gain1, gain2, gain3), refs = refs[:mats + passed], refs[mats + passed:mats + passed + 4], refs[mats + passed + 4:]
    held, done, (load_s, store_s) = refs[:parts + passed], refs[parts + passed:-2], refs[-2:]
    loads = [pltpu.make_async_copy(a, b, load_s.at[i]) for i, (a, b) in enumerate(zip(ins, held))]
    stores = [pltpu.make_async_copy(a, b, store_s.at[i]) for i, (a, b) in enumerate(zip(done + held[parts:], outs))]
    for c in loads[:2] + loads[parts:] + loads[2:parts]:
        c.start()
    at = 0
    for k, (count, rows, half, share) in enumerate(sizes):
        if k == 1:
            for i in range(passed):
                loads[parts + i].wait()
                stores[mats + i].start()
        own, got = held[2 * k], held[2 * k + 1]
        loads[2 * k].wait()
        loads[2 * k + 1].wait()
        wide = half - 2 * share
        for i in range(count):
            for way in range(2):
                lo = way * half
                if share:
                    done[at][:, lo:lo + 2 * share] = own[i, :, lo:lo + 2 * share].astype(F32)
                v = own[i, :, lo + 2 * share:lo + half].astype(F32) + got[i, :, way * wide:(way + 1) * wide].astype(F32)
                done[at][:, lo + 2 * share:lo + half] = v
            stores[at].start()
            at += 1
    me = lax.axis_index("shard")
    rows = gain1.shape[1]
    per = 128 // rows
    heads = dtable.shape[0]
    tiles = (small.shape[0] - heads) // 3
    tile = lax.broadcasted_iota(jnp.int32, (tiles, 128), 0)
    for i, dst in enumerate((gain1, gain2, gain3)):
        v = jnp.where(tile == lax.div(me, per), small[i * tiles:(i + 1) * tiles, :], 0.0)
        v = pltpu.roll(v, lax.rem(128 - lax.rem(me, per) * rows, 128), 1)
        dst[...] = jnp.sum(v, axis=0, keepdims=True)[:, :rows]
    dtable[...] = lax.dot_general(small[3 * tiles:, :], bucket_rows(buckets, buckets_count), (((1,), (1,)), ((), ())),
                                  precision=lax.Precision.HIGHEST, preferred_element_type=F32)
    for c in stores:
        c.wait()


def finish(parts, passed, small, buckets, shape, rows):
    sizes, outs = [], []
    S = jax.ShapeDtypeStruct
    for own, got in zip(parts[0::2], parts[1::2]):
        count, r, width = own.shape
        half = width // 2
        sizes.append((count, r, half, (half - got.shape[2] // 2) // 2))
        outs += [S((r, width), F32)] * count
    vm, hbm = pl.BlockSpec(memory_space=pltpu.VMEM), pl.BlockSpec(memory_space=pl.ANY)
    ins = list(parts) + list(passed)
    dma = pltpu.SemaphoreType.DMA
    return pl.pallas_call(
        functools.partial(finish_kernel, sizes, len(passed), shape[1]),
        name="finish",
        out_shape=tuple(outs) + tuple(S(a.shape, a.dtype) for a in passed) + (S(shape, F32),) + (S((1, rows), F32),) * 3,
        in_specs=[hbm] * len(ins) + [vm] * 2,
        out_specs=[hbm] * (len(outs) + len(passed)) + [vm] * 4,
        scratch_shapes=[pltpu.VMEM(a.shape, a.dtype) for a in ins] + [pltpu.VMEM(a.shape, a.dtype) for a in outs]
        + [dma((len(ins),)), dma((len(outs) + len(passed),))],
        compiler_params=pltpu.CompilerParams(vmem_limit_bytes=67043328),
    )(*ins, small, buckets)


def body(hidden_in, encoded, dec_segments, enc_segments, buckets, out_cot, norm_self, self_query, self_key, self_value,
         self_out, table, norm_cross, cross_query, cross_key, cross_value, cross_out, norm_ff, ff_gate, ff_up, ff_down, *, n):
    micro, per, length, width = hidden_in.shape
    keys = encoded.shape[2]
    count = micro * per
    rows, rows_d, ff = self_query.shape[0], ff_down.shape[0], ff_gate.shape[1]
    spare = -rows_d % 16
    if spare:
        ff_down = jnp.pad(ff_down, ((0, spare), (0, 0)))
        ff_gate, ff_up = [jnp.pad(w.reshape(rows, n, rows_d), ((0, 0), (0, 0), (0, spare))).reshape(rows, -1) for w in (ff_gate, ff_up)]
    x = hidden_in.reshape(count * length, width)
    enc = encoded.reshape(count * keys, width)
    cot = out_cot.reshape(count * length, width)
    buckets = buckets.reshape(1, length)
    weights = (self_query, self_key, self_value, self_out, cross_query, cross_out, cross_key, cross_value, ff_gate, ff_up, ff_down)
    own_gains = [g.reshape(1, rows) for g in (norm_self, norm_cross, norm_ff)]
    w, out, xt, enct, hfft, hidt, dgu, r1, x1, qkv, cq, ckv, p1, p2, gain3, gains = forward(
        n, weights, own_gains, x, enc, cot, dec_segments.reshape(count, 1, length), enc_segments.reshape(count, 1, keys), buckets, table.T)
    *parts, dtok, denc, small = backward(n, w, hfft, hidt, dgu, cot, r1, cq, ckv, p2, x1, gains, qkv, p1, x, xt, enct, gain3)
    gco, gcq, gso, gq, gg, gup, gd, gck, gcv, gk, gv, out, dtok, denc, dtable, g1, g2, g3 = finish(
        parts, (out, dtok, denc), small, buckets, table.T.shape, rows)
    if spare:
        gd = gd[:rows_d]
        gg, gup = [g.reshape(rows, n, -1)[:, :, :rows_d].reshape(rows, ff) for g in (gg, gup)]
    return (
        out.reshape(hidden_in.shape), dtok.reshape(hidden_in.shape), denc.reshape(encoded.shape),
        g1.reshape(rows), gq, gk, gv, gso, dtable.T, g2.reshape(rows), gcq, gck, gcv, gco, g3.reshape(rows), gg, gup, gd,
    )


def solution(mesh):
    tok = P(None, ("shard", "rep"), None, None)
    seg = P(None, ("shard", "rep"), None)
    vec, mat, rep = P("shard"), P("shard", None), P()
    return jax.shard_map(
        functools.partial(body, n=mesh.shape["shard"]),
        mesh=mesh,
        in_specs=(tok, tok, seg, seg, rep, tok, vec, mat, mat, mat, mat, rep, vec, mat, mat, mat, mat, vec, mat, mat, mat),
        out_specs=(tok, tok, tok, vec, mat, mat, mat, mat, rep, vec, mat, mat, mat, mat, vec, mat, mat, mat),
        check_vma=False,
    )
```

```python
import functools
import math

import jax
import jax.numpy as jnp
from jax import lax
from jax.experimental import pallas as pl
from jax.experimental.pallas import tpu as pltpu
from jax.sharding import PartitionSpec as P

MESH = pl.DeviceIdType.MESH
BF = jnp.bfloat16
F32 = jnp.float32
EPS = 1e-06
NEG = -1e30
C1 = math.sqrt(2.0 / math.pi)
C2 = 0.044715
TILE = 256


def each(count, f):
    def step(i, carry):
        f(i)
        return carry
    lax.fori_loop(0, count, step, 0)


def tile_at(i, size=TILE):
    return pl.ds(pl.multiple_of(i * size, size), size)


def dot(a, b):
    return jnp.dot(a, b, preferred_element_type=F32)


def dot_t(a, b):
    return lax.dot_general(a, b, (((1,), (1,)), ((), ())), preferred_element_type=F32)


def dot_rows(a, b):
    return lax.dot_general(a, b, (((0,), (0,)), ((), ())), preferred_element_type=F32)


def normed(src, gain, dst):
    def rows(i):
        r = tile_at(i, 32)
        v = src[r, :].astype(F32)
        t = lax.rsqrt(jnp.mean(v * v, axis=-1, keepdims=True) + EPS)
        dst[r, :] = (v * t * gain[...]).astype(BF)
    each(src.shape[0] // 32, rows)


def norm_back(src, gain, grad, base, dst, gain_sum):
    gain_sum[...] = jnp.zeros(gain_sum.shape, F32)

    def rows(i):
        r = tile_at(i, 16)
        v = src[r, :].astype(F32)
        dy = grad[r, :]
        g = gain[...]
        t = lax.rsqrt(jnp.mean(v * v, axis=-1, keepdims=True) + EPS)
        vt = v * t
        gdy = g * dy
        inner = jnp.mean(vt * gdy, axis=-1, keepdims=True)
        dst[r, :] = base[r, :].astype(F32) + t * (gdy - vt * inner)
        gain_sum[...] += jnp.sum(vt * dy, axis=0, keepdims=True)
    each(src.shape[0] // 16, rows)


def turn(src, dst):
    for b in range(src.shape[0] // 128):
        def block(c, b=b):
            dst[tile_at(c), b * 128:(b + 1) * 128] = src[b * 128:(b + 1) * 128, tile_at(c)].T
        each(src.shape[1] // TILE, block)


def head_masks():
    lane = lax.broadcasted_iota(jnp.int32, (1, 128), 1)
    even = (lane < 64).astype(F32).astype(BF)
    return even, (lane >= 64).astype(F32).astype(BF)


def pair_rows(x, masks):
    return jnp.concatenate([x * masks[0], x * masks[1]], axis=0)


def side_by_side(x):
    half = x.shape[0] // 2
    return jnp.concatenate([x[:half], x[half:]], axis=1)


def attend(i, q, k, v, p, o, neg, bias, length, keys):
    masks = head_masks()
    pairs = q.shape[1] // 128
    b, pair = lax.div(i, pairs), lax.rem(i, pairs)
    lanes = tile_at(pair, 128)
    rows, krows = tile_at(b, length), tile_at(b, keys)
    s = dot_t(pair_rows(q[rows, lanes], masks), k[krows, lanes])
    if bias is not None:
        s = s + bias[pair]
    n = neg[b]
    s = s + jnp.concatenate([n, n], axis=0)
    e = jnp.exp(s - jnp.max(s, axis=-1, keepdims=True))
    pb = (e * (1.0 / jnp.sum(e, axis=-1, keepdims=True))).astype(BF)
    p[i] = pb
    o[rows, lanes] = dot(side_by_side(pb), pair_rows(v[krows, lanes], masks)).astype(BF)


def attend_back(i, q, k, v, p, do, dq, dk, dv, diag, length, keys):
    masks = head_masks()
    pairs = q.shape[1] // 128
    b, pair = lax.div(i, pairs), lax.rem(i, pairs)
    lanes = tile_at(pair, 128)
    rows, krows = tile_at(b, length), tile_at(b, keys)
    dos = pair_rows(do[rows, lanes], masks)
    dp = dot_t(dos, v[krows, lanes])
    pb = p[i]
    pf = pb.astype(F32)
    ds = (pf * (dp - jnp.sum(pf * dp, axis=-1, keepdims=True))).astype(BF)
    dq[rows, lanes] = dot(side_by_side(ds), pair_rows(k[krows, lanes], masks)).astype(BF)
    dk[krows, lanes] = dot_rows(ds, pair_rows(q[rows, lanes], masks)).astype(BF)
    dv[krows, lanes] = dot_rows(pb, dos).astype(BF)
    if diag is not None:
        i0 = lax.broadcasted_iota(jnp.int32, (length, length), 0)
        i1 = lax.broadcasted_iota(jnp.int32, (length, length), 1)
        flip = (i0 + i1 == length - 1).astype(F32).astype(BF)
        for h in range(2):
            u = pltpu.roll(dot(flip, ds[h * length:(h + 1) * length]), 1, 1, stride=1, stride_axis=0)
            diag[2 * pair + h] += jnp.sum(u, axis=0, keepdims=True)


def position_bias(taps, bias, length):
    def pair(i):
        for h in range(2):
            w = jnp.broadcast_to(taps[pl.ds(2 * i + h, 1), :], (length, length))
            bias[i, h * length:(h + 1) * length, :] = pltpu.roll(w, 0, 1, stride=1, stride_axis=0)
    each(bias.shape[0], pair)


def seg_masks(drow, erow, neg_self, neg_cross, length):
    for b in range(drow.shape[0]):
        row = drow[b].astype(F32)
        col = jnp.broadcast_to(row, (length, length)).T
        i = lax.broadcasted_iota(jnp.int32, (length, length), 0)
        j = lax.broadcasted_iota(jnp.int32, (length, length), 1)
        neg_self[b] = jnp.where((j <= i) & (col == row), 0.0, NEG)
        enc = erow[b].astype(F32)
        for k in range(enc.shape[1] // length):
            part = slice(k * length, (k + 1) * length)
            neg_cross[b, :, part] = jnp.where(col == enc[:, part], 0.0, NEG)


def bucket_rows(buckets, count):
    length = buckets.shape[1]
    i = lax.broadcasted_iota(jnp.int32, (count, length), 0)
    hot = (i == buckets[...]).astype(F32).astype(BF)
    m = lax.broadcasted_iota(jnp.int32, (length, length), 0)
    l = lax.broadcasted_iota(jnp.int32, (length, length), 1)
    back = ((m + l == length) | ((m == 0) & (l == 0))).astype(F32).astype(BF)
    return dot(hot, back)


def project(a, w, dst, base=None, kind=BF):
    def tile(c):
        v = dot(a[...], w[:, tile_at(c)])
        if base is not None:
            v = v + base[:, tile_at(c)].astype(F32)
        dst[:, tile_at(c)] = v.astype(kind)
    each(dst.shape[1] // TILE, tile)


def project_t(terms, dst, kind=F32, begin=0, end=None):
    def tile(c):
        v = None
        for a, w in terms:
            u = dot_t(a[...], w[tile_at(c), :])
            v = u if v is None else v + u
        dst[:, tile_at(c)] = v.astype(kind)
    lax.fori_loop(begin, dst.shape[1] // TILE if end is None else end, lambda i, carry: (tile(i), carry)[1], 0)


def feed_tile(c, h, cot, wg, wu, wd, hid, dgate, dup):
    cols = tile_at(c)
    hv = h[...]
    gate = dot(hv, wg[:, cols])
    up = dot(hv, wu[:, cols])
    dhid = dot_t(cot[...], wd[cols, :])
    sq = gate * gate
    th = jnp.tanh(C1 * gate * (1.0 + C2 * sq))
    hp = 0.5 * (1.0 + th)
    act = gate * hp
    hid[:, cols] = (act * up).astype(BF)
    slope = hp + (0.5 * C1) * gate * (1.0 - th * th) * (1.0 + (3.0 * C2) * sq)
    dgate[:, cols] = (dhid * up * slope).astype(BF)
    dup[:, cols] = (dhid * act).astype(BF)


def geometry(n):
    chips = n // 2
    side = chips // 2
    s = lax.axis_index("shard")
    rep = lax.axis_index("rep")
    core = lax.rem(s, 2)
    chip = lax.div(s, 2)
    x = lax.rem(chip, 2)
    z = lax.div(chip, 2)
    ring = z + x * (chips - 1 - 2 * z)

    def device_at(position):
        p = lax.rem(position + 2 * chips, chips)
        px = lax.div(p, side)
        pz = p + px * (chips - 1 - 2 * p)
        return (pz * 2 + px) * 2 + core

    return chips, s, rep, core, ring, device_at


def rdma(src, dst, ss, rs, dev):
    return pltpu.make_async_remote_copy(src_ref=src, dst_ref=dst, send_sem=ss, recv_sem=rs, device_id=dev, device_id_type=MESH)


class Gather:
    def __init__(self, geo, pieces, across, sems):
        self.chips, self.me, self.rep, self.core, self.ring, self.device_at = geo
        self.hops = self.chips - 1
        self.pieces, self.across = pieces, across
        self.ring_s, self.ring_r, self.sib_s, self.sib_r, self.y_s, self.y_r, self.yy_s, self.yy_r, self.own_s, self.own_r = sems
        self.other = 1 - 2 * self.core
        self.sibling = (self.me + self.other, self.rep)
        self.opposite = (self.me, 1 - self.rep)
        self.ahead = ((self.device_at(self.ring + 1), self.rep), (self.device_at(self.ring - 1), self.rep))

    def source(self, way, t):
        return self.device_at(self.ring - 1 - t) if way == 0 else self.device_at(self.ring + 1 + t)

    def each(self, rep, count=None):
        most = max(len(self.pieces(0, rep)), len(self.pieces(1, rep)))
        for p in range(most if count is None else count):
            for way in range(2):
                ps = self.pieces(way, rep)
                if p < len(ps):
                    yield way, p, ps[p]

    def ring_copy(self, way, t, p, ref):
        return rdma(ref, ref, self.ring_s.at[way, t, p], self.ring_r.at[way, t, p], self.ahead[way])

    def sib_copy(self, way, t, p, ref):
        return rdma(ref, ref, self.sib_s.at[way, t, p], self.sib_r.at[way, t, p], self.sibling)

    def y_copy(self, way, t, p, ref):
        return rdma(ref, ref, self.y_s.at[way, t, p], self.y_r.at[way, t, p], self.opposite)

    def yy_copy(self, way, t, p, ref):
        return rdma(ref, ref, self.yy_s.at[way, t, p], self.yy_r.at[way, t, p], self.sibling)

    def own_copies(self, src):
        found = []
        for rep in (self.rep, 1 - self.rep):
            for way, p, ref in self.each(rep, None if rep is self.rep else self.across):
                i = 0 if rep is self.rep else 1
                r = ref(src)
                found.append(rdma(r, r, self.own_s.at[i, way, p], self.own_r.at[i, way, p], self.sibling))
        return found

    def start(self):
        for way, p, ref in self.each(self.rep):
            self.ring_copy(way, 0, p, ref(self.me)).start()
        for c in self.own_copies(self.me):
            c.start()

    def hop(self, t, last=False, which=None):
        for way, p, ref in self.each(self.rep):
            if which is not None and p != which:
                continue
            r = ref(self.source(way, t))
            self.ring_copy(way, t, p, r).wait_recv()
            if not last:
                self.ring_copy(way, t + 1, p, r).start()
            if p < self.across:
                self.y_copy(way, t, p, r).start()
            self.sib_copy(way, t, p, r).start()

    def relay(self, t):
        for way, p, ref in self.each(1 - self.rep, self.across):
            r = ref(self.source(way, t))
            self.y_copy(way, t, p, r).wait_recv()
            self.yy_copy(way, t, p, r).start()

    def complete(self):
        def step(t):
            for way, p, ref in self.each(self.rep):
                self.sib_copy(way, t, p, ref(self.source(way, t) + self.other)).wait_recv()
            for way, p, ref in self.each(1 - self.rep, self.across):
                self.yy_copy(way, t, p, ref(self.source(way, t) + self.other)).wait_recv()
        each(self.hops, step)
        for c in self.own_copies(self.me + self.other):
            c.wait_recv()

    def drain(self):
        def step(t):
            for way, p, ref in self.each(self.rep):
                r = ref(self.source(way, t))
                self.ring_copy(way, t, p, r).wait_send()
                self.sib_copy(way, t, p, r).wait_send()
                if p < self.across:
                    self.y_copy(way, t, p, r).wait_send()
            for way, p, ref in self.each(1 - self.rep, self.across):
                self.yy_copy(way, t, p, ref(self.source(way, t))).wait_send()
        each(self.hops, step)
        for c in self.own_copies(self.me):
            c.wait_send()


def gather_sems(hops, pieces, across):
    dma = pltpu.SemaphoreType.DMA
    return [dma((2, hops, pieces))] * 4 + [dma((2, hops, across))] * 4 + [dma((2, 2, pieces))] * 2


def forward_kernel(n, dims, *refs):
    length, keys = dims
    ins, refs = refs[:11], refs[11:]
    own_gains, refs = refs[:3], refs[3:]
    x, enc, cot, drow, erow, buckets, table = refs[:7]
    w_out, kept, refs = refs[7], refs[8:23], refs[23:]
    out, xt, enct, hfft, hidt, dgu, r1, x1, qkv, cq, ckv, p1, p2, gain3, gains = held = refs[:15]
    w, gu, dn, gn, taps, bias, neg_s, neg_c, h, hid, x2, dh, o = refs[15:28]
    first_sems, second_sems = refs[28:38], refs[38:48]
    load_s, store_s = refs[48:50]

    def stored(i):
        return pltpu.make_async_copy(held[i], kept[i], store_s.at[i])

    def store(*which):
        for i in which:
            stored(i).start()
    geo = geometry(n)
    chips, me, rep, core, ring, device_at = geo
    hops = chips - 1
    rows, rows_d = ins[0].shape[0], ins[10].shape[0]
    half, half_g = w.shape[2] // 2, gu.shape[2] // 2
    count = drow.shape[0]
    pairs = w.shape[2] // 128

    def block(src):
        return pl.ds(pl.multiple_of(src * rows, rows), rows)

    def block_d(src):
        return pl.ds(pl.multiple_of(src * rows_d, rows_d), rows_d)

    def attention_pieces(way, r):
        c = pl.ds(way * half, half)
        near, far = pl.ds(way * half, half // 2), pl.ds(way * half + half // 2, half // 2)
        found = [lambda s: w.at[r, block(s), c], lambda s: w.at[4 + r, block(s), c], lambda s: w.at[2 + r, block(s), near],
                 lambda s: w.at[pl.ds(2, 2), block(s), far], lambda s: w.at[pl.ds(6, 2), block(s), c]]
        return found + [lambda s: gn.at[s]] if way == 0 else found

    def feed_pieces(way, r):
        return [lambda s: gu.at[r, block(s), pl.ds(way * half_g, half_g)], lambda s: dn.at[block_d(s), pl.ds(way * half, half)]]

    first = Gather(geo, attention_pieces, 3, first_sems)
    second = Gather(geo, feed_pieces, 1, second_sems)

    width = w.shape[2]
    places = [w.at[i, block(me), :] for i in range(8)] + [gu.at[i, block(me), :] for i in range(2)] + [dn.at[block_d(me), :]]
    loads = [pltpu.make_async_copy(a, b, load_s.at[i]) for i, (a, b) in enumerate(zip(ins, places))]
    for c in loads:
        c.start()
    barrier = pltpu.get_barrier_semaphore()
    for dev in first.ahead + (first.sibling, first.opposite):
        pl.semaphore_signal(barrier, inc=1, device_id=dev, device_id_type=MESH)
    per = 128 // rows
    lane = lax.broadcasted_iota(jnp.int32, (rows, 128), 1)
    spot = lax.broadcasted_iota(jnp.int32, (rows, 128), 0)
    place = (lane == spot + lax.rem(me, per) * rows).astype(F32).astype(BF)
    gn[me] = jnp.concatenate([dot(g[...], place) for g in own_gains] + [jnp.zeros((5, 128), F32)], axis=0)
    for c in loads[:8]:
        c.wait()
    pl.semaphore_wait(barrier, 4)

    first.start()
    turn(enc, enct)
    store(2)
    first.hop(0)
    taps[...] = dot(table[...], bucket_rows(buckets, table.shape[1]).astype(BF))
    position_bias(taps, bias, length)
    seg_masks(drow, erow, neg_s, neg_c, length)

    def middle(t):
        first.hop(t)
        first.relay(t - 1)
    lax.fori_loop(1, hops - 1, lambda t, c: (middle(t), c)[1], 0)
    for c in loads[8:]:
        c.wait()
    second.start()
    first.hop(hops - 1, True)
    first.relay(hops - 2)
    first.relay(hops - 1)
    first.complete()
    weights_out = pltpu.make_async_copy(w, w_out, store_s.at[15])
    weights_out.start()
    for j in range(w.shape[2] // 128):
        v = gn[j * per]
        for i in range(1, per):
            v = v + gn[j * per + i]
        for i in range(3):
            gains[i, :, j * 128:(j + 1) * 128] = v[i:i + 1, :]
    store(14)

    def some(begin, end, f):
        lax.fori_loop(begin, end, lambda i, c: (f(i), c)[1], 0)

    def heads():
        normed(x, gains.at[0], h)
        project(h, w.at[0], qkv.at[0])

    def keys_values():
        for i in range(1, 3):
            project(h, w.at[i], qkv.at[i])

    def own(i):
        attend(i, qkv.at[0], qkv.at[1], qkv.at[2], p1, o, neg_s, bias, length, length)

    def own_result():
        store(8, 11)
        turn(h, xt.at[0])
        turn(o, xt.at[1])
        project(o, w.at[3], x1, base=x, kind=F32)

    def cross_heads():
        normed(x1, gains.at[1], h)
        project(h, w.at[4], cq)

    def cross_keys():
        store(7, 9)
        turn(h, xt.at[2])
        project(enc, w.at[6], ckv.at[0])

    def cross(i):
        attend(i, cq, ckv.at[0], ckv.at[1], p2, o, neg_c, None, length, keys)

    def before_feed():
        store(10, 12)
        turn(o, xt.at[3])
        store(1)
        project(o, w.at[5], x2, base=x1, kind=F32)
        normed(x2, gains.at[2], h)
        turn(h, hfft)
        store(3)

    total = count * pairs
    def quarters(f):
        return [functools.partial(some, total * k // 4, total * (k + 1) // 4, f) for k in range(4)]
    halves = [heads, keys_values] + quarters(own) + [own_result, cross_heads, cross_keys, lambda: project(enc, w.at[7], ckv.at[1])] + quarters(cross)
    chunks = list(zip(halves[0::2], halves[1::2]))
    for t in range(len(chunks)):
        chunks[t][0]()
        second.hop(t, t == hops - 1, 0)
        if t > 0:
            second.relay(t - 1)
        chunks[t][1]()
        second.hop(t, t == hops - 1, 1)
    if hops > len(chunks):
        def rest(t):
            second.hop(t)
            second.relay(t - 1)
        some(len(chunks), hops - 1, rest)
        second.hop(hops - 1, True)
        second.relay(hops - 2)
    before_feed()
    second.relay(hops - 1)
    second.complete()

    each(hid.shape[1] // TILE, lambda c: feed_tile(c, h, cot, gu.at[0], gu.at[1], dn, hid, dgu.at[0], dgu.at[1]))
    store(5)
    turn(hid, hidt)
    store(4)
    project_t([(dgu.at[0], gu.at[0]), (dgu.at[1], gu.at[1])], dh)
    norm_back(x2, gains.at[2], dh, cot, r1, gain3)
    store(6, 13)
    project(hid, dn, out, base=x2)
    store(0)
    first.drain()
    second.drain()
    weights_out.wait()
    for i in range(15):
        stored(i).wait()


def forward(n, weights, own_gains, x, enc, cot, drow, erow, buckets, table):
    hops = n // 2 - 1
    rows, width = weights[0].shape
    ff = weights[8].shape[1]
    tokens, etokens = x.shape[0], enc.shape[0]
    count, _, length = drow.shape
    keys = etokens // count
    pairs = width // 128
    S = jax.ShapeDtypeStruct

    def v(*shape, t=BF):
        return pltpu.VMEM(shape, t)

    kept = [
        S((tokens, width), BF), S((4, width, tokens), BF), S((width, etokens), BF),
        S((width, tokens), BF), S((ff, tokens), BF), S((2, tokens, ff), BF), S((tokens, width), F32), S((tokens, width), F32),
        S((3, tokens, width), BF), S((tokens, width), BF), S((2, etokens, width), BF),
        S((count * pairs, 2 * length, length), BF), S((count * pairs, 2 * length, keys), BF),
        S((1, width), F32), S((3, 1, width), F32),
    ]
    vm, hbm = pl.BlockSpec(memory_space=pltpu.VMEM), pl.BlockSpec(memory_space=pl.ANY)
    return pl.pallas_call(
        functools.partial(forward_kernel, n, (length, keys)),
        name="gather_forward",
        out_shape=(S((8, width, width), BF),) + tuple(kept),
        in_specs=[hbm] * 11 + [vm] * 10,
        out_specs=[hbm] * 16,
        scratch_shapes=[v(*a.shape, t=a.dtype) for a in kept] + [
            v(8, width, width), v(2, width, ff), v(ff, width), v(n, 8, 128, t=F32), v(table.shape[0], length, t=F32),
            v(pairs, 2 * length, length, t=F32), v(count, length, length, t=F32), v(count, length, keys, t=F32),
            v(tokens, width), v(tokens, ff), v(tokens, width, t=F32), v(tokens, width, t=F32), v(tokens, width),
        ] + gather_sems(hops, 6, 3) + gather_sems(hops, 2, 1) + [pltpu.SemaphoreType.DMA((11,)), pltpu.SemaphoreType.DMA((16,))],
        compiler_params=pltpu.CompilerParams(collective_id=0, has_side_effects=True, vmem_limit_bytes=67043328),
    )(*weights, *own_gains, x, enc, cot, drow, erow, buckets, table)


class Group:
    def __init__(self, left, right, size, refs):
        self.left, self.right = left, right
        self.count, self.rows, self.half, self.share = size
        self.ss, self.sr, self.ys, self.yr, self.rs, self.rr, self.own, self.got = refs

    def part(self, i, dev, start, width):
        return dot(self.left(i, dev), self.right(i, pl.ds(pl.multiple_of(start, 128), width)))


def group_shapes(size, slots):
    count, rows, half, share = size
    sib_slots, y_slots, ring_slots = slots

    def v(*shape):
        return pltpu.VMEM(shape, BF)
    crossing = [v(2, 2, count, rows, share), v(y_slots, 2, count, rows, share)] if share else [v(16, 128), v(16, 128)]
    return [v(2, 2, count, rows, half), v(sib_slots, 2, count, rows, half)] + crossing + [
        v(2, 2, count, rows, half - share), v(ring_slots, 2, count, rows, half - share)]


def reduce_sems(groups, slots):
    dma = pltpu.SemaphoreType.DMA
    sib_slots, y_slots, ring_slots = slots
    return [dma((2, 2, groups)), dma((sib_slots, 2, groups)), dma((2, 2, groups)), dma((y_slots, 2, groups)),
            dma((2, 2, groups)), dma((ring_slots, 2, groups)), dma((2, 2 * groups)), dma((2, 2 * groups)),
            pltpu.SemaphoreType.REGULAR((3, 2))]


class Reduce:
    def __init__(self, geo, groups, slots, sems):
        self.chips, self.me, self.rep, self.core, self.ring, self.device_at = geo
        self.groups = groups
        self.shared = groups[0].share > 0
        self.slots = slots
        self.sib_s, self.sib_r, self.y_s, self.y_r, self.ring_s, self.ring_r, self.fin_s, self.fin_r, self.free = sems
        self.other = 1 - self.rep
        self.sibling = (self.me + 1 - 2 * self.core, self.rep)
        self.opposite = (self.me, self.other)
        self.after = ((self.device_at(self.ring + 1), self.rep), (self.device_at(self.ring - 1), self.rep))

    def block(self, t, way, core):
        return self.device_at(self.ring + (2 * way - 1) * (1 + t)) + core - self.core

    def toward(self, way):
        return (self.after[0][0] + way * (self.after[1][0] - self.after[0][0]), self.rep)

    def behind(self, way):
        return (self.after[1][0] + way * (self.after[0][0] - self.after[1][0]), self.rep)

    def sib_copies(self, t, way):
        s, r = lax.rem(t, 2), lax.rem(t, self.slots[0])
        return [rdma(g.ss.at[s, way], g.sr.at[r, way], self.sib_s.at[s, way, i], self.sib_r.at[r, way, i], self.sibling)
                for i, g in enumerate(self.groups)]

    def y_copies(self, t, way):
        s, r = lax.rem(t, 2), lax.rem(t, self.slots[1])
        return [rdma(g.ys.at[s, way], g.yr.at[r, way], self.y_s.at[s, way, i], self.y_r.at[r, way, i], self.opposite)
                for i, g in enumerate(self.groups)]

    def ring_copies(self, t, way):
        s, r = lax.rem(t, 2), lax.rem(t + 1, self.slots[2])
        return [rdma(g.rs.at[s, way], g.rr.at[r, way], self.ring_s.at[s, way, i], self.ring_r.at[r, way, i], self.toward(way))
                for i, g in enumerate(self.groups)]

    def claim(self, kind, step, way):
        if self.slots[kind] < self.chips:
            @pl.when(step >= self.slots[kind])
            def _():
                pl.semaphore_wait(self.free.at[kind, way], 1)

    def release(self, kind, step, way, dev):
        if self.slots[kind] < self.chips:
            @pl.when(step + self.slots[kind] < self.chips)
            def _():
                pl.semaphore_signal(self.free.at[kind, way], inc=1, device_id=dev, device_id_type=MESH)

    def settle(self, t, copies):
        @pl.when(t >= 2)
        def _():
            for c in copies:
                c.wait_send()

    def to_sibling(self, t):
        s = lax.rem(t, 2)

        def go(way):
            dev = self.block(t, way, 1 - self.core)
            self.settle(t, self.sib_copies(t, way))
            for g in self.groups:
                for i in range(g.count):
                    g.ss[s, way, i] = g.part(i, dev, way * g.half, g.half).astype(BF)
            self.claim(0, t, way)
            for c in self.sib_copies(t, way):
                c.start()
        each(2, go)

    def to_across(self, t):
        s, r = lax.rem(t, 2), lax.rem(t, self.slots[0])

        def go(way):
            dev = self.block(t, way, self.core)
            self.settle(t, self.y_copies(t, way))
            for c in self.sib_copies(t, way):
                c.wait_recv()
            for g in self.groups:
                at = pl.multiple_of(self.other * g.share, 128)
                for i in range(g.count):
                    v = g.part(i, dev, way * g.half + at, g.share)
                    g.ys[s, way, i] = (v + g.sr[r, way, i, :, pl.ds(at, g.share)].astype(F32)).astype(BF)
            self.claim(1, t, way)
            for c in self.y_copies(t, way):
                c.start()
        each(2, go)

    def to_ring(self, t, at_once):
        s, b, y, r = lax.rem(t, 2), lax.rem(t, self.slots[0]), lax.rem(t, self.slots[1]), lax.rem(t, self.slots[2])

        for k, g in enumerate(self.groups):
            def go(way, k=k, g=g):
                dev = self.block(t, way, self.core)
                if not self.shared:
                    self.sib_copies(t, way)[k].wait_recv()
                lo, wide = 2 * g.share, g.half - 2 * g.share
                at = pl.multiple_of(self.rep * g.share, 128)
                common, apart = [], []
                for i in range(g.count):
                    if self.shared:
                        v = g.part(i, dev, way * g.half + at, g.share)
                        common.append(v + g.sr[b, way, i, :, pl.ds(at, g.share)].astype(F32))
                    v = g.part(i, dev, way * g.half + lo, wide)
                    apart.append(v + g.sr[b, way, i, :, lo:].astype(F32))
                self.settle(t, self.ring_copies(t, way)[k:k + 1])
                if self.shared:
                    self.y_copies(t, way)[k].wait_recv()

                @pl.when(t >= 1)
                def _():
                    self.ring_copies(t - 1, way)[k].wait_recv()
                for i in range(g.count):
                    if self.shared:
                        v = common[i] + g.yr[y, way, i].astype(F32) + g.rr[r, way, i, :, :g.share].astype(F32)
                        g.rs[s, way, i, :, :g.share] = v.astype(BF)
                    g.rs[s, way, i, :, g.share:] = (apart[i] + g.rr[r, way, i, :, g.share:].astype(F32)).astype(BF)

                @pl.when(t < self.chips - 1)
                def _():
                    if k == 0:
                        self.claim(2, t + 1, way)
                    self.ring_copies(t, way)[k].start()

                @pl.when(t == self.chips - 1)
                def _():
                    if at_once:
                        self.send_final(way, k)
                    last = (self.chips - 1) % 2
                    if self.shared:
                        cols = pl.ds(pl.multiple_of(way * g.half + self.rep * g.share, 128), g.share)
                        g.own[:, :, cols] = g.rs[last, way, :, :, :g.share]
                    rest = pl.ds(pl.multiple_of(way * g.half + lo, 128), wide)
                    g.own[:, :, rest] = g.rs[last, way, :, :, g.share:]
                if k == len(self.groups) - 1:
                    self.release(0, t, way, self.sibling)
                    if self.shared:
                        self.release(1, t, way, self.opposite)
                    self.release(2, t, way, self.behind(way))
            each(2, go)

    def send_final(self, way, k):
        for c in self.final_copies(way, k):
            c.start()

    def final_copies(self, way, k):
        g = self.groups[k]
        mine = g.rs.at[(self.chips - 1) % 2, way]
        cols = pl.ds(pl.multiple_of(way * g.half + self.rep * g.share, 128), g.share) if g.share else None
        wide = g.half - 2 * g.share
        there = pl.ds(pl.multiple_of(way * wide, 128), wide)
        found = [rdma(mine.at[:, :, pl.ds(g.share, wide)], g.got.at[:, :, there],
                      self.fin_s.at[way, 2 * k + 1], self.fin_r.at[way, 2 * k + 1], self.opposite)]
        if self.shared:
            found.append(rdma(mine.at[:, :, pl.ds(0, g.share)], g.own.at[:, :, cols],
                              self.fin_s.at[way, 2 * k], self.fin_r.at[way, 2 * k], self.opposite))
        return found

    def finish(self):
        def go(way):
            for k, g in enumerate(self.groups):
                wide = g.half - 2 * g.share
                if self.shared:
                    ref = g.own.at[:, :, pl.ds(pl.multiple_of(way * g.half + self.other * g.share, 128), g.share)]
                    rdma(ref, ref, self.fin_s.at[way, 2 * k], self.fin_r.at[way, 2 * k], self.opposite).wait_recv()
                ref = g.got.at[:, :, pl.ds(pl.multiple_of(way * wide, 128), wide)]
                rdma(ref, ref, self.fin_s.at[way, 2 * k + 1], self.fin_r.at[way, 2 * k + 1], self.opposite).wait_recv()
                for c in self.final_copies(way, k):
                    c.wait_send()
            for t in (self.chips - 2, self.chips - 1):
                for c in self.sib_copies(t, way) + (self.y_copies(t, way) if self.shared else []):
                    c.wait_send()
            for c in self.ring_copies(self.chips - 2, way):
                c.wait_send()
        each(2, go)

    def at(self, t, f, *more):
        @pl.when((t >= 0) & (t < self.chips))
        def _():
            f(t, *more)


class Butterfly:
    def __init__(self, geo, n, buf, got, sems):
        _, self.me, self.rep, _, _, _ = geo
        self.stages = n.bit_length() - 1
        self.buf, self.got = buf, got
        self.send, self.recv = sems

    def partner(self, bit):
        return (self.me + bit - 2 * bit * lax.rem(lax.div(self.me, bit), 2), self.rep)

    def copy(self, j, dev):
        return rdma(self.buf.at[j], self.got.at[j], self.send.at[j], self.recv.at[j], dev)

    def begin(self):
        self.copy(0, (self.me, 1 - self.rep)).start()

    def stage(self, j, bit):
        self.copy(j - 1, self.partner(bit)).wait_recv()
        self.buf[j] = self.buf[j - 1] + self.got[j - 1]
        self.copy(j, self.partner(bit)).start()

    def end(self, dst):
        self.copy(self.stages, self.partner(1)).wait_recv()
        dst[...] = self.buf[self.stages] + self.got[self.stages]
        for j in range(self.stages + 1):
            self.copy(j, self.partner(1)).wait_send()


OFFSETS = (0, 0, 0, 6, 8)
FINALS = (0, 1, 2, 0, 0)
CHAINS = ((2,), (3,), (4,), (0, 5), (1, 6))
SLOTS = (3, 3, 3)
FIRST_PIECE = 0


def backward_kernel(n, sizes, dims, *refs):
    length, keys = dims
    ins, w_hbm, refs = refs[:16], refs[16], refs[17:]
    kept, (small_o,), refs = refs[:16], refs[16:17], refs[17:]
    done, refs = refs[:16], refs[16:]
    outs, (dtok, denc) = done[:14], done[14:]
    held, refs = refs[:16], refs[16:]
    hfft, hidt, dgu, cot, r1, cq, ckv, p2, x1, gains, qkv, p1, x, xt, enct, gain3 = held
    bufs, refs = refs[:42], refs[42:]
    sems, refs = [refs[9 * k:9 * k + 9] for k in range(5)], refs[45:]
    sm, sm_got, sm_s, sm_r, load_s, w, w_s, dy, dye, dh, r0, do, gain12, diag, store_s = refs
    geo = geometry(n)
    chips, me, rep, core, ring, device_at = geo
    rows, rows_d = sizes[0][1], sizes[4][1]

    loads = [pltpu.make_async_copy(a, b, load_s.at[i]) for i, (a, b) in enumerate(zip(ins, held))]
    for c in loads[:4]:
        c.start()

    def stored(i):
        return pltpu.make_async_copy(done[i], kept[i], store_s.at[i])

    def fetch(i, slot):
        return pltpu.make_async_copy(w_hbm.at[i], w.at[slot], w_s.at[slot])

    def block(dev, size):
        return pl.ds(pl.multiple_of(dev * size, size), size)
    lefts = [lambda i, dev: xt[(3, 2)[i], block(dev, rows), :], lambda i, dev: xt[(1, 0)[i], block(dev, rows), :],
             lambda i, dev: hfft[block(dev, rows), :], lambda i, dev: hfft[block(dev, rows), :],
             lambda i, dev: hidt[block(dev, rows_d), :], lambda i, dev: enct[block(dev, rows), :], lambda i, dev: xt[0, block(dev, rows), :]]
    rights = [lambda i, c: dy[i, :, c], lambda i, c: dy[2 + i, :, c], lambda i, c: dgu[0, :, c], lambda i, c: dgu[1, :, c],
              lambda i, c: cot[:, c], lambda i, c: dye[i, :, c], lambda i, c: dy[4 + i, :, c]]
    groups = [Group(lefts[k], rights[k], sizes[k], bufs[6 * k:6 * k + 6] + outs[2 * k:2 * k + 2]) for k in range(7)]
    chains = [Reduce(geo, [groups[k] for k in c], SLOTS, s) for c, s in zip(CHAINS, sems)]
    tree = Butterfly(geo, n, sm, sm_got, (sm_s, sm_r))
    lead = chains[0]

    barrier = pltpu.get_barrier_semaphore()
    greet = [lead.after[0], lead.after[1], lead.sibling, lead.opposite] + [tree.partner(1 << j) for j in range(tree.stages)]
    for dev in greet:
        pl.semaphore_signal(barrier, inc=1, device_id=dev, device_id_type=MESH)
    for g in groups:
        g.rr[0] = jnp.zeros(g.rr.shape[1:], BF)
    diag[...] = jnp.zeros(diag.shape, F32)
    for c in loads[4:]:
        c.start()
    for i, slot in ((5, 0), (6, 1), (7, 2), (4, 3)):
        fetch(i, slot).start()
    for c in loads[:4]:
        c.wait()
    pl.semaphore_wait(barrier, len(greet))

    total = p1.shape[0]
    width = dh.shape[1]

    def start_back():
        for c in loads[4:]:
            c.wait()
        dy[0] = r1[...].astype(BF)
        fetch(5, 0).wait()
        project_t([(dy.at[0], w.at[0])], do, kind=BF)
        fetch(3, 0).start()

    def cross(begin, end):
        def f():
            lax.fori_loop(begin, end, lambda i, c: (attend_back(
                i, cq, ckv.at[0], ckv.at[1], p2, do, dy.at[1], dye.at[0], dye.at[1], None, length, keys), c)[1], 0)
        return f

    def own(begin, end):
        def f():
            lax.fori_loop(begin, end, lambda i, c: (attend_back(
                i, qkv.at[0], qkv.at[1], qkv.at[2], p1, do, dy.at[3], dy.at[4], dy.at[5], diag, length, length), c)[1], 0)
        return f

    def encoder(begin, end, last):
        def f():
            if not last:
                fetch(6, 1).wait()
                fetch(7, 2).wait()
            project_t([(dye.at[0], w.at[1]), (dye.at[1], w.at[2])], denc, begin=begin, end=end)
            if last:
                stored(15).start()
                fetch(0, 1).start()
                fetch(1, 2).start()
        return f

    def cross_norm():
        norm_back(x1, gains.at[1], dh, r1, r0, gain12.at[1])
        dy[2] = r0[...].astype(BF)

    def cross_query():
        fetch(4, 3).wait()
        project_t([(dy.at[1], w.at[3])], dh)
        fetch(2, 3).start()

    def own_out():
        fetch(3, 0).wait()
        project_t([(dy.at[2], w.at[0])], do, kind=BF)

    def own_in(begin, end, last):
        def f():
            if not last:
                for i, slot in ((0, 1), (1, 2), (2, 3)):
                    fetch(i, slot).wait()
            project_t([(dy.at[3], w.at[1]), (dy.at[4], w.at[2]), (dy.at[5], w.at[3])], dh, begin=begin, end=end)
        return f

    def own_norm():
        norm_back(x, gains.at[0], dh, r0, dtok, gain12.at[0])
        stored(14).start()
        for k in range(width // 128):
            for i, g in enumerate((gain12.at[0], gain12.at[1], gain3)):
                sm[0, pl.ds(i * (width // 128) + k, 1), :] = g[:, k * 128:(k + 1) * 128]
        for i in range(diag.shape[0]):
            sm[0, pl.ds(3 * (width // 128) + i, 1), :] = diag[i]

    tiles = width // TILE
    pieces = [start_back]
    pieces += [cross(total * k // 8, total * (k + 1) // 8) for k in range(8)]
    pieces += [cross_query, cross_norm, own_out]
    pieces += [own(total * k // 5, total * (k + 1) // 5) for k in range(5)]
    pieces += [encoder(0, tiles // 2, False), encoder(tiles // 2, tiles, True)]
    pieces += [own_in(0, tiles // 2, False), own_in(tiles // 2, tiles, True), own_norm]
    tree_at = 7

    def piece(u, which):
        for i in range(which, len(pieces), 3):
            pl.when(u == i // 3 + FIRST_PIECE)(pieces[i])

    def step(v, bit):
        u = v - 3
        for k, c in enumerate(chains):
            t = u - OFFSETS[k]
            c.at(t, c.to_ring, FINALS[k] == 0)
            if k < 3:
                piece(u, k)
            if FINALS[k]:
                for way in range(2):
                    for j in range(len(c.groups)):
                        pl.when(t == chips - 1 + FINALS[k] + way)(functools.partial(c.send_final, way, j))
        for k, c in enumerate(chains):
            if c.shared:
                c.at(u - OFFSETS[k] + 2, c.to_across)
        for k, c in enumerate(chains):
            c.at(u - OFFSETS[k] + 3, c.to_sibling)
        pl.when(u == tree_at)(tree.begin)
        inside = (u > tree_at) & (u <= tree_at + tree.stages)

        @pl.when(inside)
        def _():
            tree.stage(u - tree_at, bit)
        return jnp.where(inside, bit * 2, bit)

    lax.fori_loop(0, OFFSETS[-1] + chips + 3, step, jnp.int32(1))
    tree.end(small_o)
    for k, c in enumerate(chains):
        c.finish()
        for g in CHAINS[k]:
            stored(2 * g).start()
            stored(2 * g + 1).start()
    for i in range(16):
        stored(i).wait()


def shares(half, part):
    return half * part // 1408 * 128


def backward(n, w, hfft, hidt, dgu, cot, r1, cq, ckv, p2, x1, gains, qkv, p1, x, xt, enct, gain3):
    chips = n // 2
    tokens, width = x.shape
    etokens, ff = enct.shape[1], dgu.shape[2]
    length, keys = p1.shape[2], p2.shape[2]
    rows, rows_d = width // n, hidt.shape[0] // n
    half, half_g = width // 2, ff // 2
    part = shares(half, 3)
    sizes = [(2, rows, half, part), (2, rows, half, part), (1, rows, half_g, shares(half_g, 3)),
             (1, rows, half_g, shares(half_g, 3)), (1, rows_d, half, part), (2, rows, half, part), (2, rows, half, part)]
    stages = n.bit_length() - 1
    dma = pltpu.SemaphoreType.DMA
    S = jax.ShapeDtypeStruct
    vm, hbm = pl.BlockSpec(memory_space=pltpu.VMEM), pl.BlockSpec(memory_space=pl.ANY)
    outs = []
    for count, r, h, share in sizes:
        outs += [S((count, r, 2 * h), BF), S((count, r, 2 * (h - 2 * share)), BF)]
    outs += [S((tokens, width), F32), S((etokens, width), F32)]
    small = (3 * (width // 128) + width // 64, 128)
    ins = (hfft, hidt, dgu, cot, r1, cq, ckv, p2, x1, gains, qkv, p1, x, xt, enct, gain3)
    slots = tuple(min(s, chips) for s in SLOTS)
    return pl.pallas_call(
        functools.partial(backward_kernel, n, sizes, (length, keys)),
        name="backward_reduce",
        out_shape=tuple(outs) + (S(small, F32),),
        in_specs=[hbm] * 17,
        out_specs=[hbm] * 16 + [vm],
        scratch_shapes=[pltpu.VMEM(a.shape, a.dtype) for a in outs] + [pltpu.VMEM(a.shape, a.dtype) for a in ins]
        + [b for size in sizes for b in group_shapes(size, slots)]
        + [s for c in CHAINS for s in reduce_sems(len(c), slots)]
        + [pltpu.VMEM((stages + 1,) + small, F32)] * 2 + [dma((stages + 1,))] * 2
        + [dma((16,)), pltpu.VMEM((4, width, width), BF), dma((4,)), pltpu.VMEM((6, tokens, width), BF),
           pltpu.VMEM((2, etokens, width), BF), pltpu.VMEM((tokens, width), F32), pltpu.VMEM((tokens, width), F32),
           pltpu.VMEM((tokens, width), BF), pltpu.VMEM((2, 1, width), F32), pltpu.VMEM((width // 64, 1, 128), F32),
           dma((16,))],
        compiler_params=pltpu.CompilerParams(collective_id=1, has_side_effects=True, vmem_limit_bytes=67043328),
    )(*ins, w)


def finish_kernel(sizes, passed, buckets_count, *refs):
    parts, mats = 2 * len(sizes), sum(s[0] for s in sizes)
    ins, (small, buckets), refs = refs[:parts + passed], refs[parts + passed:parts + passed + 2], refs[parts + passed + 2:]
    outs, (dtable, gain1, gain2, gain3), refs = refs[:mats + passed], refs[mats + passed:mats + passed + 4], refs[mats + passed + 4:]
    held, done, (load_s, store_s) = refs[:parts + passed], refs[parts + passed:-2], refs[-2:]
    loads = [pltpu.make_async_copy(a, b, load_s.at[i]) for i, (a, b) in enumerate(zip(ins, held))]
    stores = [pltpu.make_async_copy(a, b, store_s.at[i]) for i, (a, b) in enumerate(zip(done + held[parts:], outs))]
    for c in loads[:2] + loads[parts:] + loads[2:parts]:
        c.start()
    at = 0
    for k, (count, rows, half, share) in enumerate(sizes):
        if k == 1:
            for i in range(passed):
                loads[parts + i].wait()
                stores[mats + i].start()
        own, got = held[2 * k], held[2 * k + 1]
        loads[2 * k].wait()
        loads[2 * k + 1].wait()
        wide = half - 2 * share
        for i in range(count):
            for way in range(2):
                lo = way * half
                if share:
                    done[at][:, lo:lo + 2 * share] = own[i, :, lo:lo + 2 * share].astype(F32)
                v = own[i, :, lo + 2 * share:lo + half].astype(F32) + got[i, :, way * wide:(way + 1) * wide].astype(F32)
                done[at][:, lo + 2 * share:lo + half] = v
            stores[at].start()
            at += 1
    me = lax.axis_index("shard")
    rows = gain1.shape[1]
    per = 128 // rows
    heads = dtable.shape[0]
    tiles = (small.shape[0] - heads) // 3
    tile = lax.broadcasted_iota(jnp.int32, (tiles, 128), 0)
    for i, dst in enumerate((gain1, gain2, gain3)):
        v = jnp.where(tile == lax.div(me, per), small[i * tiles:(i + 1) * tiles, :], 0.0)
        v = pltpu.roll(v, lax.rem(128 - lax.rem(me, per) * rows, 128), 1)
        dst[...] = jnp.sum(v, axis=0, keepdims=True)[:, :rows]
    dtable[...] = lax.dot_general(small[3 * tiles:, :], bucket_rows(buckets, buckets_count), (((1,), (1,)), ((), ())),
                                  precision=lax.Precision.HIGHEST, preferred_element_type=F32)
    for c in stores:
        c.wait()


def finish(parts, passed, small, buckets, shape, rows):
    sizes, outs = [], []
    S = jax.ShapeDtypeStruct
    for own, got in zip(parts[0::2], parts[1::2]):
        count, r, width = own.shape
        half = width // 2
        sizes.append((count, r, half, (half - got.shape[2] // 2) // 2))
        outs += [S((r, width), F32)] * count
    vm, hbm = pl.BlockSpec(memory_space=pltpu.VMEM), pl.BlockSpec(memory_space=pl.ANY)
    ins = list(parts) + list(passed)
    dma = pltpu.SemaphoreType.DMA
    return pl.pallas_call(
        functools.partial(finish_kernel, sizes, len(passed), shape[1]),
        name="finish",
        out_shape=tuple(outs) + tuple(S(a.shape, a.dtype) for a in passed) + (S(shape, F32),) + (S((1, rows), F32),) * 3,
        in_specs=[hbm] * len(ins) + [vm] * 2,
        out_specs=[hbm] * (len(outs) + len(passed)) + [vm] * 4,
        scratch_shapes=[pltpu.VMEM(a.shape, a.dtype) for a in ins] + [pltpu.VMEM(a.shape, a.dtype) for a in outs]
        + [dma((len(ins),)), dma((len(outs) + len(passed),))],
        compiler_params=pltpu.CompilerParams(vmem_limit_bytes=67043328),
    )(*ins, small, buckets)


def body(hidden_in, encoded, dec_segments, enc_segments, buckets, out_cot, norm_self, self_query, self_key, self_value,
         self_out, table, norm_cross, cross_query, cross_key, cross_value, cross_out, norm_ff, ff_gate, ff_up, ff_down, *, n):
    micro, per, length, width = hidden_in.shape
    keys = encoded.shape[2]
    count = micro * per
    rows, rows_d, ff = self_query.shape[0], ff_down.shape[0], ff_gate.shape[1]
    spare = -rows_d % 16
    if spare:
        ff_down = jnp.pad(ff_down, ((0, spare), (0, 0)))
        ff_gate, ff_up = [jnp.pad(w.reshape(rows, n, rows_d), ((0, 0), (0, 0), (0, spare))).reshape(rows, -1) for w in (ff_gate, ff_up)]
    x = hidden_in.reshape(count * length, width)
    enc = encoded.reshape(count * keys, width)
    cot = out_cot.reshape(count * length, width)
    buckets = buckets.reshape(1, length)
    weights = (self_query, self_key, self_value, self_out, cross_query, cross_out, cross_key, cross_value, ff_gate, ff_up, ff_down)
    own_gains = [g.reshape(1, rows) for g in (norm_self, norm_cross, norm_ff)]
    w, out, xt, enct, hfft, hidt, dgu, r1, x1, qkv, cq, ckv, p1, p2, gain3, gains = forward(
        n, weights, own_gains, x, enc, cot, dec_segments.reshape(count, 1, length), enc_segments.reshape(count, 1, keys), buckets, table.T)
    *parts, dtok, denc, small = backward(n, w, hfft, hidt, dgu, cot, r1, cq, ckv, p2, x1, gains, qkv, p1, x, xt, enct, gain3)
    gco, gcq, gso, gq, gg, gup, gd, gck, gcv, gk, gv, out, dtok, denc, dtable, g1, g2, g3 = finish(
        parts, (out, dtok, denc), small, buckets, table.T.shape, rows)
    if spare:
        gd = gd[:rows_d]
        gg, gup = [g.reshape(rows, n, -1)[:, :, :rows_d].reshape(rows, ff) for g in (gg, gup)]
    return (
        out.reshape(hidden_in.shape), dtok.reshape(hidden_in.shape), denc.reshape(encoded.shape),
        g1.reshape(rows), gq, gk, gv, gso, dtable.T, g2.reshape(rows), gcq, gck, gcv, gco, g3.reshape(rows), gg, gup, gd,
    )


def solution(mesh):
    tok = P(None, ("shard", "rep"), None, None)
    seg = P(None, ("shard", "rep"), None)
    vec, mat, rep = P("shard"), P("shard", None), P()
    return jax.shard_map(
        functools.partial(body, n=mesh.shape["shard"]),
        mesh=mesh,
        in_specs=(tok, tok, seg, seg, rep, tok, vec, mat, mat, mat, mat, rep, vec, mat, mat, mat, mat, vec, mat, mat, mat),
        out_specs=(tok, tok, tok, vec, mat, mat, mat, mat, rep, vec, mat, mat, mat, mat, vec, mat, mat, mat),
        check_vma=False,
    )
```
